32 devices in a mesh: fsdp: 32 (over z, y, x, core).
Axes of the slice: x: 2, y: 2, z: 4, core: 2. Of those that a mesh axis runs over, the one named last changes fastest.
Arguments:
- inputs: bfloat16 [64, 256, 1024], P('fsdp'), may hold values from -6 to 6
- cotangent: float32 [64, 256, 1024], P('fsdp'), may hold values from -12 to 12
- parents: int32 [64, 13], P('fsdp'), may hold values from 0 to 11, as said below
- lengths: int32 [64, 13], P('fsdp'), may hold values from 1 to 85, 256 in all within a row
- first_gain: float32 [2, 1024], P(None, 'fsdp'), may hold values from 0.5 to 1.5
- query_weight: float32 [2, 1024, 1024], P(None, 'fsdp'), may hold values from -0.1875 to 0.1875
- latent_weight: float32 [2, 1024, 512], P(None, 'fsdp'), may hold values from -0.1875 to 0.1875
- key_weight: float32 [2, 2, 256, 512], P(None, None, 'fsdp'), may hold values from -0.375 to 0.375
- value_weight: float32 [2, 2, 256, 512], P(None, None, 'fsdp'), may hold values from -0.375 to 0.375
- out_weight: float32 [2, 1024, 1024], P(None, None, 'fsdp'), may hold values from -1.5 to 1.5
- second_gain: float32 [2, 1024], P(None, 'fsdp'), may hold values from 0.5 to 1.5
- gate_weight: float32 [2, 1024, 2816], P(None, 'fsdp'), may hold values from -0.1875 to 0.1875
- up_weight: float32 [2, 1024, 2816], P(None, 'fsdp'), may hold values from -0.1875 to 0.1875
- down_weight: float32 [2, 2816, 1024], P(None, None, 'fsdp'), may hold values from -0.109375 to 0.109375
Outputs:
- outputs: float32 [64, 256, 1024], P('fsdp')
- grad_inputs: float32 [64, 256, 1024], P('fsdp')
- grad_first_gain: float32 [2, 1024], P(None, 'fsdp')
- grad_query_weight: float32 [2, 1024, 1024], P(None, 'fsdp')
- grad_latent_weight: float32 [2, 1024, 512], P(None, 'fsdp')
- grad_key_weight: float32 [2, 2, 256, 512], P(None, None, 'fsdp')
- grad_value_weight: float32 [2, 2, 256, 512], P(None, None, 'fsdp')
- grad_out_weight: float32 [2, 1024, 1024], P(None, None, 'fsdp')
- grad_second_gain: float32 [2, 1024], P(None, 'fsdp')
- grad_gate_weight: float32 [2, 1024, 2816], P(None, 'fsdp')
- grad_up_weight: float32 [2, 1024, 2816], P(None, 'fsdp')
- grad_down_weight: float32 [2, 2816, 1024], P(None, None, 'fsdp')
The draws below stay inside these ranges and needn't reach their ends.
Inputs may be any that keep to these rules, and one draw needn't show every extreme that they name: parents[t, 0] = 0 stands for the first segment, which has none; for s >= 1, parents[t, s] is an earlier segment of tree t; the last segment's parent is the one before it. `lengths`: each row sums to 256, and one entry of every row equals 85.
All inputs are finite; a program needn't handle non-finite values.
Results may differ from the reference program's by a relative error of at most 0.023.
The reference program's roundings to bfloat16 on the way count: a program that leaves them out, or rounds other values in their place, can miss the bound.
Values may be sent and summed in bfloat16 or wider, within the bound.
A program may use at most 256 MiB of HBM per device.

```python
import math
import jax
import jax.numpy as jnp
import numpy as np
from jax import lax

D = 1024
HEADS = 16
HD = 64
GROUPS = 2
LAT = 256
FF = 2816
TREE = 256
SEGS = 13
LAYERS = 2
SEG_MOST = 85
TREES = 64


def draw_parents(key, part):
    random_ints = jax.random.randint(jax.random.fold_in(key, 7), (TREES, SEGS), 0, 1 << 20)
    seg_index = jnp.arange(SEGS, dtype=jnp.int32)
    picked = random_ints % jnp.maximum(seg_index, 1)[None, :]
    picked = jnp.where(seg_index[None, :] == SEGS - 1, SEGS - 2, picked)
    return picked.astype(jnp.int32)


def raised(values, rng, source, target, blocks, factor):
    def block_of(position):
        return (jnp.arange(values.shape[position]) // (values.shape[position] // blocks)).reshape((-1,) + (1,) * (values.ndim - 1 - position))

    near = jax.random.permutation(rng, blocks)[block_of(target)]
    other_side = (block_of(target) + blocks // 2) % blocks
    return jnp.where((block_of(source) == near) | (block_of(source) == other_side), factor * values, values)


def shard_levels(stream_key, shape, pieces, least, top_value):
    def one(axis_at, shards_of):
        heights = jax.random.uniform(jax.random.fold_in(jax.random.fold_in(stream_key, 6), axis_at), (shards_of,), jnp.float32, least / len(pieces), top_value / len(pieces))
        return jnp.repeat(jnp.exp(heights), shape[axis_at] // shards_of).reshape((-1,) + (1,) * (len(shape) - axis_at - 1))

    level = one(*pieces[0])
    for cut in pieces[1:]:
        level = level * one(*cut)
    return level


def split_up(count, total, limit, lean):
    loads = [(1 << 20) // math.isqrt(standing ** lean) + 1 for standing in range(2, count + 1)]
    surplus, given = total - limit - (count - 1), [1] * (count - 1)
    while surplus > 0:
        free = [i for i in range(count - 1) if given[i] < limit]
        whole, budget = sum([loads[i] for i in free]), surplus
        for i in free:
            extra = min(limit - given[i], max(1, budget * loads[i] // whole), surplus)
            given[i] = given[i] + extra
            surplus = surplus - extra
    return np.array([limit] + given)


def uneven_parts(rng, amount, total, most, slope):
    if amount == 2:
        one = jax.random.randint(rng, (), max(1, total - most), min(most, total - 1) + 1)
        return jnp.stack([one, total - one])
    tallies = jnp.asarray(split_up(amount, total, most, slope), jnp.int32)
    twos = (amount - 1) // 2
    source_of, taker = tallies[1:1 + 2 * twos:2], tallies[2:2 + 2 * twos:2]
    slack = jnp.minimum(source_of - 1, most - taker)
    moved = jax.random.randint(jax.random.fold_in(rng, 1), (twos,), 0, 1 << 20) % (slack + 1)
    tallies = tallies.at[1:1 + 2 * twos:2].set(source_of - moved).at[2:2 + 2 * twos:2].set(taker + moved)
    return tallies[jax.random.permutation(jax.random.fold_in(rng, 2), amount)]


def scatter_about(stream_key, shape, scale, bound, pieces=(), held_as=jnp.bfloat16):
    entries = jax.random.normal(stream_key, shape, jnp.float32) * scale
    if len(pieces) > 0:
        entries = shard_levels(stream_key, shape, pieces, -0.22, 0.18) * entries
    return jnp.clip(entries, min=-bound, max=bound).astype(held_as)


def gaussian_with(own_key, shape, deviation, most, split, heavy, kind=jnp.bfloat16):
    values = deviation * jax.random.normal(own_key, shape, jnp.float32)
    if split:
        values = values * shard_levels(own_key, shape, split, -0.22, 0.18)
    return jnp.clip(raised(values, jax.random.fold_in(own_key, 3), *heavy), -most, most).astype(kind)


def setup_inputs(seed: int = 0) -> dict:
    key_list = jax.random.split(jax.random.key(seed), 15)
    return {
        "inputs": scatter_about(key_list[0], (TREES, TREE, D), 1.0, 6.0, ((0, 32),)),
        "cotangent": gaussian_with(key_list[1], (TREES, TREE, D), 1.0, 12.0, ((0, 32),), (0, 2, 32, 2.75), jnp.float32),
        "parents": draw_parents(jax.random.fold_in(key_list[14], 71), 0),
        "lengths": jax.vmap(lambda own: uneven_parts(own, SEGS, TREE, SEG_MOST, 1))(jax.random.split(key_list[3], TREES)).reshape((TREES, SEGS)).astype(jnp.int32),
        "first_gain": jnp.clip(1.0 + 0.1 * jax.random.normal(key_list[4], (LAYERS, D), jnp.float32), 0.5, 1.5),
        "query_weight": scatter_about(key_list[5], (LAYERS, D, HEADS * HD), D ** -0.5, 0.1875, ((1, 32),), jnp.float32),
        "latent_weight": scatter_about(key_list[6], (LAYERS, D, GROUPS * LAT), D ** -0.5, 0.1875, ((1, 32),), jnp.float32),
        "key_weight": scatter_about(key_list[7], (LAYERS, GROUPS, LAT, HEADS // GROUPS * HD), LAT ** -0.5, 0.375, ((2, 32),), jnp.float32),
        "value_weight": scatter_about(key_list[8], (LAYERS, GROUPS, LAT, HEADS // GROUPS * HD), LAT ** -0.5, 0.375, ((2, 32),), jnp.float32),
        "out_weight": scatter_about(key_list[9], (LAYERS, HEADS * HD, D), (D // 64) ** -0.5, 1.5, ((2, 32),), jnp.float32),
        "second_gain": jnp.clip(1.0 + 0.1 * jax.random.normal(key_list[10], (LAYERS, D), jnp.float32), 0.5, 1.5),
        "gate_weight": scatter_about(key_list[11], (LAYERS, D, FF), D ** -0.5, 0.1875, ((1, 32),), jnp.float32),
        "up_weight": scatter_about(key_list[12], (LAYERS, D, FF), D ** -0.5, 0.1875, ((1, 32),), jnp.float32),
        "down_weight": scatter_about(key_list[13], (LAYERS, FF, D), FF ** -0.5, 0.109375, ((2, 32),), jnp.float32),
    }


epsilon = 1e-05

@jax.custom_vjp
def low(v):
    return lax.optimization_barrier(v.astype(jnp.bfloat16)).astype(jnp.float32)

@jax.custom_vjp
def low_back(v):
    return v

def low_keep(v):
    return (low(v), None)

def low_pass(kept, grad):
    return (grad,)

def back_keep(v):
    return (v, None)

def back_low(kept, grad):
    return (low(grad),)
low.defvjp(low_keep, low_pass)
low_back.defvjp(back_keep, back_low)

def tree_allowed(parent_row, length_row):
    count = parent_row.shape[0]
    highest = lax.Precision.HIGHEST
    seg_index = jnp.arange(count, dtype=jnp.int32)
    step_up = ((parent_row[:, None] == seg_index[None, :]) & (seg_index[:, None] > 0)).astype(jnp.float32)
    identity = jnp.eye(count, dtype=jnp.float32)
    reach = identity
    for repeat in range(count):
        reach = jnp.minimum(identity + jnp.dot(step_up, reach, precision=highest), 1.0)
    ends = jnp.cumsum(length_row, dtype=jnp.int32)
    positions = jnp.arange(TREE, dtype=jnp.int32)
    segment = lax.optimization_barrier(jnp.sum((ends[None, :] <= positions[:, None]).astype(jnp.int32), axis=1, dtype=jnp.int32))
    member = (segment[:, None] == seg_index[None, :]).astype(jnp.float32)
    linked = jnp.dot(jnp.dot(member, reach, precision=highest), member.T, precision=highest) > 0.5
    return linked & (positions[None, :] <= positions[:, None])

def block_forward(resid, weights, allowed):
    gain_attn, query_proj, latent_proj, key_up, value_up, out_proj, gain_mlp, gate_proj, up_proj, down_proj = weights
    highest = lax.Precision.HIGHEST
    count_rows = resid.shape[0]
    head_scale = 1.0 / math.sqrt(HD)
    scale_attn = lax.rsqrt(lax.optimization_barrier(jnp.mean(resid * resid, axis=-1, keepdims=True)) + epsilon)
    normed_attn = low(resid * scale_attn * gain_attn)
    queries = low_back(low(jnp.dot(normed_attn, query_proj, precision=highest)))
    latents = low_back(low(jnp.dot(normed_attn, latent_proj, precision=highest)))
    grouped = latents.reshape(count_rows, GROUPS, LAT)
    key_rows = low_back(low(jnp.einsum('tgl,glo->tgo', grouped, key_up, precision=highest)))
    value_rows = low_back(low(jnp.einsum('tgl,glo->tgo', grouped, value_up, precision=highest)))
    heads_q = queries.reshape(count_rows, HEADS, HD)
    heads_k = key_rows.reshape(count_rows, HEADS, HD)
    heads_v = value_rows.reshape(count_rows, HEADS, HD)
    scores = low_back(jnp.einsum('qhd,khd->hqk', heads_q, heads_k, precision=highest) * head_scale)
    scores = jnp.where(allowed[None], scores, -1e+30)
    row_max = lax.optimization_barrier(jnp.max(scores, axis=-1, keepdims=True))
    exponent = jnp.exp(scores - row_max)
    probs = low(exponent / lax.optimization_barrier(jnp.sum(exponent, axis=-1, keepdims=True)))
    mixed = jnp.einsum('hqk,khd->qhd', probs, heads_v, precision=highest).reshape(count_rows, HEADS * HD)
    mixed = low_back(low(mixed))
    after_attn = resid + low_back(jnp.dot(mixed, out_proj, precision=highest))
    scale_mlp = lax.rsqrt(lax.optimization_barrier(jnp.mean(after_attn * after_attn, axis=-1, keepdims=True)) + epsilon)
    normed_mlp = low(after_attn * scale_mlp * gain_mlp)
    gate_pre = low_back(jnp.dot(normed_mlp, gate_proj, precision=highest))
    up_pre = low_back(jnp.dot(normed_mlp, up_proj, precision=highest))
    hidden = low(jax.nn.silu(gate_pre) * up_pre)
    return after_attn + low_back(jnp.dot(hidden, down_proj, precision=highest))

def reference(inputs, cotangent, parents, lengths, first_gain, query_weight, latent_weight, key_weight, value_weight, out_weight, second_gain, gate_weight, up_weight, down_weight):
    masters = (first_gain, query_weight, latent_weight, key_weight, value_weight, out_weight, second_gain, gate_weight, up_weight, down_weight)

    def forward(tokens, master_set):
        weights = tuple((low(master) for master in master_set))

        def one_tree(carry, item):
            tree_rows, parent_row, length_row = item
            allowed = tree_allowed(parent_row, length_row)
            resid = tree_rows
            for layer_index in range(LAYERS):
                resid = block_forward(resid, tuple((weight[layer_index] for weight in weights)), allowed)
            return (carry, resid)
        start = jnp.zeros((), jnp.float32)
        ignored, result = lax.scan(jax.checkpoint(one_tree), start, (tokens, parents, lengths))
        return result
    tokens = inputs.astype(jnp.float32)
    result, pullback = jax.vjp(forward, tokens, masters)
    grad_tokens, grad_masters = pullback(cotangent)
    return (result, grad_tokens) + tuple(grad_masters)
```

```python
import functools
import math

import jax
import jax.numpy as jnp
from jax import lax
from jax.experimental import pallas as pl
from jax.experimental.pallas import tpu as pltpu
from jax.sharding import PartitionSpec as P

HEADS = 16
HD = 64
GROUPS = 2
LAT = 256
LAYERS = 2
LAG = 2
epsilon = 1e-05

MESH = pl.DeviceIdType.MESH
ANY = pl.BlockSpec(memory_space=pl.ANY)
DMA = pltpu.SemaphoreType.DMA
bf16 = jnp.bfloat16
f32 = jnp.float32


def dims_of(n):
    chips = n // 2
    side = 1
    if chips & (chips - 1) == 0:
        side = 2 ** ((chips.bit_length() - 1) // 3)
    return chips // (side * side), side, side


def index(n, z, y, x, c):
    Z, Y, X = dims_of(n)
    return ((z * Y + y) * X + x) * 2 + c


def place(n):
    Z, Y, X = dims_of(n)
    me = lax.axis_index("fsdp")
    return me // (2 * X * Y), lax.rem(me // (2 * X), Y), lax.rem(me // 2, X), lax.rem(me, 2)


def greet(n, z, y, x, c):
    Z, Y, X = dims_of(n)
    peers = [index(n, lax.rem(z + o, Z), y, x, c) for o in range(1, Z)]
    peers += [index(n, z, lax.rem(y + o, Y), x, c) for o in range(1, Y)]
    peers += [index(n, z, y, lax.rem(x + o, X), c) for o in range(1, X)]
    peers += [index(n, z, y, x, 1 - c)]
    bar = pltpu.get_barrier_semaphore()
    for peer in peers:
        pl.semaphore_signal(bar, inc=1, device_id=(peer,), device_id_type=MESH)
    pl.semaphore_wait(bar, len(peers))


def remote(src, dst, send, recv, device):
    copy = pltpu.make_async_remote_copy(
        src_ref=src,
        dst_ref=dst,
        send_sem=send,
        recv_sem=recv,
        device_id=(device,),
        device_id_type=MESH,
    )
    copy.start()
    return copy


def cut(widths, target):
    out = []
    for a, w in enumerate(widths):
        k, u = max(1, round(w / target)), w // 128
        edges = [round(j * u / k) * 128 for j in range(k + 1)]
        for lo, hi in zip(edges, edges[1:]):
            half = (hi - lo) // 128
            half = half // 2 if len(out) % 2 == 0 else (half + 1) // 2
            out.append((a, lo, lo + half * 128, hi))
    return out


def run_stages(count, lag, stages):
    held = [None] * count
    last = len(stages) - 1
    for slot in range(count + lag * last):
        for s in range(last, -1, -1):
            i = slot - lag * s
            if 0 <= i < count:
                if s > 0:
                    for copy in held[i]:
                        copy.wait()
                held[i] = stages[s](i)


def gather_kernel(n, chunks, count, *refs):
    Z, Y, X = dims_of(n)
    ins, outs = refs[:count], refs[count : 2 * count]
    own_sem, zs, zr, as_, ar, bs, br, cs, cr = refs[2 * count :]
    z, y, x, c = place(n)
    greet(n, z, y, x, c)

    def along_z(i):
        a, lo, mid, hi = chunks[i]
        src, dst = ins[a].at[:, lo:hi], outs[a].at[z, y, x, c, :, lo:hi]
        own = pltpu.make_async_copy(src, dst, own_sem.at[i])
        own.start()
        return [own] + [
            remote(src, dst, zs.at[i, o - 1], zr.at[i, o - 1], index(n, lax.rem(z + o, Z), y, x, c))
            for o in range(1, Z)
        ]

    def to_x(o):
        return index(n, z, y, lax.rem(x + o, X), c)

    def to_y(o):
        return index(n, z, lax.rem(y + o, Y), x, c)

    def first_side(i):
        a, lo, mid, hi = chunks[i]
        copies = []
        for h, (start, end, size, to) in enumerate(((lo, mid, X, to_x), (mid, hi, Y, to_y))):
            part = outs[a].at[:, y, x, c, :, start:end]
            for o in range(1, size if end > start else 1):
                copies.append(remote(part, part, as_.at[i, h, o - 1], ar.at[i, h, o - 1], to(o)))
        return copies

    def second_side(i):
        a, lo, mid, hi = chunks[i]
        copies = []
        for o in range(1, Y if mid > lo else 1):
            part = outs[a].at[:, y, :, c, :, lo:mid]
            copies.append(remote(part, part, bs.at[i, 0, o - 1], br.at[i, 0, o - 1], to_y(o)))
        for o in range(1, X):
            part = outs[a].at[:, :, x, c, :, mid:hi]
            copies.append(remote(part, part, bs.at[i, 1, o - 1], br.at[i, 1, o - 1], to_x(o)))
        return copies

    def to_partner(i):
        a, lo, mid, hi = chunks[i]
        part = outs[a].at[:, :, :, c, :, lo:hi]
        return [remote(part, part, cs.at[i], cr.at[i], index(n, z, y, x, 1 - c))]

    run_stages(len(chunks), LAG, [along_z, first_side, second_side, to_partner, lambda i: []])


def gather(n, shards, target, cid):
    Z, Y, X = dims_of(n)
    chunks = cut([s.shape[1] for s in shards], target)
    N, ends, sides = len(chunks), max(Z - 1, 1), max(X, Y, 2) - 1
    got = pl.pallas_call(
        functools.partial(gather_kernel, n, chunks, len(shards)),
        out_shape=[jax.ShapeDtypeStruct((Z, Y, X, 2) + s.shape, s.dtype) for s in shards],
        in_specs=[ANY] * len(shards),
        out_specs=[ANY] * len(shards),
        scratch_shapes=[DMA((N,)), DMA((N, ends)), DMA((N, ends))]
        + [DMA((N, 2, sides))] * 4
        + [DMA((N,)), DMA((N,))],
        compiler_params=pltpu.CompilerParams(
            collective_id=cid, has_side_effects=True, vmem_limit_bytes=1 << 20
        ),
    )(*shards)
    return [g.reshape(n * s.shape[0], s.shape[1]) for g, s in zip(got, shards)]


def scatter_kernel(n, chunks, count, K, *refs):
    Z, Y, X = dims_of(n)
    ins, outs = refs[:count], refs[count : 2 * count]
    L0, R0, P1, R1, P2, R2, R3, ls, s0, r0, s1, r1, s2, r2, s3, r3 = refs[2 * count :]
    z, y, x, c = place(n)
    greet(n, z, y, x, c)

    def from_partner(i):
        a, lo, mid, hi = chunks[i]
        k, w = i % K, hi - lo
        own = pltpu.make_async_copy(
            ins[a].at[:, :, :, c, :, lo:hi], L0.at[k, :, :, :, :, 0:w], ls.at[k]
        )
        own.start()
        return [
            own,
            remote(
                ins[a].at[:, :, :, 1 - c, :, lo:hi],
                R0.at[k, :, :, :, :, 0:w],
                s0.at[k],
                r0.at[k],
                index(n, z, y, x, 1 - c),
            ),
        ]

    def first_side(i):
        a, lo, mid, hi = chunks[i]
        k, w, h = i % K, hi - lo, mid - lo

        def add(j, carry):
            at = (k, j // (Y * X), lax.rem(j // X, Y), lax.rem(j, X), slice(None), slice(0, w))
            L0[at] = (L0[at].astype(f32) + R0[at].astype(f32)).astype(bf16)
            return carry

        lax.fori_loop(0, Z * Y * X, add, 0)
        copies = []
        for o in range(1, Y if h > 0 else 1):
            d = lax.rem(y + o, Y)
            src, dst = L0.at[k, :, d, :, :, 0:h], R1.at[k, o - 1, :, 0:X, :, 0:h]
            copies.append(remote(src, dst, s1.at[k, 0, o - 1], r1.at[k, 0, o - 1], index(n, z, d, x, c)))
        for o in range(1, X):
            d = lax.rem(x + o, X)
            src, dst = L0.at[k, :, :, d, :, h:w], R1.at[k, o - 1, :, 0:Y, :, h:w]
            copies.append(remote(src, dst, s1.at[k, 1, o - 1], r1.at[k, 1, o - 1], index(n, z, y, d, c)))
        return copies

    def second_side(i):
        a, lo, mid, hi = chunks[i]
        k, w, h = i % K, hi - lo, mid - lo
        for half, start, end, size, terms in ((0, 0, h, X, Y), (1, h, w, Y, X)):
            if start == end:
                continue

            def add(j, carry):
                zz, ss = j // size, lax.rem(j, size)
                if half == 0:
                    total = L0[k, zz, y, ss, :, start:end].astype(f32)
                else:
                    total = L0[k, zz, ss, x, :, start:end].astype(f32)
                for o in range(1, terms):
                    total = total + R1[k, o - 1, zz, ss, :, start:end].astype(f32)
                P1[k, zz, ss, :, start:end] = total.astype(bf16)
                return carry

            lax.fori_loop(0, Z * size, add, 0)
        copies = []
        for o in range(1, X if h > 0 else 1):
            d = lax.rem(x + o, X)
            src, dst = P1.at[k, :, d, :, 0:h], R2.at[k, o - 1, :, :, 0:h]
            copies.append(remote(src, dst, s2.at[k, 0, o - 1], r2.at[k, 0, o - 1], index(n, z, y, d, c)))
        for o in range(1, Y):
            d = lax.rem(y + o, Y)
            src, dst = P1.at[k, :, d, :, h:w], R2.at[k, o - 1, :, :, h:w]
            copies.append(remote(src, dst, s2.at[k, 1, o - 1], r2.at[k, 1, o - 1], index(n, z, d, x, c)))
        return copies

    def along_z(i):
        a, lo, mid, hi = chunks[i]
        k, w, h = i % K, hi - lo, mid - lo
        for start, end, terms, mine in ((0, h, X, x), (h, w, Y, y)):
            if start == end:
                continue

            def add(zz, carry):
                total = P1[k, zz, mine, :, start:end].astype(f32)
                for o in range(1, terms):
                    total = total + R2[k, o - 1, zz, :, start:end].astype(f32)
                P2[k, zz, :, start:end] = total.astype(bf16)
                return carry

            lax.fori_loop(0, Z, add, 0)
        copies = []
        for o in range(1, Z):
            d = lax.rem(z + o, Z)
            src, dst = P2.at[k, d, :, 0:w], R3.at[k, o - 1, :, 0:w]
            copies.append(remote(src, dst, s3.at[k, o - 1], r3.at[k, o - 1], index(n, d, y, x, c)))
        return copies

    def finish(i):
        a, lo, mid, hi = chunks[i]
        k, w = i % K, hi - lo
        total = P2[k, z, :, 0:w].astype(f32)
        for o in range(1, Z):
            total = total + R3[k, o - 1, :, 0:w].astype(f32)
        outs[a][:, lo:hi] = total
        return []

    run_stages(len(chunks), LAG, [from_partner, first_side, second_side, along_z, finish])


def scatter(n, parts, target, cid):
    Z, Y, X = dims_of(n)
    chunks = cut([p.shape[1] for p in parts], target)
    K = 2 * LAG + 1
    rows = parts[0].shape[0] // n
    most = max(X, Y)
    sides, ends = max(most, 2) - 1, max(Z - 1, 1)
    wide = max(hi - lo for a, lo, mid, hi in chunks)
    vmem = lambda *shape: pltpu.VMEM((K,) + shape + (rows, wide), bf16)
    return pl.pallas_call(
        functools.partial(scatter_kernel, n, chunks, len(parts), K),
        out_shape=[jax.ShapeDtypeStruct((rows, p.shape[1]), f32) for p in parts],
        in_specs=[ANY] * len(parts),
        out_specs=[pl.BlockSpec(memory_space=pltpu.VMEM)] * len(parts),
        scratch_shapes=[
            vmem(Z, Y, X),
            vmem(Z, Y, X),
            vmem(Z, most),
            vmem(sides, Z, most),
            vmem(Z),
            vmem(sides, Z),
            vmem(ends),
        ]
        + [DMA((K,))] * 3
        + [DMA((K, 2, sides))] * 4
        + [DMA((K, ends))] * 2,
        compiler_params=pltpu.CompilerParams(
            collective_id=cid, has_side_effects=True, vmem_limit_bytes=60 << 20
        ),
    )(*[p.reshape((Z, Y, X, 2, rows, p.shape[1])) for p in parts])


def tree_allowed(parents, lengths, tree):
    count = parents.shape[1]
    seg = jnp.arange(count, dtype=jnp.int32)
    identity = jnp.eye(count, dtype=f32)
    step_up = (parents[:, :, None] == seg) & (seg[:, None] > 0)
    reach = identity + step_up.astype(f32)
    power = 1
    while power < count:
        reach = jnp.minimum(jnp.einsum("tab,tbc->tac", reach, reach), 1.0)
        power *= 2
    ends = jnp.cumsum(lengths, axis=1, dtype=jnp.int32)
    positions = jnp.arange(tree, dtype=jnp.int32)
    segment = jnp.sum((ends[:, None, :] <= positions[:, None]).astype(jnp.int32), axis=2)
    member = (segment[:, :, None] == seg).astype(f32)
    linked = jnp.einsum("tia,tja->tij", jnp.einsum("tib,tba->tia", member, reach), member) > 0.5
    return linked & (positions[None, :] <= positions[:, None])


def mm(left, right):
    return jnp.einsum("ta,ab->tb", left, right, preferred_element_type=f32)


def mm_t(left, right):
    return jnp.einsum("tb,ab->ta", left, right, preferred_element_type=f32)


def outer(left, right):
    return jnp.einsum("ta,tb->ab", left, right, preferred_element_type=f32)


def norm_rows(resid, gain):
    scale = lax.rsqrt(jnp.mean(resid * resid, axis=-1, keepdims=True) + epsilon)
    return scale, (resid * scale * gain.astype(f32)).astype(bf16)


def norm_back(grad_normed, resid, scale, gain):
    gain_grad = jnp.sum(grad_normed * resid * scale, axis=0)
    weighted = grad_normed * gain.astype(f32)
    inner = jnp.mean(weighted * resid, axis=-1, keepdims=True)
    return gain_grad, scale * weighted - resid * (scale * scale * scale) * inner


def heads_of(rows, trees):
    return rows.reshape(trees, -1, HEADS, HD)


def flat(rows):
    return rows.reshape(-1, HEADS * HD)


def masked_scores(q, k, allowed):
    scores = jnp.einsum("bqhd,bkhd->bhqk", q, k, preferred_element_type=f32)
    return jnp.where(allowed[:, None], scores * (1.0 / math.sqrt(HD)), -1e30)


def groups_of(c):
    return [c[:, g * LAT : (g + 1) * LAT] for g in range(GROUPS)]


def halves(rows):
    w = HEADS // GROUPS * HD
    return [rows[:, g * w : (g + 1) * w] for g in range(GROUPS)]


def layer_forward(resid, weights, gains, allowed):
    wq, wl, wk, wv, wo, wg, wu, wd = weights
    trees = allowed.shape[0]
    scale1, n1 = norm_rows(resid, gains[0])
    q = mm(n1, wq).astype(bf16)
    c = mm(n1, wl).astype(bf16)
    k = jnp.concatenate([mm(cg, wk[g]) for g, cg in enumerate(groups_of(c))], 1).astype(bf16)
    v = jnp.concatenate([mm(cg, wv[g]) for g, cg in enumerate(groups_of(c))], 1).astype(bf16)
    scores = masked_scores(heads_of(q, trees), heads_of(k, trees), allowed)
    top = jnp.max(scores, axis=-1, keepdims=True)
    exponent = jnp.exp(scores - top)
    total = jnp.sum(exponent, axis=-1, keepdims=True)
    log_total = top + jnp.log(total)
    probs = (exponent / total).astype(bf16)
    o = jnp.einsum("bhqk,bkhd->bqhd", probs, heads_of(v, trees), preferred_element_type=f32)
    o = flat(o.astype(bf16))
    middle = resid + mm_t(o, wo)
    scale2, n2 = norm_rows(middle, gains[1])
    a = mm(n2, wg)
    b = mm(n2, wu)
    hidden = (jax.nn.silu(a) * b).astype(bf16)
    out = middle + mm_t(hidden, wd)
    return out, (resid, scale1, n1, q, c, k, v, log_total, o, middle, scale2, n2, a, b, hidden)


def layer_backward(grad, kept, weights, gains, allowed):
    wq, wl, wk, wv, wo, wg, wu, wd = weights
    resid, scale1, n1, q, c, k, v, log_total, o, middle, scale2, n2, a, b, hidden = kept
    trees = allowed.shape[0]
    head_scale = 1.0 / math.sqrt(HD)
    gf = grad.astype(bf16)
    d_down = outer(gf, hidden)
    dz = mm(gf, wd)
    sig = jax.nn.sigmoid(a)
    da = (dz * b * sig * (1.0 + a * (1.0 - sig))).astype(bf16)
    db = (dz * a * sig).astype(bf16)
    d_gate = outer(n2, da)
    d_up = outer(n2, db)
    dm = mm_t(da, wg) + mm_t(db, wu)
    d_gain2, back = norm_back(dm, middle, scale2, gains[1])
    grad1 = grad + back
    ga = grad1.astype(bf16)
    d_out = outer(ga, o)
    do = heads_of(mm(ga, wo).astype(bf16), trees)
    qh, kh, vh = heads_of(q, trees), heads_of(k, trees), heads_of(v, trees)
    probs = jnp.exp(masked_scores(qh, kh, allowed) - log_total)
    dv = jnp.einsum("bhqk,bqhd->bkhd", probs.astype(bf16), do, preferred_element_type=f32)
    dp = jnp.einsum("bqhd,bkhd->bhqk", do, vh, preferred_element_type=f32)
    ds = (probs * (dp - jnp.sum(probs * dp, axis=-1, keepdims=True))).astype(bf16)
    dq = jnp.einsum("bhqk,bkhd->bqhd", ds, kh, preferred_element_type=f32) * head_scale
    dk = jnp.einsum("bhqk,bqhd->bkhd", ds, qh, preferred_element_type=f32) * head_scale
    dq, dk, dv = flat(dq.astype(bf16)), flat(dk.astype(bf16)), flat(dv.astype(bf16))
    cg, dkg, dvg = groups_of(c), halves(dk), halves(dv)
    d_key = jnp.stack([outer(cg[g], dkg[g]) for g in range(GROUPS)])
    d_value = jnp.stack([outer(cg[g], dvg[g]) for g in range(GROUPS)])
    dc = jnp.concatenate(
        [mm_t(dkg[g], wk[g]) + mm_t(dvg[g], wv[g]) for g in range(GROUPS)], 1
    ).astype(bf16)
    d_latent = outer(n1, dc)
    d_query = outer(n1, dq)
    dn = mm_t(dq, wq) + mm_t(dc, wl)
    d_gain1, back = norm_back(dn, resid, scale1, gains[0])
    return grad1 + back, (d_query, d_latent, d_key, d_value, d_out, d_gate, d_up, d_down), (d_gain1, d_gain2)


def body(inputs, cotangent, parents, lengths, g1, wq, wl, wk, wv, wo, g2, wg, wu, wd, *, n):
    trees, tree, width = inputs.shape
    rows = wq.shape[1]
    latr = wk.shape[2]

    def packed(layer):
        cast = lambda w: w[layer].astype(bf16)
        kv = jnp.stack([wk[layer], wv[layer]]).astype(bf16).reshape(-1, wk.shape[3])
        return [cast(wq), cast(wl), kv, cast(wo).T, cast(wg), cast(wu), cast(wd).T]

    gain_rows = jnp.stack([g1[0], g2[0], g1[1], g2[1]], axis=1).astype(bf16)
    gain_rows = jnp.pad(gain_rows, ((0, 0), (0, 128 - 2 * LAYERS)))
    got = gather(n, [gain_rows] + packed(0) + packed(1), 704, 0)
    gains = got[0][:, : 2 * LAYERS].T.reshape(LAYERS, 2, width)

    def unpacked(part):
        q, l, kv, o, g, u, d = part
        kv = kv.reshape(n, 2, GROUPS, latr, -1).transpose(1, 2, 0, 3, 4).reshape(2, GROUPS, LAT, -1)
        return (q, l, kv[0], kv[1], o, g, u, d)

    weights = [unpacked(got[1:8]), unpacked(got[8:15])]
    allowed = tree_allowed(parents, lengths, tree)
    resid = inputs.reshape(trees * tree, width).astype(f32)
    kept = []
    for layer in range(LAYERS):
        resid, keep = layer_forward(resid, weights[layer], gains[layer], allowed)
        kept.append(keep)
    outputs = resid.reshape(inputs.shape)
    grad = cotangent.reshape(trees * tree, width)
    parts, gain_grads = [None] * LAYERS, [None] * LAYERS
    for layer in reversed(range(LAYERS)):
        grad, grads, gain_grads[layer] = layer_backward(
            grad, kept[layer], weights[layer], gains[layer], allowed
        )
        dq, dl, dk, dv, do, dg, du, dd = [d.astype(bf16) for d in grads]
        kv = jnp.stack([dk, dv]).reshape(2, GROUPS, n, latr, -1).transpose(2, 0, 1, 3, 4)
        parts[layer] = [dd, dg, du, do, dq, dl, kv.reshape(n * rows, -1)]
    gain_part = jnp.stack(gain_grads[0] + gain_grads[1], axis=1).astype(bf16)
    gain_part = jnp.pad(gain_part, ((0, 0), (0, 128 - 2 * LAYERS)))
    summed = scatter(n, parts[1] + parts[0] + [gain_part], 704, 1)
    out = []
    for layer in range(LAYERS):
        dd, dg, du, do, dq, dl, kv = summed[(1 - layer) * 7 : (1 - layer) * 7 + 7]
        kv = kv.reshape(2, GROUPS, latr, -1)
        gain = summed[14]
        out.append(
            (gain[:, 2 * layer], dq, dl, kv[0], kv[1], do.T, gain[:, 2 * layer + 1], dg, du, dd.T)
        )
    stacked = tuple(jnp.stack([out[layer][slot] for layer in range(LAYERS)]) for slot in range(10))
    return (outputs, grad.reshape(inputs.shape)) + stacked


def solution(mesh):
    n = mesh.shape["fsdp"]
    by_one, by_two = P(None, "fsdp"), P(None, "fsdp", None)
    by_lat, by_last = P(None, None, "fsdp", None), P(None, None, "fsdp")
    params = (by_one, by_two, by_two, by_lat, by_lat, by_last, by_one, by_two, by_two, by_last)
    trees = P("fsdp", None, None)
    return jax.shard_map(
        functools.partial(body, n=n),
        mesh=mesh,
        in_specs=(trees, trees, P("fsdp", None), P("fsdp", None)) + params,
        out_specs=(trees, trees) + params,
        check_vma=False,
    )
```

```python
import functools
import math

import jax
import jax.numpy as jnp
from jax import lax
from jax.experimental import pallas as pl
from jax.experimental.pallas import tpu as pltpu
from jax.sharding import PartitionSpec as P

HEADS = 16
HD = 64
GROUPS = 2
LAT = 256
LAYERS = 2
LAG = 2
epsilon = 1e-05

MESH = pl.DeviceIdType.MESH
ANY = pl.BlockSpec(memory_space=pl.ANY)
DMA = pltpu.SemaphoreType.DMA
bf16 = jnp.bfloat16
f32 = jnp.float32


def dims_of(n):
    chips = n // 2
    side = 1
    if chips & (chips - 1) == 0:
        side = 2 ** ((chips.bit_length() - 1) // 3)
    return chips // (side * side), side, side


def index(n, z, y, x, c):
    Z, Y, X = dims_of(n)
    return ((z * Y + y) * X + x) * 2 + c


def place(n):
    Z, Y, X = dims_of(n)
    me = lax.axis_index("fsdp")
    return me // (2 * X * Y), lax.rem(me // (2 * X), Y), lax.rem(me // 2, X), lax.rem(me, 2)


def greet(n, z, y, x, c):
    Z, Y, X = dims_of(n)
    peers = [index(n, lax.rem(z + o, Z), y, x, c) for o in range(1, Z)]
    peers += [index(n, z, lax.rem(y + o, Y), x, c) for o in range(1, Y)]
    peers += [index(n, z, y, lax.rem(x + o, X), c) for o in range(1, X)]
    peers += [index(n, z, y, x, 1 - c)]
    bar = pltpu.get_barrier_semaphore()
    for peer in peers:
        pl.semaphore_signal(bar, inc=1, device_id=(peer,), device_id_type=MESH)
    pl.semaphore_wait(bar, len(peers))


def remote(src, dst, send, recv, device):
    copy = pltpu.make_async_remote_copy(
        src_ref=src,
        dst_ref=dst,
        send_sem=send,
        recv_sem=recv,
        device_id=(device,),
        device_id_type=MESH,
    )
    copy.start()
    return copy


def cut(widths, target):
    out = []
    for a, w in enumerate(widths):
        k, u = max(1, round(w / target)), w // 128
        edges = [round(j * u / k) * 128 for j in range(k + 1)]
        for lo, hi in zip(edges, edges[1:]):
            half = (hi - lo) // 128
            half = half // 2 if len(out) % 2 == 0 else (half + 1) // 2
            out.append((a, lo, lo + half * 128, hi))
    return out


def run_stages(count, lag, stages):
    held = [None] * count
    last = len(stages) - 1
    for slot in range(count + lag * last):
        for s in range(last, -1, -1):
            i = slot - lag * s
            if 0 <= i < count:
                if s > 0:
                    for copy in held[i]:
                        copy.wait()
                held[i] = stages[s](i)


def gather_kernel(n, chunks, count, *refs):
    Z, Y, X = dims_of(n)
    ins, outs = refs[:count], refs[count : 2 * count]
    own_sem, zs, zr, as_, ar, bs, br, cs, cr = refs[2 * count :]
    z, y, x, c = place(n)
    greet(n, z, y, x, c)

    def along_z(i):
        a, lo, mid, hi = chunks[i]
        src, dst = ins[a].at[:, lo:hi], outs[a].at[z, y, x, c, :, lo:hi]
        own = pltpu.make_async_copy(src, dst, own_sem.at[i])
        own.start()
        return [own] + [
            remote(src, dst, zs.at[i, o - 1], zr.at[i, o - 1], index(n, lax.rem(z + o, Z), y, x, c))
            for o in range(1, Z)
        ]

    def to_x(o):
        return index(n, z, y, lax.rem(x + o, X), c)

    def to_y(o):
        return index(n, z, lax.rem(y + o, Y), x, c)

    def first_side(i):
        a, lo, mid, hi = chunks[i]
        copies = []
        for h, (start, end, size, to) in enumerate(((lo, mid, X, to_x), (mid, hi, Y, to_y))):
            part = outs[a].at[:, y, x, c, :, start:end]
            for o in range(1, size if end > start else 1):
                copies.append(remote(part, part, as_.at[i, h, o - 1], ar.at[i, h, o - 1], to(o)))
        return copies

    def second_side(i):
        a, lo, mid, hi = chunks[i]
        copies = []
        for o in range(1, Y if mid > lo else 1):
            part = outs[a].at[:, y, :, c, :, lo:mid]
            copies.append(remote(part, part, bs.at[i, 0, o - 1], br.at[i, 0, o - 1], to_y(o)))
        for o in range(1, X):
            part = outs[a].at[:, :, x, c, :, mid:hi]
            copies.append(remote(part, part, bs.at[i, 1, o - 1], br.at[i, 1, o - 1], to_x(o)))
        return copies

    def to_partner(i):
        a, lo, mid, hi = chunks[i]
        part = outs[a].at[:, :, :, c, :, lo:hi]
        return [remote(part, part, cs.at[i], cr.at[i], index(n, z, y, x, 1 - c))]

    run_stages(len(chunks), LAG, [along_z, first_side, second_side, to_partner, lambda i: []])


def gather(n, shards, target, cid):
    Z, Y, X = dims_of(n)
    chunks = cut([s.shape[1] for s in shards], target)
    N, ends, sides = len(chunks), max(Z - 1, 1), max(X, Y, 2) - 1
    got = pl.pallas_call(
        functools.partial(gather_kernel, n, chunks, len(shards)),
        out_shape=[jax.ShapeDtypeStruct((Z, Y, X, 2) + s.shape, s.dtype) for s in shards],
        in_specs=[ANY] * len(shards),
        out_specs=[ANY] * len(shards),
        scratch_shapes=[DMA((N,)), DMA((N, ends)), DMA((N, ends))]
        + [DMA((N, 2, sides))] * 4
        + [DMA((N,)), DMA((N,))],
        compiler_params=pltpu.CompilerParams(
            collective_id=cid, has_side_effects=True, vmem_limit_bytes=1 << 20
        ),
    )(*shards)
    return [g.reshape(n * s.shape[0], s.shape[1]) for g, s in zip(got, shards)]


def scatter_kernel(n, jobs, lefts, chunks, K, *refs):
    Z, Y, X = dims_of(n)
    count = len(jobs)
    left_refs, ins, outs = refs[:lefts], refs[lefts : lefts + count], refs[lefts + count : lefts + 2 * count]
    (LB, RB, G, R0, P1, R1, P2, R2, R3, lsem, ls, s0, r0, s1, r1, s2, r2, s3, r3) = refs[lefts + 2 * count :]
    z, y, x, c = place(n)
    rows = G.shape[5]

    order = []
    for a, lo, mid, hi in chunks:
        if jobs[a][0] is not None and (not order or order[-1] != jobs[a][0]):
            order.append(jobs[a][0])
    firsts, turn = {}, -1
    for i, (a, lo, mid, hi) in enumerate(chunks):
        left = jobs[a][0]
        if left is not None and (turn < 0 or order[turn] != left):
            turn += 1
            firsts[i] = turn
    turn_of, now = {}, -1
    for i in range(len(chunks)):
        now = firsts.get(i, now)
        turn_of[i] = now

    def left_copy(t):
        return pltpu.make_async_copy(left_refs[order[t]], LB.at[t % 2], lsem.at[t % 2])

    def load(i):
        a, lo, mid, hi = chunks[i]
        if jobs[a][0] is None:
            src, dst = ins[a].at[:, :, :, :, :, lo:hi], G.at[i % K, :, :, :, :, :, 0 : hi - lo]
        else:
            src, dst = ins[a].at[:, lo:hi], RB.at[i % 2, :, 0 : hi - lo]
        return pltpu.make_async_copy(src, dst, ls.at[i % 2])

    left_copy(0).start()
    if len(order) > 1:
        left_copy(1).start()
    load(0).start()
    greet(n, z, y, x, c)

    def from_partner(i):
        a, lo, mid, hi = chunks[i]
        k, w = i % K, hi - lo
        load(i).wait()
        if i + 1 < len(chunks):
            load(i + 1).start()
        t = turn_of[i]
        if jobs[a][0] is not None:
            if i in firsts:
                left_copy(t).wait()
            depth = LB.shape[2] // Z

            def block(zz, carry):
                at = pl.ds(pl.multiple_of(zz * depth, depth), depth)
                part = lax.dot_general(
                    LB[t % 2, :, at],
                    RB[i % 2, :, 0:w],
                    (((0,), (0,)), ((), ())),
                    preferred_element_type=f32,
                )
                G[k, zz, :, :, :, :, 0:w] = part.astype(bf16).reshape(Y, X, 2, rows, w)
                return carry

            lax.fori_loop(0, Z, block, 0)
        if i + 1 in firsts and 0 <= t < len(order) - 2:
            left_copy(t + 2).start()
        return [
            remote(
                G.at[k, :, :, :, 1 - c, :, 0:w],
                R0.at[k, :, :, :, :, 0:w],
                s0.at[k],
                r0.at[k],
                index(n, z, y, x, 1 - c),
            )
        ]

    def first_side(i):
        a, lo, mid, hi = chunks[i]
        k, w, h = i % K, hi - lo, mid - lo

        def add(j, carry):
            zz, yy, xx = j // (Y * X), lax.rem(j // X, Y), lax.rem(j, X)
            total = G[k, zz, yy, xx, c, :, 0:w].astype(f32) + R0[k, zz, yy, xx, :, 0:w].astype(f32)
            G[k, zz, yy, xx, c, :, 0:w] = total.astype(bf16)
            return carry

        lax.fori_loop(0, Z * Y * X, add, 0)
        copies = []
        for o in range(1, Y if h > 0 else 1):
            d = lax.rem(y + o, Y)
            src, dst = G.at[k, :, d, :, c, :, 0:h], R1.at[k, o - 1, :, 0:X, :, 0:h]
            copies.append(remote(src, dst, s1.at[k, 0, o - 1], r1.at[k, 0, o - 1], index(n, z, d, x, c)))
        for o in range(1, X):
            d = lax.rem(x + o, X)
            src, dst = G.at[k, :, :, d, c, :, h:w], R1.at[k, o - 1, :, 0:Y, :, h:w]
            copies.append(remote(src, dst, s1.at[k, 1, o - 1], r1.at[k, 1, o - 1], index(n, z, y, d, c)))
        return copies

    def second_side(i):
        a, lo, mid, hi = chunks[i]
        k, w, h = i % K, hi - lo, mid - lo
        for half, start, end, size, terms in ((0, 0, h, X, Y), (1, h, w, Y, X)):
            if start == end:
                continue

            def add(j, carry):
                zz, ss = j // size, lax.rem(j, size)
                if half == 0:
                    total = G[k, zz, y, ss, c, :, start:end].astype(f32)
                else:
                    total = G[k, zz, ss, x, c, :, start:end].astype(f32)
                for o in range(1, terms):
                    total = total + R1[k, o - 1, zz, ss, :, start:end].astype(f32)
                P1[k, zz, ss, :, start:end] = total.astype(bf16)
                return carry

            lax.fori_loop(0, Z * size, add, 0)
        copies = []
        for o in range(1, X if h > 0 else 1):
            d = lax.rem(x + o, X)
            src, dst = P1.at[k, :, d, :, 0:h], R2.at[k, o - 1, :, :, 0:h]
            copies.append(remote(src, dst, s2.at[k, 0, o - 1], r2.at[k, 0, o - 1], index(n, z, y, d, c)))
        for o in range(1, Y):
            d = lax.rem(y + o, Y)
            src, dst = P1.at[k, :, d, :, h:w], R2.at[k, o - 1, :, :, h:w]
            copies.append(remote(src, dst, s2.at[k, 1, o - 1], r2.at[k, 1, o - 1], index(n, z, d, x, c)))
        return copies

    def along_z(i):
        a, lo, mid, hi = chunks[i]
        k, w, h = i % K, hi - lo, mid - lo
        for start, end, terms, mine in ((0, h, X, x), (h, w, Y, y)):
            if start == end:
                continue

            def add(zz, carry):
                total = P1[k, zz, mine, :, start:end].astype(f32)
                for o in range(1, terms):
                    total = total + R2[k, o - 1, zz, :, start:end].astype(f32)
                P2[k, zz, :, start:end] = total.astype(bf16)
                return carry

            lax.fori_loop(0, Z, add, 0)
        copies = []
        for o in range(1, Z):
            d = lax.rem(z + o, Z)
            src, dst = P2.at[k, d, :, 0:w], R3.at[k, o - 1, :, 0:w]
            copies.append(remote(src, dst, s3.at[k, o - 1], r3.at[k, o - 1], index(n, d, y, x, c)))
        return copies

    def finish(i):
        a, lo, mid, hi = chunks[i]
        k, w = i % K, hi - lo
        total = P2[k, z, :, 0:w].astype(f32)
        for o in range(1, Z):
            total = total + R3[k, o - 1, :, 0:w].astype(f32)
        outs[a][:, lo:hi] = total
        return []

    run_stages(len(chunks), LAG, [from_partner, first_side, second_side, along_z, finish])


def scatter(n, lefts, jobs, target, cid):
    Z, Y, X = dims_of(n)
    parts = [part for left, part in jobs]
    chunks = cut([p.shape[1] for p in parts], target)
    K = 2 * LAG + 1
    tokens, width = lefts[0].shape
    rows = width // n
    most = max(X, Y)
    sides, ends = max(most, 2) - 1, max(Z - 1, 1)
    wide = max(hi - lo for a, lo, mid, hi in chunks)
    vmem = lambda *shape: pltpu.VMEM((K,) + shape + (rows, wide), bf16)
    jobs = [left for left, part in jobs]
    operands = [
        p if left is not None else p.reshape((Z, Y, X, 2, rows, p.shape[1])) for left, p in zip(jobs, parts)
    ]
    return pl.pallas_call(
        functools.partial(scatter_kernel, n, [(left, None) for left in jobs], len(lefts), chunks, K),
        out_shape=[jax.ShapeDtypeStruct((rows, p.shape[1]), f32) for p in parts],
        in_specs=[ANY] * (len(lefts) + len(parts)),
        out_specs=[pl.BlockSpec(memory_space=pltpu.VMEM)] * len(parts),
        scratch_shapes=[
            pltpu.VMEM((2, tokens, width), bf16),
            pltpu.VMEM((2, tokens, wide), bf16),
            vmem(Z, Y, X, 2),
            vmem(Z, Y, X),
            vmem(Z, most),
            vmem(sides, Z, most),
            vmem(Z),
            vmem(sides, Z),
            vmem(ends),
            DMA((2,)),
            DMA((2,)),
            DMA((K,)),
            DMA((K,)),
        ]
        + [DMA((K, 2, sides))] * 4
        + [DMA((K, ends))] * 2,
        compiler_params=pltpu.CompilerParams(
            collective_id=cid, has_side_effects=True, vmem_limit_bytes=60 << 20
        ),
    )(*lefts, *operands)


def tree_allowed(parents, lengths, tree):
    count = parents.shape[1]
    seg = jnp.arange(count, dtype=jnp.int32)
    identity = jnp.eye(count, dtype=f32)
    step_up = (parents[:, :, None] == seg) & (seg[:, None] > 0)
    reach = identity + step_up.astype(f32)
    power = 1
    while power < count:
        reach = jnp.minimum(jnp.einsum("tab,tbc->tac", reach, reach), 1.0)
        power *= 2
    ends = jnp.cumsum(lengths, axis=1, dtype=jnp.int32)
    positions = jnp.arange(tree, dtype=jnp.int32)
    segment = jnp.sum((ends[:, None, :] <= positions[:, None]).astype(jnp.int32), axis=2)
    member = (segment[:, :, None] == seg).astype(f32)
    linked = jnp.einsum("tia,tja->tij", jnp.einsum("tib,tba->tia", member, reach), member) > 0.5
    return linked & (positions[None, :] <= positions[:, None])


def mm(left, right):
    return jnp.einsum("ta,ab->tb", left, right, preferred_element_type=f32)


def mm_t(left, right):
    return jnp.einsum("tb,ab->ta", left, right, preferred_element_type=f32)


def outer(left, right):
    return jnp.einsum("ta,tb->ab", left, right, preferred_element_type=f32)


def norm_rows(resid, gain):
    scale = lax.rsqrt(jnp.mean(resid * resid, axis=-1, keepdims=True) + epsilon)
    return scale, (resid * scale * gain.astype(f32)).astype(bf16)


def norm_back(grad_normed, resid, scale, gain):
    gain_grad = jnp.sum(grad_normed * resid * scale, axis=0)
    weighted = grad_normed * gain.astype(f32)
    inner = jnp.mean(weighted * resid, axis=-1, keepdims=True)
    return gain_grad, scale * weighted - resid * (scale * scale * scale) * inner


def heads_of(rows, trees):
    return rows.reshape(trees, -1, HEADS, HD)


def flat(rows):
    return rows.reshape(-1, HEADS * HD)


def masked_scores(q, k, allowed):
    scores = jnp.einsum("bqhd,bkhd->bhqk", q, k, preferred_element_type=f32)
    return jnp.where(allowed[:, None], scores * (1.0 / math.sqrt(HD)), -1e30)


def groups_of(c):
    return [c[:, g * LAT : (g + 1) * LAT] for g in range(GROUPS)]


def halves(rows):
    w = HEADS // GROUPS * HD
    return [rows[:, g * w : (g + 1) * w] for g in range(GROUPS)]


def layer_forward(resid, weights, gains, allowed):
    wq, wl, wk, wv, wo, wg, wu, wd = weights
    trees = allowed.shape[0]
    scale1, n1 = norm_rows(resid, gains[0])
    q = mm(n1, wq).astype(bf16)
    c = mm(n1, wl).astype(bf16)
    k = jnp.concatenate([mm(cg, wk[g]) for g, cg in enumerate(groups_of(c))], 1).astype(bf16)
    v = jnp.concatenate([mm(cg, wv[g]) for g, cg in enumerate(groups_of(c))], 1).astype(bf16)
    scores = masked_scores(heads_of(q, trees), heads_of(k, trees), allowed)
    top = jnp.max(scores, axis=-1, keepdims=True)
    exponent = jnp.exp(scores - top)
    total = jnp.sum(exponent, axis=-1, keepdims=True)
    log_total = top + jnp.log(total)
    probs = (exponent / total).astype(bf16)
    o = jnp.einsum("bhqk,bkhd->bqhd", probs, heads_of(v, trees), preferred_element_type=f32)
    o = flat(o.astype(bf16))
    middle = resid + mm_t(o, wo)
    scale2, n2 = norm_rows(middle, gains[1])
    a = mm(n2, wg)
    b = mm(n2, wu)
    hidden = (jax.nn.silu(a) * b).astype(bf16)
    out = middle + mm_t(hidden, wd)
    return out, (resid, scale1, n1, q, c, k, v, log_total, o, middle, scale2, n2, a, b, hidden)


def layer_backward(grad, kept, weights, gains, allowed):
    wq, wl, wk, wv, wo, wg, wu, wd = weights
    resid, scale1, n1, q, c, k, v, log_total, o, middle, scale2, n2, a, b, hidden = kept
    trees = allowed.shape[0]
    head_scale = 1.0 / math.sqrt(HD)
    gf = grad.astype(bf16)
    dz = mm(gf, wd)
    sig = jax.nn.sigmoid(a)
    da = (dz * b * sig * (1.0 + a * (1.0 - sig))).astype(bf16)
    db = (dz * a * sig).astype(bf16)
    dm = mm_t(da, wg) + mm_t(db, wu)
    d_gain2, back = norm_back(dm, middle, scale2, gains[1])
    grad1 = grad + back
    ga = grad1.astype(bf16)
    do = heads_of(mm(ga, wo).astype(bf16), trees)
    qh, kh, vh = heads_of(q, trees), heads_of(k, trees), heads_of(v, trees)
    probs = jnp.exp(masked_scores(qh, kh, allowed) - log_total)
    dv = jnp.einsum("bhqk,bqhd->bkhd", probs.astype(bf16), do, preferred_element_type=f32)
    dp = jnp.einsum("bqhd,bkhd->bhqk", do, vh, preferred_element_type=f32)
    ds = (probs * (dp - jnp.sum(probs * dp, axis=-1, keepdims=True))).astype(bf16)
    dq = jnp.einsum("bhqk,bkhd->bqhd", ds, kh, preferred_element_type=f32) * head_scale
    dk = jnp.einsum("bhqk,bqhd->bkhd", ds, qh, preferred_element_type=f32) * head_scale
    dq, dk, dv = flat(dq.astype(bf16)), flat(dk.astype(bf16)), flat(dv.astype(bf16))
    cg, dkg, dvg = groups_of(c), halves(dk), halves(dv)
    d_key = jnp.stack([outer(cg[g], dkg[g]) for g in range(GROUPS)])
    d_value = jnp.stack([outer(cg[g], dvg[g]) for g in range(GROUPS)])
    dc = jnp.concatenate(
        [mm_t(dkg[g], wk[g]) + mm_t(dvg[g], wv[g]) for g in range(GROUPS)], 1
    ).astype(bf16)
    dn = mm_t(dq, wq) + mm_t(dc, wl)
    d_gain1, back = norm_back(dn, resid, scale1, gains[0])
    lefts = [gf, n2, ga, n1]
    jobs = [(0, hidden), (1, da), (1, db), (2, o), (3, dq), (3, dc)]
    return grad1 + back, lefts, jobs, (d_key, d_value), (d_gain1, d_gain2)


def body(inputs, cotangent, parents, lengths, g1, wq, wl, wk, wv, wo, g2, wg, wu, wd, *, n):
    trees, tree, width = inputs.shape
    rows = wq.shape[1]
    latr = wk.shape[2]

    def packed(layer):
        cast = lambda w: w[layer].astype(bf16)
        kv = jnp.stack([wk[layer], wv[layer]]).astype(bf16).reshape(-1, wk.shape[3])
        return [cast(wq), cast(wl), kv, cast(wo).T, cast(wg), cast(wu), cast(wd).T]

    gain_rows = jnp.stack([g1[0], g2[0], g1[1], g2[1]], axis=1).astype(bf16)
    gain_rows = jnp.pad(gain_rows, ((0, 0), (0, 128 - 2 * LAYERS)))
    got = gather(n, [gain_rows] + packed(0) + packed(1), 704, 0)
    gains = got[0][:, : 2 * LAYERS].T.reshape(LAYERS, 2, width)

    def unpacked(part):
        q, l, kv, o, g, u, d = part
        kv = kv.reshape(n, 2, GROUPS, latr, -1).transpose(1, 2, 0, 3, 4).reshape(2, GROUPS, LAT, -1)
        return (q, l, kv[0], kv[1], o, g, u, d)

    weights = [unpacked(got[1:8]), unpacked(got[8:15])]
    allowed = tree_allowed(parents, lengths, tree)
    resid = inputs.reshape(trees * tree, width).astype(f32)
    kept = []
    for layer in range(LAYERS):
        resid, keep = layer_forward(resid, weights[layer], gains[layer], allowed)
        kept.append(keep)
    outputs = resid.reshape(inputs.shape)
    grad = cotangent.reshape(trees * tree, width)
    lefts, jobs, gain_grads = [], [], [None] * LAYERS
    for layer in reversed(range(LAYERS)):
        grad, left, job, kv, gain_grads[layer] = layer_backward(
            grad, kept[layer], weights[layer], gains[layer], allowed
        )
        kv = jnp.stack(kv).astype(bf16).reshape(2, GROUPS, n, latr, -1).transpose(2, 0, 1, 3, 4)
        jobs += [(len(lefts) + at, part) for at, part in job] + [(None, kv.reshape(n * rows, -1))]
        lefts += left
    gain_part = jnp.stack(gain_grads[0] + gain_grads[1], axis=1).astype(bf16)
    gain_part = jnp.pad(gain_part, ((0, 0), (0, 128 - 2 * LAYERS)))
    summed = scatter(n, lefts, jobs + [(None, gain_part)], 704, 1)
    out = []
    for layer in range(LAYERS):
        dd, dg, du, do, dq, dl, kv = summed[(1 - layer) * 7 : (1 - layer) * 7 + 7]
        kv = kv.reshape(2, GROUPS, latr, -1)
        gain = summed[14]
        out.append(
            (gain[:, 2 * layer], dq, dl, kv[0], kv[1], do.T, gain[:, 2 * layer + 1], dg, du, dd.T)
        )
    stacked = tuple(jnp.stack([out[layer][slot] for layer in range(LAYERS)]) for slot in range(10))
    return (outputs, grad.reshape(inputs.shape)) + stacked


def solution(mesh):
    n = mesh.shape["fsdp"]
    by_one, by_two = P(None, "fsdp"), P(None, "fsdp", None)
    by_lat, by_last = P(None, None, "fsdp", None), P(None, None, "fsdp")
    params = (by_one, by_two, by_two, by_lat, by_lat, by_last, by_one, by_two, by_two, by_last)
    trees = P("fsdp", None, None)
    return jax.shard_map(
        functools.partial(body, n=n),
        mesh=mesh,
        in_specs=(trees, trees, P("fsdp", None), P("fsdp", None)) + params,
        out_specs=(trees, trees) + params,
        check_vma=False,
    )
```

```python
import functools
import math

import jax
import jax.numpy as jnp
from jax import lax
from jax.experimental import pallas as pl
from jax.experimental.pallas import tpu as pltpu
from jax.sharding import PartitionSpec as P

HEADS = 16
HD = 64
GROUPS = 2
LAT = 256
LAYERS = 2
LAG = 2
epsilon = 1e-05

MESH = pl.DeviceIdType.MESH
ANY = pl.BlockSpec(memory_space=pltpu.HBM)
DMA = pltpu.SemaphoreType.DMA
bf16 = jnp.bfloat16
f32 = jnp.float32


def dims_of(n):
    chips = n // 2
    side = 1
    if chips & (chips - 1) == 0:
        side = 2 ** ((chips.bit_length() - 1) // 3)
    return chips // (side * side), side, side


def index(n, z, y, x, c):
    Z, Y, X = dims_of(n)
    return ((z * Y + y) * X + x) * 2 + c


def place(n):
    Z, Y, X = dims_of(n)
    me = lax.axis_index("fsdp")
    return me // (2 * X * Y), lax.rem(me // (2 * X), Y), lax.rem(me // 2, X), lax.rem(me, 2)


def greet(n, z, y, x, c):
    Z, Y, X = dims_of(n)
    peers = [index(n, lax.rem(z + o, Z), y, x, c) for o in range(1, Z)]
    peers += [index(n, z, lax.rem(y + o, Y), x, c) for o in range(1, Y)]
    peers += [index(n, z, y, lax.rem(x + o, X), c) for o in range(1, X)]
    peers += [index(n, z, y, x, 1 - c)]
    bar = pltpu.get_barrier_semaphore()
    for peer in peers:
        pl.semaphore_signal(bar, inc=1, device_id=(peer,), device_id_type=MESH)
    pl.semaphore_wait(bar, len(peers))


def remote(src, dst, send, recv, device):
    copy = pltpu.make_async_remote_copy(
        src_ref=src,
        dst_ref=dst,
        send_sem=send,
        recv_sem=recv,
        device_id=(device,),
        device_id_type=MESH,
    )
    copy.start()
    return copy


def cut(widths, target):
    out = []
    for a, w in enumerate(widths):
        k, u = max(1, round(w / target)), w // 128
        edges = [round(j * u / k) * 128 for j in range(k + 1)]
        for lo, hi in zip(edges, edges[1:]):
            half = (hi - lo) // 128
            half = half // 2 if len(out) % 2 == 0 else (half + 1) // 2
            out.append((a, lo, lo + half * 128, hi))
    return out


def run_stages(count, lag, stages):
    held = [None] * count
    last = len(stages) - 1
    for slot in range(count + lag * last):
        for s in range(last, -1, -1):
            i = slot - lag * s
            if 0 <= i < count:
                if s > 0:
                    for copy in held[i]:
                        copy.wait()
                held[i] = stages[s](i)


def gather_kernel(n, chunks, count, *refs):
    Z, Y, X = dims_of(n)
    ins, outs = refs[:count], refs[count : 2 * count]
    own_sem, zs, zr, as_, ar, bs, br, cs, cr = refs[2 * count :]
    z, y, x, c = place(n)
    greet(n, z, y, x, c)

    def along_z(i):
        a, lo, mid, hi = chunks[i]
        src, dst = ins[a].at[:, lo:hi], outs[a].at[z, y, x, c, :, lo:hi]
        own = pltpu.make_async_copy(src, dst, own_sem.at[i])
        own.start()
        return [own] + [
            remote(src, dst, zs.at[i, o - 1], zr.at[i, o - 1], index(n, lax.rem(z + o, Z), y, x, c))
            for o in range(1, Z)
        ]

    def to_x(o):
        return index(n, z, y, lax.rem(x + o, X), c)

    def to_y(o):
        return index(n, z, lax.rem(y + o, Y), x, c)

    def first_side(i):
        a, lo, mid, hi = chunks[i]
        copies = []
        for h, (start, end, size, to) in enumerate(((lo, mid, X, to_x), (mid, hi, Y, to_y))):
            part = outs[a].at[:, y, x, c, :, start:end]
            for o in range(1, size if end > start else 1):
                copies.append(remote(part, part, as_.at[i, h, o - 1], ar.at[i, h, o - 1], to(o)))
        return copies

    def second_side(i):
        a, lo, mid, hi = chunks[i]
        copies = []
        for o in range(1, Y if mid > lo else 1):
            part = outs[a].at[:, y, :, c, :, lo:mid]
            copies.append(remote(part, part, bs.at[i, 0, o - 1], br.at[i, 0, o - 1], to_y(o)))
        for o in range(1, X):
            part = outs[a].at[:, :, x, c, :, mid:hi]
            copies.append(remote(part, part, bs.at[i, 1, o - 1], br.at[i, 1, o - 1], to_x(o)))
        return copies

    def to_partner(i):
        a, lo, mid, hi = chunks[i]
        part = outs[a].at[:, :, :, c, :, lo:hi]
        return [remote(part, part, cs.at[i], cr.at[i], index(n, z, y, x, 1 - c))]

    run_stages(len(chunks), LAG, [along_z, first_side, second_side, to_partner, lambda i: []])


def gather(n, shards, target, cid):
    Z, Y, X = dims_of(n)
    chunks = cut([s.shape[1] for s in shards], target)
    N, ends, sides = len(chunks), max(Z - 1, 1), max(X, Y, 2) - 1
    got = pl.pallas_call(
        functools.partial(gather_kernel, n, chunks, len(shards)),
        out_shape=[jax.ShapeDtypeStruct((Z, Y, X, 2) + s.shape, s.dtype) for s in shards],
        in_specs=[ANY] * len(shards),
        out_specs=[ANY] * len(shards),
        scratch_shapes=[DMA((N,)), DMA((N, ends)), DMA((N, ends))]
        + [DMA((N, 2, sides))] * 4
        + [DMA((N,)), DMA((N,))],
        compiler_params=pltpu.CompilerParams(
            collective_id=cid, has_side_effects=True, vmem_limit_bytes=60 << 20
        ),
    )(*shards)
    return [g.reshape(n * s.shape[0], s.shape[1]) for g, s in zip(got, shards)]


def scatter_kernel(n, jobs, lefts, chunks, K, *refs):
    Z, Y, X = dims_of(n)
    count = len(jobs)
    left_refs, ins, outs = refs[:lefts], refs[lefts : lefts + count], refs[lefts + count : lefts + 2 * count]
    (LB, RB, G, R0, P1, R1, P2, R2, R3, lsem, ls, s0, r0, s1, r1, s2, r2, s3, r3) = refs[lefts + 2 * count :]
    z, y, x, c = place(n)
    rows = G.shape[5]

    order = []
    for a, lo, mid, hi in chunks:
        if jobs[a][0] is not None and (not order or order[-1] != jobs[a][0]):
            order.append(jobs[a][0])
    firsts, turn = {}, -1
    for i, (a, lo, mid, hi) in enumerate(chunks):
        left = jobs[a][0]
        if left is not None and (turn < 0 or order[turn] != left):
            turn += 1
            firsts[i] = turn
    turn_of, now = {}, -1
    for i in range(len(chunks)):
        now = firsts.get(i, now)
        turn_of[i] = now

    def left_copy(t):
        return pltpu.make_async_copy(left_refs[order[t]], LB.at[t % 2], lsem.at[t % 2])

    def load(i):
        a, lo, mid, hi = chunks[i]
        if jobs[a][0] is None:
            src, dst = ins[a].at[:, :, :, :, :, lo:hi], G.at[i % K, :, :, :, :, :, 0 : hi - lo]
        else:
            src, dst = ins[a].at[:, lo:hi], RB.at[i % 2, :, 0 : hi - lo]
        return pltpu.make_async_copy(src, dst, ls.at[i % 2])

    left_copy(0).start()
    if len(order) > 1:
        left_copy(1).start()
    load(0).start()
    greet(n, z, y, x, c)

    def from_partner(i):
        a, lo, mid, hi = chunks[i]
        k, w = i % K, hi - lo
        load(i).wait()
        if i + 1 < len(chunks):
            load(i + 1).start()
        t = turn_of[i]
        if jobs[a][0] is not None:
            if i in firsts:
                left_copy(t).wait()
            depth = LB.shape[2] // Z

            def block(zz, carry):
                at = pl.ds(pl.multiple_of(zz * depth, depth), depth)
                part = lax.dot_general(
                    LB[t % 2, :, at],
                    RB[i % 2, :, 0:w],
                    (((0,), (0,)), ((), ())),
                    preferred_element_type=f32,
                )
                G[k, zz, :, :, :, :, 0:w] = part.astype(bf16).reshape(Y, X, 2, rows, w)
                return carry

            lax.fori_loop(0, Z, block, 0)
        if i + 1 in firsts and 0 <= t < len(order) - 2:
            left_copy(t + 2).start()
        return [
            remote(
                G.at[k, :, :, :, 1 - c, :, 0:w],
                R0.at[k, :, :, :, :, 0:w],
                s0.at[k],
                r0.at[k],
                index(n, z, y, x, 1 - c),
            )
        ]

    def first_side(i):
        a, lo, mid, hi = chunks[i]
        k, w, h = i % K, hi - lo, mid - lo

        def add(j, carry):
            zz, yy, xx = j // (Y * X), lax.rem(j // X, Y), lax.rem(j, X)
            total = G[k, zz, yy, xx, c, :, 0:w].astype(f32) + R0[k, zz, yy, xx, :, 0:w].astype(f32)
            G[k, zz, yy, xx, c, :, 0:w] = total.astype(bf16)
            return carry

        lax.fori_loop(0, Z * Y * X, add, 0)
        copies = []
        for o in range(1, Y if h > 0 else 1):
            d = lax.rem(y + o, Y)
            src, dst = G.at[k, :, d, :, c, :, 0:h], R1.at[k, o - 1, :, 0:X, :, 0:h]
            copies.append(remote(src, dst, s1.at[k, 0, o - 1], r1.at[k, 0, o - 1], index(n, z, d, x, c)))
        for o in range(1, X):
            d = lax.rem(x + o, X)
            src, dst = G.at[k, :, :, d, c, :, h:w], R1.at[k, o - 1, :, 0:Y, :, h:w]
            copies.append(remote(src, dst, s1.at[k, 1, o - 1], r1.at[k, 1, o - 1], index(n, z, y, d, c)))
        return copies

    def second_side(i):
        a, lo, mid, hi = chunks[i]
        k, w, h = i % K, hi - lo, mid - lo
        for half, start, end, size, terms in ((0, 0, h, X, Y), (1, h, w, Y, X)):
            if start == end:
                continue

            def add(j, carry):
                zz, ss = j // size, lax.rem(j, size)
                if half == 0:
                    total = G[k, zz, y, ss, c, :, start:end].astype(f32)
                else:
                    total = G[k, zz, ss, x, c, :, start:end].astype(f32)
                for o in range(1, terms):
                    total = total + R1[k, o - 1, zz, ss, :, start:end].astype(f32)
                P1[k, zz, ss, :, start:end] = total.astype(bf16)
                return carry

            lax.fori_loop(0, Z * size, add, 0)
        copies = []
        for o in range(1, X if h > 0 else 1):
            d = lax.rem(x + o, X)
            src, dst = P1.at[k, :, d, :, 0:h], R2.at[k, o - 1, :, :, 0:h]
            copies.append(remote(src, dst, s2.at[k, 0, o - 1], r2.at[k, 0, o - 1], index(n, z, y, d, c)))
        for o in range(1, Y):
            d = lax.rem(y + o, Y)
            src, dst = P1.at[k, :, d, :, h:w], R2.at[k, o - 1, :, :, h:w]
            copies.append(remote(src, dst, s2.at[k, 1, o - 1], r2.at[k, 1, o - 1], index(n, z, d, x, c)))
        return copies

    def along_z(i):
        a, lo, mid, hi = chunks[i]
        k, w, h = i % K, hi - lo, mid - lo
        for start, end, terms, mine in ((0, h, X, x), (h, w, Y, y)):
            if start == end:
                continue

            def add(zz, carry):
                total = P1[k, zz, mine, :, start:end].astype(f32)
                for o in range(1, terms):
                    total = total + R2[k, o - 1, zz, :, start:end].astype(f32)
                P2[k, zz, :, start:end] = total.astype(bf16)
                return carry

            lax.fori_loop(0, Z, add, 0)
        copies = []
        for o in range(1, Z):
            d = lax.rem(z + o, Z)
            src, dst = P2.at[k, d, :, 0:w], R3.at[k, o - 1, :, 0:w]
            copies.append(remote(src, dst, s3.at[k, o - 1], r3.at[k, o - 1], index(n, d, y, x, c)))
        return copies

    def finish(i):
        a, lo, mid, hi = chunks[i]
        k, w = i % K, hi - lo
        total = P2[k, z, :, 0:w].astype(f32)
        for o in range(1, Z):
            total = total + R3[k, o - 1, :, 0:w].astype(f32)
        outs[a][:, lo:hi] = total
        return []

    run_stages(len(chunks), LAG, [from_partner, first_side, second_side, along_z, finish])


def scatter(n, lefts, jobs, target, cid):
    Z, Y, X = dims_of(n)
    parts = [part for left, part in jobs]
    chunks = cut([p.shape[1] for p in parts], target)
    K = 2 * LAG + 1
    tokens, width = lefts[0].shape
    rows = width // n
    most = max(X, Y)
    sides, ends = max(most, 2) - 1, max(Z - 1, 1)
    wide = max(hi - lo for a, lo, mid, hi in chunks)
    vmem = lambda *shape: pltpu.VMEM((K,) + shape + (rows, wide), bf16)
    jobs = [left for left, part in jobs]
    operands = [
        p if left is not None else p.reshape((Z, Y, X, 2, rows, p.shape[1])) for left, p in zip(jobs, parts)
    ]
    return pl.pallas_call(
        functools.partial(scatter_kernel, n, [(left, None) for left in jobs], len(lefts), chunks, K),
        out_shape=[jax.ShapeDtypeStruct((rows, p.shape[1]), f32) for p in parts],
        in_specs=[ANY] * (len(lefts) + len(parts)),
        out_specs=[pl.BlockSpec(memory_space=pltpu.VMEM)] * len(parts),
        scratch_shapes=[
            pltpu.VMEM((2, tokens, width), bf16),
            pltpu.VMEM((2, tokens, wide), bf16),
            vmem(Z, Y, X, 2),
            vmem(Z, Y, X),
            vmem(Z, most),
            vmem(sides, Z, most),
            vmem(Z),
            vmem(sides, Z),
            vmem(ends),
            DMA((2,)),
            DMA((2,)),
            DMA((K,)),
            DMA((K,)),
        ]
        + [DMA((K, 2, sides))] * 4
        + [DMA((K, ends))] * 2,
        compiler_params=pltpu.CompilerParams(
            collective_id=cid, has_side_effects=True, vmem_limit_bytes=60 << 20
        ),
    )(*lefts, *operands)


NT = (((1,), (1,)), ((), ()))
TN = (((0,), (0,)), ((), ()))


def dot(a, b):
    return jnp.dot(a, b, preferred_element_type=f32)


def dot_nt(a, b):
    return lax.dot_general(a, b, NT, preferred_element_type=f32)


def dot_tn(a, b):
    return lax.dot_general(a, b, TN, preferred_element_type=f32)


def tiles(size, tile):
    def run(body):
        def step(j, carry):
            body(pl.ds(pl.multiple_of(j * tile, tile), tile))
            return carry

        lax.fori_loop(0, size // tile, step, 0)

    return run


def build_bias(parents, lengths, bias):
    trees, tree = bias.shape[0], bias.shape[1]
    count = parents.shape[1]
    key = lax.broadcasted_iota(jnp.int32, (1, tree), 1)
    row = lax.broadcasted_iota(jnp.int32, (tree, 1), 0)
    for t in range(trees):
        start = jnp.int32(0)
        reach, total = [], jnp.zeros((tree, tree), f32)
        for s in range(count):
            end = start + lengths[t, s]
            line = jnp.where((key >= start) & (key < end), 1.0, 0.0)
            for u in range(s):
                line = line + jnp.where(parents[t, s] == u, reach[u], 0.0)
            reach.append(line)
            total = total + jnp.where((row >= start) & (row < end), 1.0, 0.0) * line
            start = end
        seen = (total > 0.5) & (key <= row)
        bias[t] = jnp.where(seen, 0.0, -1e30)


def norm_to(dst, src, gain, rows=64):
    @tiles(src.shape[0], rows)
    def _(at):
        h = src[at, :]
        r = lax.rsqrt(jnp.mean(h * h, axis=-1, keepdims=True) + epsilon)
        dst[at, :] = (h * r * gain).astype(bf16)


def attention_forward(q, k, v, bias, o, stats):
    trees, tree = bias.shape[0], bias.shape[1]
    pairs = q.shape[1] // 128
    scale = 1.0 / math.sqrt(HD)
    lane = lax.broadcasted_iota(jnp.int32, (tree, 128), 1)

    def step(j, carry):
        t, pair = j // pairs, lax.rem(j, pairs)
        rows = pl.ds(pl.multiple_of(t * tree, tree), tree)
        cols = pl.ds(pl.multiple_of(pair * 128, 128), 128)
        q2, k2, v2 = q[rows, cols], k[rows, cols], v[rows, cols]
        mixed, log_total = [], stats[rows, :]
        for half in range(2):
            mine = (lane >= HD) if half else (lane < HD)
            s = dot_nt(jnp.where(mine, q2, jnp.zeros_like(q2)), k2) * scale + bias[t]
            top = jnp.max(s, axis=-1, keepdims=True)
            e = jnp.exp(s - top)
            total = jnp.sum(e, axis=-1, keepdims=True)
            p = (e * (1.0 / total)).astype(bf16)
            mixed.append(dot(p, v2))
            log_total = jnp.where(lane == pair * 2 + half, top + jnp.log(total), log_total)
        stats[rows, :] = log_total
        o[rows, cols] = jnp.where(lane < HD, mixed[0], mixed[1]).astype(bf16)
        return carry

    lax.fori_loop(0, trees * pairs, step, 0)


def forward_kernel(h_ref, gains, bias_ref, wq_, wl_, wk_, wv_, wo_, wg_, wu_, wd_,
                   out, n1, q, c, k, v, o, stats, h1, n2, a_, b_, z_,
                   wq, wl, wk, wv, wo, wg, wu, wd, z, ab, wsem, osem):
    loads = []
    for i, (src, dst) in enumerate(
        ((wq_, wq), (wl_, wl), (wk_, wk), (wv_, wv), (wo_, wo), (wg_, wg), (wu_, wu), (wd_, wd))
    ):
        loads.append(pltpu.make_async_copy(src, dst, wsem.at[i]))
        loads[-1].start()
    norm_to(n1, h_ref, gains[0:1, :])
    half = wk.shape[2]
    loads[0].wait()

    @tiles(wq.shape[1], 512)
    def _(at):
        q[:, at] = dot(n1[...], wq[:, at]).astype(bf16)

    loads[1].wait()
    c[...] = dot(n1[...], wl[...]).astype(bf16)
    loads[2].wait()
    loads[3].wait()
    for g in range(GROUPS):
        cg = c[:, g * LAT : (g + 1) * LAT]
        k[:, g * half : (g + 1) * half] = dot(cg, wk[g]).astype(bf16)
        v[:, g * half : (g + 1) * half] = dot(cg, wv[g]).astype(bf16)
    stats[...] = jnp.zeros_like(stats)
    attention_forward(q, k, v, bias_ref, o, stats)
    loads[4].wait()

    @tiles(wo.shape[0], 512)
    def _(at):
        h1[:, at] = h_ref[:, at] + dot_nt(o[...], wo[at, :])

    norm_to(n2, h1, gains[1:2, :])
    loads[5].wait()
    loads[6].wait()
    count = wg.shape[1] // 256

    def put(j, which, dst):
        at = pl.ds(pl.multiple_of(j * 256, 256), 256)
        return pltpu.make_async_copy(ab.at[which, lax.rem(j, 2)], dst.at[:, at], osem.at[which, lax.rem(j, 2)])

    def step(j, carry):
        at = pl.ds(pl.multiple_of(j * 256, 256), 256)

        @pl.when(j >= 2)
        def _():
            put(j - 2, 0, a_).wait()
            put(j - 2, 1, b_).wait()

        a = dot(n2[...], wg[:, at])
        b = dot(n2[...], wu[:, at])
        ab[0, lax.rem(j, 2)] = a
        ab[1, lax.rem(j, 2)] = b
        put(j, 0, a_).start()
        put(j, 1, b_).start()
        z[:, at] = (a / (1.0 + jnp.exp(-a)) * b).astype(bf16)
        return carry

    lax.fori_loop(0, count, step, 0)
    zc = pltpu.make_async_copy(z, z_, osem.at[0, 2])
    zc.start()
    loads[7].wait()

    @tiles(wd.shape[0], 256)
    def _(at):
        out[:, at] = h1[:, at] + dot_nt(z[...], wd[at, :])

    zc.wait()
    for j in (count - 2, count - 1):
        put(j, 0, a_).wait()
        put(j, 1, b_).wait()


VM = pl.BlockSpec(memory_space=pltpu.VMEM)
SM = pl.BlockSpec(memory_space=pltpu.SMEM)


def layer_forward(h, weights, gains, bias):
    tokens, width = h.shape
    ff = weights[5].shape[1]
    like = lambda w, t: jax.ShapeDtypeStruct((tokens, w), t)
    wide = weights[0].shape[1]
    lat = weights[1].shape[1]
    shapes = [like(width, f32), like(width, bf16), like(wide, bf16), like(lat, bf16), like(wide, bf16),
              like(wide, bf16), like(wide, bf16), like(128, f32), like(width, f32), like(width, bf16),
              like(ff, f32), like(ff, f32), like(ff, bf16)]
    return pl.pallas_call(
        forward_kernel,
        out_shape=shapes,
        in_specs=[VM, VM, VM] + [ANY] * 8,
        out_specs=[VM] * 10 + [ANY] * 3,
        scratch_shapes=[pltpu.VMEM(w.shape, bf16) for w in weights]
        + [pltpu.VMEM((tokens, ff), bf16), pltpu.VMEM((2, 2, tokens, 256), f32), DMA((8,)), DMA((2, 3))],
        compiler_params=pltpu.CompilerParams(vmem_limit_bytes=62 << 20),
    )(h, gains, bias, *weights)


def bias_kernel(parents, lengths, bias):
    build_bias(parents, lengths, bias)


def tree_bias(parents, lengths, tree):
    return pl.pallas_call(
        bias_kernel,
        out_shape=jax.ShapeDtypeStruct((parents.shape[0], tree, tree), f32),
        in_specs=[SM, SM],
        out_specs=VM,
    )(parents, lengths)


def norm_back_to(dst, carry_in, dn, h_ref, gain, gain_grad, low=None, rows=64):
    gain_grad[...] = jnp.zeros_like(gain_grad)

    @tiles(h_ref.shape[0], rows)
    def _(at):
        h, d = h_ref[at, :], dn[at, :]
        r = lax.rsqrt(jnp.mean(h * h, axis=-1, keepdims=True) + epsilon)
        gain_grad[...] += jnp.sum(d * h * r, axis=0, keepdims=True)
        weighted = d * gain
        inner = jnp.mean(weighted * h, axis=-1, keepdims=True)
        total = carry_in[at, :] + (r * weighted - h * (r * r * r) * inner)
        dst[at, :] = total
        if low is not None:
            low[at, :] = total.astype(bf16)


def attention_backward(q, k, v, do, bias, stats, dq, dk, dv):
    trees, tree = bias.shape[0], bias.shape[1]
    pairs = q.shape[1] // 128
    scale = 1.0 / math.sqrt(HD)
    lane = lax.broadcasted_iota(jnp.int32, (tree, 128), 1)

    def step(j, carry):
        t, pair = j // pairs, lax.rem(j, pairs)
        rows = pl.ds(pl.multiple_of(t * tree, tree), tree)
        cols = pl.ds(pl.multiple_of(pair * 128, 128), 128)
        q2, k2, v2, do2 = q[rows, cols], k[rows, cols], v[rows, cols], do[rows, cols]
        logs = stats[rows, :]
        zero = jnp.zeros_like(q2)
        got = []
        for half in range(2):
            mine = (lane >= HD) if half else (lane < HD)
            log_total = jnp.sum(jnp.where(lane == pair * 2 + half, logs, 0.0), axis=-1, keepdims=True)
            s = dot_nt(jnp.where(mine, q2, zero), k2) * scale + bias[t]
            p = jnp.exp(s - log_total)
            dp = dot_nt(jnp.where(mine, do2, zero), v2)
            inner = jnp.sum(p * dp, axis=-1, keepdims=True)
            ds = (p * (dp - inner)).astype(bf16)
            got.append((dot(ds, k2), dot_tn(ds, q2), dot_tn(p.astype(bf16), do2)))
        low = lane < HD
        dq[rows, cols] = (jnp.where(low, got[0][0], got[1][0]) * scale).astype(bf16)
        dk[rows, cols] = (jnp.where(low, got[0][1], got[1][1]) * scale).astype(bf16)
        dv[rows, cols] = jnp.where(low, got[0][2], got[1][2]).astype(bf16)
        return carry

    lax.fori_loop(0, trees * pairs, step, 0)


def backward_kernel(g_ref, h_ref, h1_ref, gains, bias_ref, stats_ref, q, k, v, c, a_, b_, wq_, wl_, wk_, wv_, wo_, wg_, wu_, wd_,
                    out, gf, da_, db_, ga, dq, dk, dv, dc, dkey, dvalue, dg1, dg2,
                    wq, wl, wk, wv, wo, wg, wu, wd, da, db, ab, dm, do, wsem, asem, osem):
    loads = []
    for i, (src, dst) in enumerate(
        ((wd_, wd), (wg_, wg), (wu_, wu), (wo_, wo), (wk_, wk), (wv_, wv), (wq_, wq), (wl_, wl))
    ):
        loads.append(pltpu.make_async_copy(src, dst, wsem.at[i]))
    count = wg.shape[1] // 256

    def get(j, which, src):
        at = pl.ds(pl.multiple_of(j * 256, 256), 256)
        return pltpu.make_async_copy(src.at[:, at], ab.at[which, lax.rem(j, 2)], asem.at[which, lax.rem(j, 2)])

    loads[0].start()
    get(0, 0, a_).start()
    get(0, 1, b_).start()
    for load in loads[1:]:
        load.start()

    @tiles(g_ref.shape[0], 64)
    def _(at):
        gf[at, :] = g_ref[at, :].astype(bf16)

    loads[0].wait()

    def step(j, carry):
        at = pl.ds(pl.multiple_of(j * 256, 256), 256)
        get(j, 0, a_).wait()
        get(j, 1, b_).wait()

        @pl.when(j + 1 < count)
        def _():
            get(j + 1, 0, a_).start()
            get(j + 1, 1, b_).start()

        dz = dot(gf[...], wd[:, at])
        a, b = ab[0, lax.rem(j, 2)], ab[1, lax.rem(j, 2)]
        sig = 1.0 / (1.0 + jnp.exp(-a))
        da[:, at] = (dz * b * sig * (1.0 + a * (1.0 - sig))).astype(bf16)
        db[:, at] = (dz * a * sig).astype(bf16)
        return carry

    lax.fori_loop(0, count, step, 0)
    outs = [pltpu.make_async_copy(da, da_, osem.at[0]), pltpu.make_async_copy(db, db_, osem.at[1])]
    for copy in outs:
        copy.start()
    loads[1].wait()
    loads[2].wait()

    @tiles(wg.shape[0], 256)
    def _(at):
        dm[:, at] = dot_nt(da[...], wg[at, :]) + dot_nt(db[...], wu[at, :])

    norm_back_to(out, g_ref, dm, h1_ref, gains[1:2, :], dg2, low=ga)
    loads[3].wait()

    @tiles(wo.shape[1], 512)
    def _(at):
        do[:, at] = dot(ga[...], wo[:, at]).astype(bf16)

    attention_backward(q, k, v, do, bias_ref, stats_ref, dq, dk, dv)
    loads[4].wait()
    loads[5].wait()
    half = wk.shape[2]
    for g in range(GROUPS):
        at = slice(g * half, (g + 1) * half)
        lat = slice(g * LAT, (g + 1) * LAT)
        dkey[g] = dot_tn(c[:, lat], dk[:, at]).astype(bf16)
        dvalue[g] = dot_tn(c[:, lat], dv[:, at]).astype(bf16)
        dc[:, lat] = (dot_nt(dk[:, at], wk[g]) + dot_nt(dv[:, at], wv[g])).astype(bf16)
    loads[6].wait()
    loads[7].wait()

    @tiles(wq.shape[0], 512)
    def _(at):
        dm[:, at] = dot_nt(dq[...], wq[at, :]) + dot_nt(dc[...], wl[at, :])

    norm_back_to(out, out, dm, h_ref, gains[0:1, :], dg1)
    for copy in outs:
        copy.wait()


def layer_backward(grad, kept, weights, gains, bias):
    h, n1, q, c, k, v, o, stats, h1, n2, a, b, z = kept
    tokens, width = h.shape
    ff, wide, lat = a.shape[1], q.shape[1], c.shape[1]
    like = lambda w, t: jax.ShapeDtypeStruct((tokens, w), t)
    wk = weights[2]
    line = jax.ShapeDtypeStruct((1, width), f32)
    shapes = [like(width, f32), like(width, bf16), like(ff, bf16), like(ff, bf16), like(width, bf16),
              like(wide, bf16), like(wide, bf16), like(wide, bf16), like(lat, bf16),
              jax.ShapeDtypeStruct(wk.shape, bf16), jax.ShapeDtypeStruct(wk.shape, bf16), line, line]
    out, gf, da, db, ga, dq, dk, dv, dc, dkey, dvalue, dg1, dg2 = pl.pallas_call(
        backward_kernel,
        out_shape=shapes,
        in_specs=[VM] * 10 + [ANY] * 10,
        out_specs=[VM, VM, ANY, ANY] + [VM] * 9,
        scratch_shapes=[pltpu.VMEM(w.shape, bf16) for w in weights]
        + [pltpu.VMEM((tokens, ff), bf16)] * 2
        + [pltpu.VMEM((2, 2, tokens, 256), f32), pltpu.VMEM((tokens, width), f32), pltpu.VMEM((tokens, wide), bf16),
           DMA((8,)), DMA((2, 2)), DMA((2,))],
        compiler_params=pltpu.CompilerParams(vmem_limit_bytes=62 << 20),
    )(grad, h, h1, gains, bias, stats, q, k, v, c, a, b, *weights)
    lefts = [gf, n2, ga, n1]
    jobs = [(0, z), (1, da), (1, db), (2, o), (3, dq), (3, dc)]
    return out, lefts, jobs, (dkey, dvalue), (dg1[0], dg2[0])


def body(inputs, cotangent, parents, lengths, g1, wq, wl, wk, wv, wo, g2, wg, wu, wd, *, n):
    trees, tree, width = inputs.shape
    rows = wq.shape[1]
    latr = wk.shape[2]

    def packed(layer):
        cast = lambda w: w[layer].astype(bf16)
        kv = jnp.stack([wk[layer], wv[layer]]).astype(bf16).reshape(-1, wk.shape[3])
        return [cast(wq), cast(wl), kv, cast(wo).T, cast(wg), cast(wu), cast(wd).T]

    gain_rows = jnp.stack([g1[0], g2[0], g1[1], g2[1]], axis=1).astype(bf16)
    gain_rows = jnp.pad(gain_rows, ((0, 0), (0, 128 - 2 * LAYERS)))
    got = gather(n, [gain_rows] + packed(0) + packed(1), 704, 0)
    gains = got[0][:, : 2 * LAYERS].T.astype(f32).reshape(LAYERS, 2, width)

    def unpacked(part):
        q, l, kv, o, g, u, d = part
        kv = kv.reshape(n, 2, GROUPS, latr, -1).transpose(1, 2, 0, 3, 4).reshape(2, GROUPS, LAT, -1)
        return (q, l, kv[0], kv[1], o, g, u, d)

    weights = [unpacked(got[1:8]), unpacked(got[8:15])]
    bias = tree_bias(parents, lengths, tree)
    resid = inputs.reshape(trees * tree, width).astype(f32)
    kept = []
    for layer in range(LAYERS):
        got_layer = layer_forward(resid, weights[layer], gains[layer], bias)
        kept.append((resid,) + tuple(got_layer[1:]))
        resid = got_layer[0]
    outputs = resid.reshape(inputs.shape)
    grad = cotangent.reshape(trees * tree, width)
    lefts, jobs, gain_grads = [], [], [None] * LAYERS
    for layer in reversed(range(LAYERS)):
        grad, left, job, kv, gain_grads[layer] = layer_backward(
            grad, kept[layer], weights[layer], gains[layer], bias
        )
        kv = jnp.stack(kv).astype(bf16).reshape(2, GROUPS, n, latr, -1).transpose(2, 0, 1, 3, 4)
        jobs += [(len(lefts) + at, part) for at, part in job] + [(None, kv.reshape(n * rows, -1))]
        lefts += left
    gain_part = jnp.stack(gain_grads[0] + gain_grads[1], axis=1).astype(bf16)
    gain_part = jnp.pad(gain_part, ((0, 0), (0, 128 - 2 * LAYERS)))
    summed = scatter(n, lefts, jobs + [(None, gain_part)], 704, 1)
    out = []
    for layer in range(LAYERS):
        dd, dg, du, do, dq, dl, kv = summed[(1 - layer) * 7 : (1 - layer) * 7 + 7]
        kv = kv.reshape(2, GROUPS, latr, -1)
        gain = summed[14]
        out.append(
            (gain[:, 2 * layer], dq, dl, kv[0], kv[1], do.T, gain[:, 2 * layer + 1], dg, du, dd.T)
        )
    stacked = tuple(jnp.stack([out[layer][slot] for layer in range(LAYERS)]) for slot in range(10))
    return (outputs, grad.reshape(inputs.shape)) + stacked


def solution(mesh):
    n = mesh.shape["fsdp"]
    by_one, by_two = P(None, "fsdp"), P(None, "fsdp", None)
    by_lat, by_last = P(None, None, "fsdp", None), P(None, None, "fsdp")
    params = (by_one, by_two, by_two, by_lat, by_lat, by_last, by_one, by_two, by_two, by_last)
    trees = P("fsdp", None, None)
    return jax.shard_map(
        functools.partial(body, n=n),
        mesh=mesh,
        in_specs=(trees, trees, P("fsdp", None), P("fsdp", None)) + params,
        out_specs=(trees, trees) + params,
        check_vma=False,
    )
```

```python
import functools
import math

import jax
import jax.numpy as jnp
from jax import lax
from jax.experimental import pallas as pl
from jax.experimental.pallas import tpu as pltpu
from jax.sharding import PartitionSpec as P

HEADS = 16
HD = 64
GROUPS = 2
LAT = 256
LAYERS = 2
LAG = 2
epsilon = 1e-05

MESH = pl.DeviceIdType.MESH
ANY = pl.BlockSpec(memory_space=pltpu.HBM)
DMA = pltpu.SemaphoreType.DMA
bf16 = jnp.bfloat16
f32 = jnp.float32


def dims_of(n):
    chips = n // 2
    side = 1
    if chips & (chips - 1) == 0:
        side = 2 ** ((chips.bit_length() - 1) // 3)
    return chips // (side * side), side, side


def index(n, z, y, x, c):
    Z, Y, X = dims_of(n)
    return ((z * Y + y) * X + x) * 2 + c


def place(n):
    Z, Y, X = dims_of(n)
    me = lax.axis_index("fsdp")
    return me // (2 * X * Y), lax.rem(me // (2 * X), Y), lax.rem(me // 2, X), lax.rem(me, 2)


def greet(n, z, y, x, c):
    Z, Y, X = dims_of(n)
    peers = [index(n, lax.rem(z + o, Z), y, x, c) for o in range(1, Z)]
    peers += [index(n, z, lax.rem(y + o, Y), x, c) for o in range(1, Y)]
    peers += [index(n, z, y, lax.rem(x + o, X), c) for o in range(1, X)]
    peers += [index(n, z, y, x, 1 - c)]
    bar = pltpu.get_barrier_semaphore()
    for peer in peers:
        pl.semaphore_signal(bar, inc=1, device_id=(peer,), device_id_type=MESH)
    pl.semaphore_wait(bar, len(peers))


def remote(src, dst, send, recv, device):
    copy = pltpu.make_async_remote_copy(
        src_ref=src,
        dst_ref=dst,
        send_sem=send,
        recv_sem=recv,
        device_id=(device,),
        device_id_type=MESH,
    )
    copy.start()
    return copy


def cut(widths, target):
    out = []
    for a, w in enumerate(widths):
        k, u = max(1, round(w / target)), w // 128
        edges = [round(j * u / k) * 128 for j in range(k + 1)]
        for lo, hi in zip(edges, edges[1:]):
            half = (hi - lo) // 128
            half = half // 2 if len(out) % 2 == 0 else (half + 1) // 2
            out.append((a, lo, lo + half * 128, hi))
    return out


def run_stages(count, lag, stages):
    held = [None] * count
    last = len(stages) - 1
    for slot in range(count + lag * last):
        for s in range(last, -1, -1):
            i = slot - lag * s
            if 0 <= i < count:
                if s > 0:
                    for copy in held[i]:
                        copy.wait()
                held[i] = stages[s](i)


def gather_kernel(n, chunks, count, *refs):
    Z, Y, X = dims_of(n)
    ins, outs = refs[:count], refs[count : 2 * count]
    own_sem, zs, zr, as_, ar, bs, br, cs, cr = refs[2 * count :]
    z, y, x, c = place(n)
    greet(n, z, y, x, c)

    def along_z(i):
        a, lo, mid, hi = chunks[i]
        src, dst = ins[a].at[:, lo:hi], outs[a].at[z, y, x, c, :, lo:hi]
        own = pltpu.make_async_copy(src, dst, own_sem.at[i])
        own.start()
        return [own] + [
            remote(src, dst, zs.at[i, o - 1], zr.at[i, o - 1], index(n, lax.rem(z + o, Z), y, x, c))
            for o in range(1, Z)
        ]

    def to_x(o):
        return index(n, z, y, lax.rem(x + o, X), c)

    def to_y(o):
        return index(n, z, lax.rem(y + o, Y), x, c)

    def first_side(i):
        a, lo, mid, hi = chunks[i]
        copies = []
        for h, (start, end, size, to) in enumerate(((lo, mid, X, to_x), (mid, hi, Y, to_y))):
            part = outs[a].at[:, y, x, c, :, start:end]
            for o in range(1, size if end > start else 1):
                copies.append(remote(part, part, as_.at[i, h, o - 1], ar.at[i, h, o - 1], to(o)))
        return copies

    def second_side(i):
        a, lo, mid, hi = chunks[i]
        copies = []
        for o in range(1, Y if mid > lo else 1):
            part = outs[a].at[:, y, :, c, :, lo:mid]
            copies.append(remote(part, part, bs.at[i, 0, o - 1], br.at[i, 0, o - 1], to_y(o)))
        for o in range(1, X):
            part = outs[a].at[:, :, x, c, :, mid:hi]
            copies.append(remote(part, part, bs.at[i, 1, o - 1], br.at[i, 1, o - 1], to_x(o)))
        return copies

    def to_partner(i):
        a, lo, mid, hi = chunks[i]
        part = outs[a].at[:, :, :, c, :, lo:hi]
        return [remote(part, part, cs.at[i], cr.at[i], index(n, z, y, x, 1 - c))]

    run_stages(len(chunks), LAG, [along_z, first_side, second_side, to_partner, lambda i: []])


def gather(n, shards, target, cid):
    Z, Y, X = dims_of(n)
    chunks = cut([s.shape[1] for s in shards], target)
    N, ends, sides = len(chunks), max(Z - 1, 1), max(X, Y, 2) - 1
    got = pl.pallas_call(
        functools.partial(gather_kernel, n, chunks, len(shards)),
        out_shape=[jax.ShapeDtypeStruct((Z, Y, X, 2) + s.shape, s.dtype) for s in shards],
        in_specs=[ANY] * len(shards),
        out_specs=[ANY] * len(shards),
        scratch_shapes=[DMA((N,)), DMA((N, ends)), DMA((N, ends))]
        + [DMA((N, 2, sides))] * 4
        + [DMA((N,)), DMA((N,))],
        compiler_params=pltpu.CompilerParams(
            collective_id=cid, has_side_effects=True, vmem_limit_bytes=60 << 20
        ),
    )(*shards)
    return [g.reshape(n * s.shape[0], s.shape[1]) for g, s in zip(got, shards)]


NT = (((1,), (1,)), ((), ()))
TN = (((0,), (0,)), ((), ()))


def dot(a, b):
    return jnp.dot(a, b, preferred_element_type=f32)


def dot_nt(a, b):
    return lax.dot_general(a, b, NT, preferred_element_type=f32)


def dot_tn(a, b):
    return lax.dot_general(a, b, TN, preferred_element_type=f32)


def tiles(size, tile):
    def run(body):
        def step(j, carry):
            body(pl.ds(pl.multiple_of(j * tile, tile), tile))
            return carry

        lax.fori_loop(0, size // tile, step, 0)

    return run


def build_bias(parents, lengths, bias):
    trees, tree = bias.shape[0], bias.shape[1]
    count = parents.shape[1]
    key = lax.broadcasted_iota(jnp.int32, (1, tree), 1)
    row = lax.broadcasted_iota(jnp.int32, (tree, 1), 0)
    for t in range(trees):
        start = jnp.int32(0)
        reach, total = [], jnp.zeros((tree, tree), f32)
        for s in range(count):
            end = start + lengths[t, s]
            line = jnp.where((key >= start) & (key < end), 1.0, 0.0)
            for u in range(s):
                line = line + jnp.where(parents[t, s] == u, reach[u], 0.0)
            reach.append(line)
            total = total + jnp.where((row >= start) & (row < end), 1.0, 0.0) * line
            start = end
        seen = (total > 0.5) & (key <= row)
        bias[t] = jnp.where(seen, 0.0, -1e30)


def norm_to(dst, src, gain, rows=64):
    @tiles(src.shape[0], rows)
    def _(at):
        h = src[at, :]
        r = lax.rsqrt(jnp.mean(h * h, axis=-1, keepdims=True) + epsilon)
        dst[at, :] = (h * r * gain).astype(bf16)


def attention_forward(q, k, v, bias, o, stats):
    trees, tree = bias.shape[0], bias.shape[1]
    pairs = q.shape[1] // 128
    scale = 1.0 / math.sqrt(HD)
    lane = lax.broadcasted_iota(jnp.int32, (tree, 128), 1)

    def step(j, carry):
        t, pair = j // pairs, lax.rem(j, pairs)
        rows = pl.ds(pl.multiple_of(t * tree, tree), tree)
        cols = pl.ds(pl.multiple_of(pair * 128, 128), 128)
        q2, k2, v2 = q[rows, cols], k[rows, cols], v[rows, cols]
        mixed, log_total = [], stats[rows, :]
        for half in range(2):
            mine = (lane >= HD) if half else (lane < HD)
            s = dot_nt(jnp.where(mine, q2, jnp.zeros_like(q2)), k2) * scale + bias[t]
            top = jnp.max(s, axis=-1, keepdims=True)
            e = jnp.exp(s - top)
            total = jnp.sum(e, axis=-1, keepdims=True)
            p = (e * (1.0 / total)).astype(bf16)
            mixed.append(dot(p, v2))
            log_total = jnp.where(lane == pair * 2 + half, top + jnp.log(total), log_total)
        stats[rows, :] = log_total
        o[rows, cols] = jnp.where(lane < HD, mixed[0], mixed[1]).astype(bf16)
        return carry

    lax.fori_loop(0, trees * pairs, step, 0)


def spread_latents(cp, c):
    lat, width = c.shape[1], cp.shape[1]
    n = lax.axis_size("fsdp")
    quarter = width // n // 4
    bits = quarter.bit_length() - 1
    col = lax.broadcasted_iota(jnp.int32, (lat, width), 1)
    latent = ((col >> bits) & 1) * LAT + (col >> (bits + 2)) * quarter + (col & (quarter - 1))
    pick = jnp.where(latent == lax.broadcasted_iota(jnp.int32, (lat, width), 0), 1.0, 0.0).astype(bf16)
    cp[...] = dot(c[...], pick).astype(bf16)


def forward_kernel(h_ref, gains, bias_ref, wq_, wl_, wk_, wv_, wo_, wg_, wu_, wd_,
                   out, n1, q, c, k, v, o, stats, h1, n2, cp, a_, b_, z_,
                   wq, wl, wk, wv, wo, wg, wu, wd, z, ab, wsem, osem):
    loads = []
    for i, (src, dst) in enumerate(
        ((wq_, wq), (wl_, wl), (wk_, wk), (wv_, wv), (wo_, wo), (wg_, wg), (wu_, wu), (wd_, wd))
    ):
        loads.append(pltpu.make_async_copy(src, dst, wsem.at[i]))
        loads[-1].start()
    norm_to(n1, h_ref, gains[0:1, :])
    half = wk.shape[2]
    loads[0].wait()

    @tiles(wq.shape[1], 512)
    def _(at):
        q[:, at] = dot(n1[...], wq[:, at]).astype(bf16)

    loads[1].wait()
    c[...] = dot(n1[...], wl[...]).astype(bf16)
    spread_latents(cp, c)
    loads[2].wait()
    loads[3].wait()
    for g in range(GROUPS):
        cg = c[:, g * LAT : (g + 1) * LAT]
        k[:, g * half : (g + 1) * half] = dot(cg, wk[g]).astype(bf16)
        v[:, g * half : (g + 1) * half] = dot(cg, wv[g]).astype(bf16)
    stats[...] = jnp.zeros_like(stats)
    attention_forward(q, k, v, bias_ref, o, stats)
    loads[4].wait()

    @tiles(wo.shape[0], 512)
    def _(at):
        h1[:, at] = h_ref[:, at] + dot_nt(o[...], wo[at, :])

    norm_to(n2, h1, gains[1:2, :])
    loads[5].wait()
    loads[6].wait()
    count = wg.shape[1] // 256

    def put(j, which, dst):
        at = pl.ds(pl.multiple_of(j * 256, 256), 256)
        return pltpu.make_async_copy(ab.at[which, lax.rem(j, 2)], dst.at[:, at], osem.at[which, lax.rem(j, 2)])

    def step(j, carry):
        at = pl.ds(pl.multiple_of(j * 256, 256), 256)

        @pl.when(j >= 2)
        def _():
            put(j - 2, 0, a_).wait()
            put(j - 2, 1, b_).wait()

        a = dot(n2[...], wg[:, at])
        b = dot(n2[...], wu[:, at])
        ab[0, lax.rem(j, 2)] = a
        ab[1, lax.rem(j, 2)] = b
        put(j, 0, a_).start()
        put(j, 1, b_).start()
        z[:, at] = (a / (1.0 + jnp.exp(-a)) * b).astype(bf16)
        return carry

    lax.fori_loop(0, count, step, 0)
    zc = pltpu.make_async_copy(z, z_, osem.at[0, 2])
    zc.start()
    loads[7].wait()

    @tiles(wd.shape[0], 256)
    def _(at):
        out[:, at] = h1[:, at] + dot_nt(z[...], wd[at, :])

    zc.wait()
    for j in (count - 2, count - 1):
        put(j, 0, a_).wait()
        put(j, 1, b_).wait()


VM = pl.BlockSpec(memory_space=pltpu.VMEM)
SM = pl.BlockSpec(memory_space=pltpu.SMEM)


def layer_forward(h, weights, gains, bias):
    tokens, width = h.shape
    ff = weights[5].shape[1]
    like = lambda w, t: jax.ShapeDtypeStruct((tokens, w), t)
    wide = weights[0].shape[1]
    lat = weights[1].shape[1]
    shapes = [like(width, f32), like(width, bf16), like(wide, bf16), like(lat, bf16), like(wide, bf16),
              like(wide, bf16), like(wide, bf16), like(128, f32), like(width, f32), like(width, bf16), like(width, bf16),
              like(ff, f32), like(ff, f32), like(ff, bf16)]
    return pl.pallas_call(
        forward_kernel,
        out_shape=shapes,
        in_specs=[VM, VM, VM] + [ANY] * 8,
        out_specs=[VM] * 11 + [ANY] * 3,
        scratch_shapes=[pltpu.VMEM(w.shape, bf16) for w in weights]
        + [pltpu.VMEM((tokens, ff), bf16), pltpu.VMEM((2, 2, tokens, 256), f32), DMA((8,)), DMA((2, 3))],
        compiler_params=pltpu.CompilerParams(vmem_limit_bytes=62 << 20),
    )(h, gains, bias, *weights)


def bias_kernel(parents, lengths, bias):
    build_bias(parents, lengths, bias)


def tree_bias(parents, lengths, tree):
    return pl.pallas_call(
        bias_kernel,
        out_shape=jax.ShapeDtypeStruct((parents.shape[0], tree, tree), f32),
        in_specs=[SM, SM],
        out_specs=VM,
    )(parents, lengths)


def norm_back_to(dst, carry_in, dn, h_ref, gain, gain_grad, low=None, rows=64):
    gain_grad[...] = jnp.zeros_like(gain_grad)

    @tiles(h_ref.shape[0], rows)
    def _(at):
        h, d = h_ref[at, :], dn[at, :]
        r = lax.rsqrt(jnp.mean(h * h, axis=-1, keepdims=True) + epsilon)
        gain_grad[...] += jnp.sum(d * h * r, axis=0, keepdims=True)
        weighted = d * gain
        inner = jnp.mean(weighted * h, axis=-1, keepdims=True)
        total = carry_in[at, :] + (r * weighted - h * (r * r * r) * inner)
        dst[at, :] = total
        if low is not None:
            low[at, :] = total.astype(bf16)


def attention_backward_step(q, k, v, do, bias, stats, dq, dk, dv):
    trees, tree = bias.shape[0], bias.shape[1]
    pairs = q.shape[1] // 128
    scale = 1.0 / math.sqrt(HD)
    lane = lax.broadcasted_iota(jnp.int32, (tree, 128), 1)

    def step(j):
        t, pair = j // pairs, lax.rem(j, pairs)
        rows = pl.ds(pl.multiple_of(t * tree, tree), tree)
        cols = pl.ds(pl.multiple_of(pair * 128, 128), 128)
        q2, k2, v2, do2 = q[rows, cols], k[rows, cols], v[rows, cols], do[rows, cols]
        logs = stats[rows, :]
        zero = jnp.zeros_like(q2)
        got = []
        for half in range(2):
            mine = (lane >= HD) if half else (lane < HD)
            log_total = jnp.sum(jnp.where(lane == pair * 2 + half, logs, 0.0), axis=-1, keepdims=True)
            s = dot_nt(jnp.where(mine, q2, zero), k2) * scale + bias[t]
            p = jnp.exp(s - log_total)
            dp = dot_nt(jnp.where(mine, do2, zero), v2)
            inner = jnp.sum(p * dp, axis=-1, keepdims=True)
            ds = (p * (dp - inner)).astype(bf16)
            got.append((dot(ds, k2), dot_tn(ds, q2), dot_tn(p.astype(bf16), do2)))
        low = lane < HD
        dq[rows, cols] = (jnp.where(low, got[0][0], got[1][0]) * scale).astype(bf16)
        dk[rows, cols] = (jnp.where(low, got[0][1], got[1][1]) * scale).astype(bf16)
        dv[rows, cols] = jnp.where(low, got[0][2], got[1][2]).astype(bf16)

    return step


class Scatter:
    def __init__(self, n, chunks, jobs, K, outs, bufs, sems, gain_rows):
        self.n, self.chunks, self.jobs, self.K, self.outs = n, chunks, jobs, K, outs
        self.LB, self.RB, self.G, self.R0, self.P1, self.R1, self.P2, self.R2, self.R3 = bufs
        self.lsem, self.ls, self.s0, self.r0, self.s1, self.r1, self.s2, self.r2, self.s3, self.r3 = sems
        self.gain_rows = gain_rows
        self.ready = set()
        self.stages = [self.from_partner, self.first_side, self.second_side, self.along_z, self.finish]
        self.held = [None] * len(chunks)
        self.at = 0
        self.started = False
        turns, last = [], None
        for a, lo, mid, hi in chunks:
            left = jobs[a]["left"]
            if left is not last and left is not None:
                turns.append(a)
                last = left
            turns_now = len(turns) - 1
            self.turn = getattr(self, "turn", []) + [turns_now]
        self.turns = turns

    def left_copy(self, t):
        return pltpu.make_async_copy(self.jobs[self.turns[t]]["left"], self.LB.at[t % 2], self.lsem.at[t % 2])

    def first_of(self, i):
        return self.jobs[self.chunks[i][0]]["left"] is not None and (i == 0 or self.turn[i] != self.turn[i - 1])

    def right_copy(self, i, which=0):
        a, lo, mid, hi = self.chunks[i]
        return pltpu.make_async_copy(
            self.jobs[a]["right"][which].at[:, lo:hi], self.RB.at[i % 2, :, 0 : hi - lo], self.ls.at[i % 2]
        )

    def fetch(self, i):
        if self.first_of(i):
            self.left_copy(self.turn[i]).start()
        if self.jobs[self.chunks[i][0]]["left"] is not None:
            self.right_copy(i).start()

    def has(self, i):
        return i >= len(self.chunks) or all(w in self.ready for w in self.jobs[self.chunks[i][0]]["needs"])

    def slot(self, times=1):
        for _ in range(times):
            i = self.at
            if i < len(self.chunks) and not (self.has(i) and self.has(i + 1)):
                return
            if not self.started:
                self.fetch(0)
                self.started = True
            last = len(self.stages) - 1
            if i >= len(self.chunks) + LAG * last:
                return
            for s in range(last, -1, -1):
                j = i - LAG * s
                if 0 <= j < len(self.chunks):
                    if s > 0:
                        for copy in self.held[j]:
                            copy.wait()
                    self.held[j] = self.stages[s](j)
            self.at += 1

    def drain(self):
        while self.at < len(self.chunks) + LAG * (len(self.stages) - 1):
            before = self.at
            self.slot()
            assert self.at > before

    def from_partner(self, i):
        Z, Y, X = dims_of(self.n)
        z, y, x, c = place(self.n)
        a, lo, mid, hi = self.chunks[i]
        k, w = i % self.K, hi - lo
        G, LB, RB = self.G, self.LB, self.RB
        rows = G.shape[6 - 1]
        job = self.jobs[a]
        t = self.turn[i]
        depth = LB.shape[2] // Z
        if job["left"] is not None:
            if self.first_of(i):
                self.left_copy(t).wait()
            self.right_copy(i).wait()
        if i + 1 < len(self.chunks):
            self.fetch(i + 1)
        if job["left"] is None:
            lines = self.gain_rows[...].astype(bf16)
            pick = lax.broadcasted_iota(jnp.int32, (lines.shape[0], w), 0)
            pick = (pick == lax.broadcasted_iota(jnp.int32, (lines.shape[0], w), 1)).astype(bf16)
            for zz in range(Z):
                part = dot_tn(lines[:, zz * depth : (zz + 1) * depth], pick)
                G[k, zz, :, :, :, :, 0:w] = part.astype(bf16).reshape(Y, X, 2, rows, w)
        elif len(job["right"]) == 1:

            def block(zz, carry):
                at = pl.ds(pl.multiple_of(zz * depth, depth), depth)
                part = dot_tn(LB[t % 2, :, at], RB[i % 2, :, 0:w])
                G[k, zz, :, :, :, :, 0:w] = part.astype(bf16).reshape(Y, X, 2, rows, w)
                return carry

            lax.fori_loop(0, Z, block, 0)
        else:
            quarter = rows // 4
            group = lax.broadcasted_iota(jnp.int32, (rows, w), 0) >> (quarter.bit_length() - 1)
            for which in range(4):
                if which:
                    copy = self.right_copy(i, which)
                    copy.start()
                    copy.wait()

                def block(zz, carry):
                    at = pl.ds(pl.multiple_of(zz * depth, depth), depth)
                    part = dot_tn(LB[t % 2, :, at], RB[i % 2, :, 0:w]).reshape(Y, X, 2, rows, w)
                    if which:
                        part = jnp.where(group == which, part, G[k, zz, :, :, :, :, 0:w].astype(f32))
                    G[k, zz, :, :, :, :, 0:w] = part.astype(bf16)
                    return carry

                lax.fori_loop(0, Z, block, 0)
        return [
            remote(
                G.at[k, :, :, :, 1 - c, :, 0:w],
                self.R0.at[k, :, :, :, :, 0:w],
                self.s0.at[k],
                self.r0.at[k],
                index(self.n, z, y, x, 1 - c),
            )
        ]

    def first_side(self, i):
        n, G, R0, R1 = self.n, self.G, self.R0, self.R1
        Z, Y, X = dims_of(n)
        z, y, x, c = place(n)
        a, lo, mid, hi = self.chunks[i]
        k, w, h = i % self.K, hi - lo, mid - lo

        def add(j, carry):
            zz, yy, xx = j // (Y * X), lax.rem(j // X, Y), lax.rem(j, X)
            total = G[k, zz, yy, xx, c, :, 0:w].astype(f32) + R0[k, zz, yy, xx, :, 0:w].astype(f32)
            G[k, zz, yy, xx, c, :, 0:w] = total.astype(bf16)
            return carry

        lax.fori_loop(0, Z * Y * X, add, 0)
        copies = []
        for o in range(1, Y if h > 0 else 1):
            d = lax.rem(y + o, Y)
            src, dst = G.at[k, :, d, :, c, :, 0:h], R1.at[k, o - 1, :, 0:X, :, 0:h]
            copies.append(remote(src, dst, self.s1.at[k, 0, o - 1], self.r1.at[k, 0, o - 1], index(n, z, d, x, c)))
        for o in range(1, X):
            d = lax.rem(x + o, X)
            src, dst = G.at[k, :, :, d, c, :, h:w], R1.at[k, o - 1, :, 0:Y, :, h:w]
            copies.append(remote(src, dst, self.s1.at[k, 1, o - 1], self.r1.at[k, 1, o - 1], index(n, z, y, d, c)))
        return copies

    def second_side(self, i):
        n, G, P1, R1, R2 = self.n, self.G, self.P1, self.R1, self.R2
        Z, Y, X = dims_of(n)
        z, y, x, c = place(n)
        a, lo, mid, hi = self.chunks[i]
        k, w, h = i % self.K, hi - lo, mid - lo
        for half, start, end, size, terms in ((0, 0, h, X, Y), (1, h, w, Y, X)):
            if start == end:
                continue

            def add(j, carry):
                zz, ss = j // size, lax.rem(j, size)
                if half == 0:
                    total = G[k, zz, y, ss, c, :, start:end].astype(f32)
                else:
                    total = G[k, zz, ss, x, c, :, start:end].astype(f32)
                for o in range(1, terms):
                    total = total + R1[k, o - 1, zz, ss, :, start:end].astype(f32)
                P1[k, zz, ss, :, start:end] = total.astype(bf16)
                return carry

            lax.fori_loop(0, Z * size, add, 0)
        copies = []
        for o in range(1, X if h > 0 else 1):
            d = lax.rem(x + o, X)
            src, dst = P1.at[k, :, d, :, 0:h], R2.at[k, o - 1, :, :, 0:h]
            copies.append(remote(src, dst, self.s2.at[k, 0, o - 1], self.r2.at[k, 0, o - 1], index(n, z, y, d, c)))
        for o in range(1, Y):
            d = lax.rem(y + o, Y)
            src, dst = P1.at[k, :, d, :, h:w], R2.at[k, o - 1, :, :, h:w]
            copies.append(remote(src, dst, self.s2.at[k, 1, o - 1], self.r2.at[k, 1, o - 1], index(n, z, d, x, c)))
        return copies

    def along_z(self, i):
        n, P1, P2, R2, R3 = self.n, self.P1, self.P2, self.R2, self.R3
        Z, Y, X = dims_of(n)
        z, y, x, c = place(n)
        a, lo, mid, hi = self.chunks[i]
        k, w, h = i % self.K, hi - lo, mid - lo
        for start, end, terms, mine in ((0, h, X, x), (h, w, Y, y)):
            if start == end:
                continue

            def add(zz, carry):
                total = P1[k, zz, mine, :, start:end].astype(f32)
                for o in range(1, terms):
                    total = total + R2[k, o - 1, zz, :, start:end].astype(f32)
                P2[k, zz, :, start:end] = total.astype(bf16)
                return carry

            lax.fori_loop(0, Z, add, 0)
        copies = []
        for o in range(1, Z):
            d = lax.rem(z + o, Z)
            src, dst = P2.at[k, d, :, 0:w], R3.at[k, o - 1, :, 0:w]
            copies.append(remote(src, dst, self.s3.at[k, o - 1], self.r3.at[k, o - 1], index(n, d, y, x, c)))
        return copies

    def finish(self, i):
        Z, Y, X = dims_of(self.n)
        z, y, x, c = place(self.n)
        a, lo, mid, hi = self.chunks[i]
        k, w = i % self.K, hi - lo
        total = self.P2[k, z, :, 0:w].astype(f32)
        for o in range(1, Z):
            total = total + self.R3[k, o - 1, :, 0:w].astype(f32)
        self.outs[a][:, lo:hi] = total
        return []


def loop(lo, hi, body):
    def step(j, carry):
        body(j)
        return carry

    lax.fori_loop(lo, hi, step, 0)


def span(j, size):
    return pl.ds(pl.multiple_of(j * size, size), size)


KEPT = ("h", "n1", "q", "k", "v", "o", "stats", "h1", "n2", "a", "b", "z", "cp")
NAMES = ("wq", "wl", "wk", "wv", "wo", "wg", "wu", "wd")
MADE = ("gf", "da", "db", "ga", "dq", "dk", "dv", "dc")


def backward_kernel(n, chunks, K, counts, *refs):
    it = iter(refs)
    take = lambda names: {name: next(it) for name in names}
    cot, gains, bias = next(it), next(it), next(it)
    kept = {layer: take(KEPT) for layer in reversed(range(LAYERS))}
    weights = {layer: take(NAMES) for layer in reversed(range(LAYERS))}
    grad_out = next(it)
    outs = [next(it) for _ in range(counts)]
    made = {layer: take(MADE) for layer in reversed(range(LAYERS))}
    bufs = [next(it) for _ in range(9)]
    gain_rows = next(it)
    v = take(("gf", "da", "db", "ga", "do", "q", "k", "v", "dq", "dk", "dv", "dc", "stats",
              "g", "h", "dm", "ab", "wd", "wgu", "wo", "wk", "wv", "wq", "wl"))
    sems = [next(it) for _ in range(10)]
    insem, outsem, asem, wsem = [next(it) for _ in range(4)]

    jobs = []
    for layer in reversed(range(LAYERS)):
        s, m = kept[layer], made[layer]
        need = lambda *names: [(layer, name) for name in names]
        jobs += [
            {"left": m["gf"], "right": [s["z"]], "needs": need("gf")},
            {"left": s["n2"], "right": [m["da"]], "needs": need("da")},
            {"left": s["n2"], "right": [m["db"]], "needs": need("db")},
            {"left": m["ga"], "right": [s["o"]], "needs": need("ga")},
            {"left": s["n1"], "right": [m["dq"]], "needs": need("dq")},
            {"left": s["n1"], "right": [m["dc"]], "needs": need("dc")},
        ]
        half = m["dk"].shape[1] // GROUPS
        rights = [m[name].at[:, g * half : (g + 1) * half] for name in ("dk", "dv") for g in range(GROUPS)]
        jobs += [{"left": s["cp"], "right": rights, "needs": need("dk", "dv")}]
    jobs += [{"left": None, "right": None, "needs": [(0, "end")]}]
    scatter = Scatter(n, chunks, jobs, K, outs, bufs, sems, gain_rows)
    slot = scatter.slot

    ff, width = v["da"].shape[1], v["g"].shape[1]
    count = ff // 256
    tokens = v["g"].shape[0]
    gain_rows[...] = jnp.zeros_like(gain_rows)
    greeted = []

    for layer in reversed(range(LAYERS)):
        s, w, m = kept[layer], weights[layer], made[layer]
        first = layer == LAYERS - 1
        copies = {}

        def load(name, src, at):
            copies[name] = pltpu.make_async_copy(src, v[name], insem.at[at])
            copies[name].start()

        def tile_ab(j, which):
            src = s["ab"[which]]
            return pltpu.make_async_copy(src.at[:, span(j, 256)], v["ab"].at[which, lax.rem(j, 2)], asem.at[which, lax.rem(j, 2)])

        def tile_wd(j):
            return pltpu.make_async_copy(w["wd"].at[:, span(j, 256)], v["wd"].at[lax.rem(j, 2)], wsem.at[0, lax.rem(j, 2)])

        def tile_gu(j, which):
            src = w["wg"] if which == 0 else w["wu"]
            return pltpu.make_async_copy(src.at[span(j, 256), :], v["wgu"].at[which, j % 2], wsem.at[1 + which, j % 2])

        def publish(name):
            copy = pltpu.make_async_copy(v[name], m[name], outsem.at[MADE.index(name)])
            copy.start()
            return copy

        if first:
            load("g", cot, 0)
        tile_wd(0).start()
        tile_ab(0, 0).start()
        tile_ab(0, 1).start()
        load("h", s["h1"], 1)
        for at, name in enumerate(("q", "k", "v", "stats")):
            load(name, s[name], 2 + at)
        for at, name in enumerate(("wo", "wk", "wv", "wq", "wl")):
            load(name, w[name], 6 + at)
        for j in range(2):
            tile_gu(j, 0).start()
            tile_gu(j, 1).start()
        if first:
            z, y, x, c = place(n)
            greet(n, z, y, x, c)
            copies["g"].wait()

        @tiles(tokens, 64)
        def _(at):
            v["gf"][at, :] = v["g"][at, :].astype(bf16)

        publish("gf").wait()
        scatter.ready.add((layer, "gf"))
        slot()

        def dz_step(j):
            at = span(j, 256)
            tile_wd(j).wait()
            tile_ab(j, 0).wait()
            tile_ab(j, 1).wait()

            @pl.when(j + 1 < count)
            def _():
                tile_wd(j + 1).start()
                tile_ab(j + 1, 0).start()
                tile_ab(j + 1, 1).start()

            dz = dot(v["gf"][...], v["wd"][lax.rem(j, 2)])
            a, b = v["ab"][0, lax.rem(j, 2)], v["ab"][1, lax.rem(j, 2)]
            sig = 1.0 / (1.0 + jnp.exp(-a))
            v["da"][:, at] = (dz * b * sig * (1.0 + a * (1.0 - sig))).astype(bf16)
            v["db"][:, at] = (dz * a * sig).astype(bf16)

        cuts = [0, count // 3, 2 * count // 3, count]
        for lo, hi in zip(cuts, cuts[1:]):
            loop(lo, hi, dz_step)
            slot()
        out_da, out_db = publish("da"), publish("db")
        for j in range(width // 256):
            tile_gu(j, 0).wait()
            tile_gu(j, 1).wait()
            at = slice(j * 256, (j + 1) * 256)
            v["dm"][:, at] = dot_nt(v["da"][...], v["wgu"][0, j % 2]) + dot_nt(v["db"][...], v["wgu"][1, j % 2])
            if j + 2 < width // 256:
                tile_gu(j + 2, 0).start()
                tile_gu(j + 2, 1).start()
            if j == 0:
                out_da.wait()
                out_db.wait()
                scatter.ready |= {(layer, "da"), (layer, "db")}
            if j % 2:
                slot()
        copies["h"].wait()
        norm_back_to(v["g"], v["g"], v["dm"], v["h"], gains[2 * layer + 1 : 2 * layer + 2, :],
                     gain_rows.at[2 * layer + 1 : 2 * layer + 2, :], low=v["ga"])
        copies["h"] = pltpu.make_async_copy(s["h"], v["h"], insem.at[1])
        copies["h"].start()
        out_ga = publish("ga")
        slot()
        copies["wo"].wait()

        @tiles(width, 512)
        def _(at):
            v["do"][:, at] = dot(v["ga"][...], v["wo"][:, at]).astype(bf16)

        out_ga.wait()
        scatter.ready.add((layer, "ga"))
        for name in ("q", "k", "v", "stats"):
            copies[name].wait()
        pairs = bias.shape[0] * v["q"].shape[1] // 128
        step = attention_backward_step(v["q"], v["k"], v["v"], v["do"], bias, v["stats"], v["dq"], v["dk"], v["dv"])
        for part in range(4):
            loop(part * pairs // 4, (part + 1) * pairs // 4, step)
            slot()
        out_q = [publish(name) for name in ("dq", "dk", "dv")]
        copies["wk"].wait()
        copies["wv"].wait()
        half = v["wk"].shape[2]
        for g in range(GROUPS):
            at = slice(g * half, (g + 1) * half)
            both = dot_nt(v["dk"][:, at], v["wk"][g]) + dot_nt(v["dv"][:, at], v["wv"][g])
            v["dc"][:, g * LAT : (g + 1) * LAT] = both.astype(bf16)
        for copy in out_q:
            copy.wait()
        scatter.ready |= {(layer, "dq"), (layer, "dk"), (layer, "dv")}
        out_dc = publish("dc")
        copies["wq"].wait()
        copies["wl"].wait()

        @tiles(width, 512)
        def _(at):
            v["dm"][:, at] = dot_nt(v["dq"][...], v["wq"][at, :]) + dot_nt(v["dc"][...], v["wl"][at, :])

        out_dc.wait()
        scatter.ready.add((layer, "dc"))
        slot()
        copies["h"].wait()
        norm_back_to(v["g"], v["g"], v["dm"], v["h"], gains[2 * layer : 2 * layer + 1, :],
                     gain_rows.at[2 * layer : 2 * layer + 1, :])
        scatter.ready.add((layer, "end"))
        slot()
    last = pltpu.make_async_copy(v["g"], grad_out, insem.at[0])
    last.start()
    scatter.drain()
    last.wait()


def backward(n, cot, gains, bias, kept, weights, target, cid):
    Z, Y, X = dims_of(n)
    tokens, width = cot.shape
    rows = width // n
    ff = weights[0][5].shape[1]
    wide, lat = weights[0][0].shape[1], weights[0][1].shape[1]
    half = weights[0][2].shape[2]
    widths = [ff, ff, ff, wide, wide, lat, half] * LAYERS + [128]
    chunks = cut(widths, target)
    K = 2 * LAG + 1
    most = max(X, Y)
    sides, ends = max(most, 2) - 1, max(Z - 1, 1)
    most_wide = max(hi - lo for a, lo, mid, hi in chunks)
    ring = lambda *shape: pltpu.VMEM((K,) + shape + (rows, most_wide), bf16)
    tok = lambda w, t=bf16: pltpu.VMEM((tokens, w), t)
    made = dict(gf=width, da=ff, db=ff, ga=width, dq=wide, dk=wide, dv=wide, dc=lat)
    layers = list(reversed(range(LAYERS)))
    operands = [cot, gains, bias]
    for layer in layers:
        operands += [kept[layer][name] for name in KEPT]
    for layer in layers:
        operands += list(weights[layer])
    shapes = [jax.ShapeDtypeStruct((tokens, width), f32)]
    shapes += [jax.ShapeDtypeStruct((rows, w), f32) for w in widths]
    shapes += [jax.ShapeDtypeStruct((tokens, made[name]), bf16) for layer in layers for name in MADE]
    got = pl.pallas_call(
        functools.partial(backward_kernel, n, chunks, K, len(widths)),
        out_shape=shapes,
        in_specs=[ANY, VM, VM] + [ANY] * (len(operands) - 3),
        out_specs=[ANY] + [VM] * len(widths) + [ANY] * (LAYERS * len(MADE)),
        scratch_shapes=[
            pltpu.VMEM((2, tokens, width), bf16),
            pltpu.VMEM((2, tokens, most_wide), bf16),
            ring(Z, Y, X, 2),
            ring(Z, Y, X),
            ring(Z, most),
            ring(sides, Z, most),
            ring(Z),
            ring(sides, Z),
            ring(ends),
            pltpu.VMEM((8, width), f32),
            tok(width), tok(ff), tok(ff), tok(width), tok(wide), tok(wide), tok(wide), tok(wide),
            tok(wide), tok(wide), tok(wide), tok(lat), tok(128, f32),
            tok(width, f32), tok(width, f32), tok(width, f32),
            pltpu.VMEM((2, 2, tokens, 256), f32),
            pltpu.VMEM((2, width, 256), bf16),
            pltpu.VMEM((2, 2, 256, ff), bf16),
        ]
        + [pltpu.VMEM(weights[0][i].shape, bf16) for i in (4, 2, 3, 0, 1)]
        + [DMA((2,)), DMA((2,)), DMA((K,)), DMA((K,))]
        + [DMA((K, 2, sides))] * 4
        + [DMA((K, ends))] * 2
        + [DMA((11,)), DMA((len(MADE),)), DMA((2, 2)), DMA((3, 2))],
        compiler_params=pltpu.CompilerParams(
            collective_id=cid, has_side_effects=True, vmem_limit_bytes=63 << 20
        ),
    )(*operands)
    return got[0], got[1 : 1 + len(widths)]


def body(inputs, cotangent, parents, lengths, g1, wq, wl, wk, wv, wo, g2, wg, wu, wd, *, n):
    trees, tree, width = inputs.shape
    rows = wq.shape[1]
    latr = wk.shape[2]

    def packed(layer):
        cast = lambda w: w[layer].astype(bf16)
        kv = jnp.stack([wk[layer], wv[layer]]).astype(bf16).reshape(-1, wk.shape[3])
        return [cast(wq), cast(wl), kv, cast(wo).T, cast(wg), cast(wu), cast(wd).T]

    gain_rows = jnp.stack([g1[0], g2[0], g1[1], g2[1]], axis=1).astype(bf16)
    gain_rows = jnp.pad(gain_rows, ((0, 0), (0, 128 - 2 * LAYERS)))
    got = gather(n, [gain_rows] + packed(0) + packed(1), 704, 0)
    gains = got[0][:, : 2 * LAYERS].T.astype(f32).reshape(LAYERS, 2, width)

    def unpacked(part):
        q, l, kv, o, g, u, d = part
        kv = kv.reshape(n, 2, GROUPS, latr, -1).transpose(1, 2, 0, 3, 4).reshape(2, GROUPS, LAT, -1)
        return (q, l, kv[0], kv[1], o, g, u, d)

    weights = [unpacked(got[1:8]), unpacked(got[8:15])]
    bias = tree_bias(parents, lengths, tree)
    resid = inputs.reshape(trees * tree, width).astype(f32)
    kept = []
    for layer in range(LAYERS):
        out, n1, q, c, k, v, o, stats, h1, n2, cp, a, b, z = layer_forward(
            resid, weights[layer], gains[layer], bias
        )
        kept.append(
            dict(h=resid, n1=n1, q=q, c=c, k=k, v=v, o=o, stats=stats, h1=h1, n2=n2, a=a, b=b, z=z, cp=cp)
        )
        resid = out
    outputs = resid.reshape(inputs.shape)
    cot = cotangent.reshape(trees * tree, width)
    grad, summed = backward(n, cot, gains.reshape(2 * LAYERS, width), bias, kept, weights, 576, 1)
    out = []
    for layer in range(LAYERS):
        dd, dg, du, do, dq, dl, kv = summed[(1 - layer) * 7 : (1 - layer) * 7 + 7]
        kv = kv.reshape(2, GROUPS, latr, -1)
        gain = summed[14]
        out.append(
            (gain[:, 2 * layer], dq, dl, kv[0], kv[1], do.T, gain[:, 2 * layer + 1], dg, du, dd.T)
        )
    stacked = tuple(jnp.stack([out[layer][slot] for layer in range(LAYERS)]) for slot in range(10))
    return (outputs, grad.reshape(inputs.shape)) + stacked


def solution(mesh):
    n = mesh.shape["fsdp"]
    by_one, by_two = P(None, "fsdp"), P(None, "fsdp", None)
    by_lat, by_last = P(None, None, "fsdp", None), P(None, None, "fsdp")
    params = (by_one, by_two, by_two, by_lat, by_lat, by_last, by_one, by_two, by_two, by_last)
    trees = P("fsdp", None, None)
    return jax.shard_map(
        functools.partial(body, n=n),
        mesh=mesh,
        in_specs=(trees, trees, P("fsdp", None), P("fsdp", None)) + params,
        out_specs=(trees, trees) + params,
        check_vma=False,
    )
```

```python
import functools
import math

import jax
import jax.numpy as jnp
from jax import lax
from jax.experimental import pallas as pl
from jax.experimental.pallas import tpu as pltpu
from jax.sharding import PartitionSpec as P

HEADS = 16
HD = 64
GROUPS = 2
LAT = 256
LAYERS = 2
LAG = 2
epsilon = 1e-05

MESH = pl.DeviceIdType.MESH
ANY = pl.BlockSpec(memory_space=pltpu.HBM)
DMA = pltpu.SemaphoreType.DMA
bf16 = jnp.bfloat16
f32 = jnp.float32


def dims_of(n):
    chips = n // 2
    side = 1
    if chips & (chips - 1) == 0:
        side = 2 ** ((chips.bit_length() - 1) // 3)
    return chips // (side * side), side, side


def index(n, z, y, x, c):
    Z, Y, X = dims_of(n)
    return ((z * Y + y) * X + x) * 2 + c


def place(n):
    Z, Y, X = dims_of(n)
    me = lax.axis_index("fsdp")
    return me // (2 * X * Y), lax.rem(me // (2 * X), Y), lax.rem(me // 2, X), lax.rem(me, 2)


def greet(n, z, y, x, c):
    Z, Y, X = dims_of(n)
    peers = [index(n, lax.rem(z + o, Z), y, x, c) for o in range(1, Z)]
    peers += [index(n, z, lax.rem(y + o, Y), x, c) for o in range(1, Y)]
    peers += [index(n, z, y, lax.rem(x + o, X), c) for o in range(1, X)]
    peers += [index(n, z, y, x, 1 - c)]
    bar = pltpu.get_barrier_semaphore()
    for peer in peers:
        pl.semaphore_signal(bar, inc=1, device_id=(peer,), device_id_type=MESH)
    pl.semaphore_wait(bar, len(peers))


def remote(src, dst, send, recv, device):
    copy = pltpu.make_async_remote_copy(
        src_ref=src,
        dst_ref=dst,
        send_sem=send,
        recv_sem=recv,
        device_id=(device,),
        device_id_type=MESH,
    )
    copy.start()
    return copy


def cut(widths, target):
    out = []
    for a, w in enumerate(widths):
        k, u = max(1, round(w / target)), w // 128
        edges = [round(j * u / k) * 128 for j in range(k + 1)]
        for lo, hi in zip(edges, edges[1:]):
            half = (hi - lo) // 128
            half = half // 2 if len(out) % 2 == 0 else (half + 1) // 2
            out.append((a, lo, lo + half * 128, hi))
    return out


NT = (((1,), (1,)), ((), ()))
TN = (((0,), (0,)), ((), ()))


def dot(a, b):
    return jnp.dot(a, b, preferred_element_type=f32)


def dot_nt(a, b):
    return lax.dot_general(a, b, NT, preferred_element_type=f32)


def dot_tn(a, b):
    return lax.dot_general(a, b, TN, preferred_element_type=f32)


def tiles(size, tile):
    def run(body):
        def step(j, carry):
            body(pl.ds(pl.multiple_of(j * tile, tile), tile))
            return carry

        lax.fori_loop(0, size // tile, step, 0)

    return run


def build_bias(parents, lengths, bias):
    trees, tree = bias.shape[0], bias.shape[1]
    count = parents.shape[1]
    key = lax.broadcasted_iota(jnp.int32, (1, tree), 1)
    row = lax.broadcasted_iota(jnp.int32, (tree, 1), 0)
    for t in range(trees):
        start = jnp.int32(0)
        reach, total = [], jnp.zeros((tree, tree), f32)
        for s in range(count):
            end = start + lengths[t, s]
            line = jnp.where((key >= start) & (key < end), 1.0, 0.0)
            for u in range(s):
                line = line + jnp.where(parents[t, s] == u, reach[u], 0.0)
            reach.append(line)
            total = total + jnp.where((row >= start) & (row < end), 1.0, 0.0) * line
            start = end
        seen = (total > 0.5) & (key <= row)
        bias[t] = jnp.where(seen, 0.0, -1e30)


def norm_to(dst, src, gain, rows=64):
    @tiles(src.shape[0], rows)
    def _(at):
        h = src[at, :]
        r = lax.rsqrt(jnp.mean(h * h, axis=-1, keepdims=True) + epsilon)
        dst[at, :] = (h * r * gain).astype(bf16)


def attention_forward_step(q, k, v, bias, o, stats):
    trees, tree = bias.shape[0], bias.shape[1]
    pairs = q.shape[1] // 128
    scale = 1.0 / math.sqrt(HD)
    lane = lax.broadcasted_iota(jnp.int32, (tree, 128), 1)

    def step(j):
        t, pair = j // pairs, lax.rem(j, pairs)
        rows = pl.ds(pl.multiple_of(t * tree, tree), tree)
        cols = pl.ds(pl.multiple_of(pair * 128, 128), 128)
        q2, k2, v2 = q[rows, cols], k[rows, cols], v[rows, cols]
        mixed, log_total = [], stats[rows, :]
        for half in range(2):
            mine = (lane >= HD) if half else (lane < HD)
            s = dot_nt(jnp.where(mine, q2, jnp.zeros_like(q2)), k2) * scale + bias[t]
            top = jnp.max(s, axis=-1, keepdims=True)
            e = jnp.exp(s - top)
            total = jnp.sum(e, axis=-1, keepdims=True)
            p = (e * (1.0 / total)).astype(bf16)
            mixed.append(dot(p, v2))
            log_total = jnp.where(lane == pair * 2 + half, top + jnp.log(total), log_total)
        stats[rows, :] = log_total
        o[rows, cols] = jnp.where(lane < HD, mixed[0], mixed[1]).astype(bf16)

    return step


VM = pl.BlockSpec(memory_space=pltpu.VMEM)
SM = pl.BlockSpec(memory_space=pltpu.SMEM)


def norm_back_to(dst, carry_in, dn, h_ref, gain, gain_grad, low=None, rows=64):
    gain_grad[...] = jnp.zeros_like(gain_grad)

    @tiles(h_ref.shape[0], rows)
    def _(at):
        h, d = h_ref[at, :], dn[at, :]
        r = lax.rsqrt(jnp.mean(h * h, axis=-1, keepdims=True) + epsilon)
        gain_grad[...] += jnp.sum(d * h * r, axis=0, keepdims=True)
        weighted = d * gain
        inner = jnp.mean(weighted * h, axis=-1, keepdims=True)
        total = carry_in[at, :] + (r * weighted - h * (r * r * r) * inner)
        dst[at, :] = total
        if low is not None:
            low[at, :] = total.astype(bf16)


def attention_backward_step(q, k, v, do, bias, stats, dq, dk, dv):
    trees, tree = bias.shape[0], bias.shape[1]
    pairs = q.shape[1] // 128
    scale = 1.0 / math.sqrt(HD)
    lane = lax.broadcasted_iota(jnp.int32, (tree, 128), 1)

    def step(j):
        t, pair = j // pairs, lax.rem(j, pairs)
        rows = pl.ds(pl.multiple_of(t * tree, tree), tree)
        cols = pl.ds(pl.multiple_of(pair * 128, 128), 128)
        q2, k2, v2, do2 = q[rows, cols], k[rows, cols], v[rows, cols], do[rows, cols]
        logs = stats[rows, :]
        zero = jnp.zeros_like(q2)
        got = []
        for half in range(2):
            mine = (lane >= HD) if half else (lane < HD)
            log_total = jnp.sum(jnp.where(lane == pair * 2 + half, logs, 0.0), axis=-1, keepdims=True)
            s = dot_nt(jnp.where(mine, q2, zero), k2) * scale + bias[t]
            p = jnp.exp(s - log_total)
            dp = dot_nt(jnp.where(mine, do2, zero), v2)
            inner = jnp.sum(p * dp, axis=-1, keepdims=True)
            ds = (p * (dp - inner)).astype(bf16)
            got.append((dot(ds, k2), dot_tn(ds, q2), dot_tn(p.astype(bf16), do2)))
        low = lane < HD
        dq[rows, cols] = (jnp.where(low, got[0][0], got[1][0]) * scale).astype(bf16)
        dk[rows, cols] = (jnp.where(low, got[0][1], got[1][1]) * scale).astype(bf16)
        dv[rows, cols] = jnp.where(low, got[0][2], got[1][2]).astype(bf16)

    return step


class Scatter:
    def __init__(self, n, chunks, jobs, K, outs, bufs, sems, gain_rows):
        self.n, self.chunks, self.jobs, self.K, self.outs = n, chunks, jobs, K, outs
        self.LB, self.RB, self.G, self.R0, self.P1, self.R1, self.P2, self.R2, self.R3 = bufs
        self.lsem, self.ls, self.s0, self.r0, self.s1, self.r1, self.s2, self.r2, self.s3, self.r3 = sems
        self.gain_rows = gain_rows
        self.ready = set()
        self.stages = [self.from_partner, self.first_side, self.second_side, self.along_z, self.finish]
        self.held = [None] * len(chunks)
        self.at = 0
        self.started = False
        turns, last = [], None
        for a, lo, mid, hi in chunks:
            left = jobs[a]["left"]
            if left is not last and left is not None:
                turns.append(a)
                last = left
            turns_now = len(turns) - 1
            self.turn = getattr(self, "turn", []) + [turns_now]
        self.turns = turns

    def left_copy(self, t):
        return pltpu.make_async_copy(self.jobs[self.turns[t]]["left"], self.LB.at[t % 2], self.lsem.at[t % 2])

    def first_of(self, i):
        return self.jobs[self.chunks[i][0]]["left"] is not None and (i == 0 or self.turn[i] != self.turn[i - 1])

    def right_copy(self, i, which=0):
        a, lo, mid, hi = self.chunks[i]
        return pltpu.make_async_copy(
            self.jobs[a]["right"][which].at[:, lo:hi], self.RB.at[i % 2, :, 0 : hi - lo], self.ls.at[i % 2]
        )

    def fetch(self, i):
        if self.first_of(i):
            self.left_copy(self.turn[i]).start()
        if self.jobs[self.chunks[i][0]]["left"] is not None:
            self.right_copy(i).start()

    def has(self, i):
        return i >= len(self.chunks) or all(w in self.ready for w in self.jobs[self.chunks[i][0]]["needs"])

    def slot(self, times=1):
        for _ in range(times):
            i = self.at
            if i < len(self.chunks) and not (self.has(i) and self.has(i + 1)):
                return
            if not self.started:
                self.fetch(0)
                self.started = True
            last = len(self.stages) - 1
            if i >= len(self.chunks) + LAG * last:
                return
            for s in range(last, -1, -1):
                j = i - LAG * s
                if 0 <= j < len(self.chunks):
                    if s > 0:
                        for copy in self.held[j]:
                            copy.wait()
                    self.held[j] = self.stages[s](j)
            self.at += 1

    def drain(self):
        while self.at < len(self.chunks) + LAG * (len(self.stages) - 1):
            before = self.at
            self.slot()
            assert self.at > before

    def from_partner(self, i):
        Z, Y, X = dims_of(self.n)
        z, y, x, c = place(self.n)
        a, lo, mid, hi = self.chunks[i]
        k, w = i % self.K, hi - lo
        G, LB, RB = self.G, self.LB, self.RB
        rows = G.shape[6 - 1]
        job = self.jobs[a]
        t = self.turn[i]
        depth = LB.shape[2] // Z
        if job["left"] is not None:
            if self.first_of(i):
                self.left_copy(t).wait()
            self.right_copy(i).wait()
        if i + 1 < len(self.chunks):
            self.fetch(i + 1)
        if job["left"] is None:
            lines = self.gain_rows[...].astype(bf16)
            pick = lax.broadcasted_iota(jnp.int32, (lines.shape[0], w), 0)
            pick = (pick == lax.broadcasted_iota(jnp.int32, (lines.shape[0], w), 1)).astype(bf16)
            for zz in range(Z):
                part = dot_tn(lines[:, zz * depth : (zz + 1) * depth], pick)
                G[k, zz, :, :, :, :, 0:w] = part.astype(bf16).reshape(Y, X, 2, rows, w)
        elif len(job["right"]) == 1:

            def block(zz, carry):
                at = pl.ds(pl.multiple_of(zz * depth, depth), depth)
                part = dot_tn(LB[t % 2, :, at], RB[i % 2, :, 0:w])
                G[k, zz, :, :, :, :, 0:w] = part.astype(bf16).reshape(Y, X, 2, rows, w)
                return carry

            lax.fori_loop(0, Z, block, 0)
        else:
            quarter = rows // 4
            group = lax.broadcasted_iota(jnp.int32, (rows, w), 0) >> (quarter.bit_length() - 1)
            for which in range(4):
                if which:
                    copy = self.right_copy(i, which)
                    copy.start()
                    copy.wait()

                def block(zz, carry):
                    at = pl.ds(pl.multiple_of(zz * depth, depth), depth)
                    part = dot_tn(LB[t % 2, :, at], RB[i % 2, :, 0:w]).reshape(Y, X, 2, rows, w)
                    if which:
                        part = jnp.where(group == which, part, G[k, zz, :, :, :, :, 0:w].astype(f32))
                    G[k, zz, :, :, :, :, 0:w] = part.astype(bf16)
                    return carry

                lax.fori_loop(0, Z, block, 0)
        return [
            remote(
                G.at[k, :, :, :, 1 - c, :, 0:w],
                self.R0.at[k, :, :, :, :, 0:w],
                self.s0.at[k],
                self.r0.at[k],
                index(self.n, z, y, x, 1 - c),
            )
        ]

    def first_side(self, i):
        n, G, R0, R1 = self.n, self.G, self.R0, self.R1
        Z, Y, X = dims_of(n)
        z, y, x, c = place(n)
        a, lo, mid, hi = self.chunks[i]
        k, w, h = i % self.K, hi - lo, mid - lo

        def add(j, carry):
            zz, yy, xx = j // (Y * X), lax.rem(j // X, Y), lax.rem(j, X)
            total = G[k, zz, yy, xx, c, :, 0:w].astype(f32) + R0[k, zz, yy, xx, :, 0:w].astype(f32)
            G[k, zz, yy, xx, c, :, 0:w] = total.astype(bf16)
            return carry

        lax.fori_loop(0, Z * Y * X, add, 0)
        copies = []
        for o in range(1, Y if h > 0 else 1):
            d = lax.rem(y + o, Y)
            src, dst = G.at[k, :, d, :, c, :, 0:h], R1.at[k, o - 1, :, 0:X, :, 0:h]
            copies.append(remote(src, dst, self.s1.at[k, 0, o - 1], self.r1.at[k, 0, o - 1], index(n, z, d, x, c)))
        for o in range(1, X):
            d = lax.rem(x + o, X)
            src, dst = G.at[k, :, :, d, c, :, h:w], R1.at[k, o - 1, :, 0:Y, :, h:w]
            copies.append(remote(src, dst, self.s1.at[k, 1, o - 1], self.r1.at[k, 1, o - 1], index(n, z, y, d, c)))
        return copies

    def second_side(self, i):
        n, G, P1, R1, R2 = self.n, self.G, self.P1, self.R1, self.R2
        Z, Y, X = dims_of(n)
        z, y, x, c = place(n)
        a, lo, mid, hi = self.chunks[i]
        k, w, h = i % self.K, hi - lo, mid - lo
        for half, start, end, size, terms in ((0, 0, h, X, Y), (1, h, w, Y, X)):
            if start == end:
                continue

            def add(j, carry):
                zz, ss = j // size, lax.rem(j, size)
                if half == 0:
                    total = G[k, zz, y, ss, c, :, start:end].astype(f32)
                else:
                    total = G[k, zz, ss, x, c, :, start:end].astype(f32)
                for o in range(1, terms):
                    total = total + R1[k, o - 1, zz, ss, :, start:end].astype(f32)
                P1[k, zz, ss, :, start:end] = total.astype(bf16)
                return carry

            lax.fori_loop(0, Z * size, add, 0)
        copies = []
        for o in range(1, X if h > 0 else 1):
            d = lax.rem(x + o, X)
            src, dst = P1.at[k, :, d, :, 0:h], R2.at[k, o - 1, :, :, 0:h]
            copies.append(remote(src, dst, self.s2.at[k, 0, o - 1], self.r2.at[k, 0, o - 1], index(n, z, y, d, c)))
        for o in range(1, Y):
            d = lax.rem(y + o, Y)
            src, dst = P1.at[k, :, d, :, h:w], R2.at[k, o - 1, :, :, h:w]
            copies.append(remote(src, dst, self.s2.at[k, 1, o - 1], self.r2.at[k, 1, o - 1], index(n, z, d, x, c)))
        return copies

    def along_z(self, i):
        n, P1, P2, R2, R3 = self.n, self.P1, self.P2, self.R2, self.R3
        Z, Y, X = dims_of(n)
        z, y, x, c = place(n)
        a, lo, mid, hi = self.chunks[i]
        k, w, h = i % self.K, hi - lo, mid - lo
        for start, end, terms, mine in ((0, h, X, x), (h, w, Y, y)):
            if start == end:
                continue

            def add(zz, carry):
                total = P1[k, zz, mine, :, start:end].astype(f32)
                for o in range(1, terms):
                    total = total + R2[k, o - 1, zz, :, start:end].astype(f32)
                P2[k, zz, :, start:end] = total.astype(bf16)
                return carry

            lax.fori_loop(0, Z, add, 0)
        copies = []
        for o in range(1, Z):
            d = lax.rem(z + o, Z)
            src, dst = P2.at[k, d, :, 0:w], R3.at[k, o - 1, :, 0:w]
            copies.append(remote(src, dst, self.s3.at[k, o - 1], self.r3.at[k, o - 1], index(n, d, y, x, c)))
        return copies

    def finish(self, i):
        Z, Y, X = dims_of(self.n)
        z, y, x, c = place(self.n)
        a, lo, mid, hi = self.chunks[i]
        k, w = i % self.K, hi - lo
        total = self.P2[k, z, :, 0:w].astype(f32)
        for o in range(1, Z):
            total = total + self.R3[k, o - 1, :, 0:w].astype(f32)
        self.outs[a][:, lo:hi] = total
        return []


def loop(lo, hi, body):
    def step(j, carry):
        body(j)
        return carry

    lax.fori_loop(lo, hi, step, 0)


def span(j, size):
    return pl.ds(pl.multiple_of(j * size, size), size)


KEPT = ("h", "n1", "q", "k", "v", "o", "stats", "h1", "n2", "a", "b", "z", "cp")
NAMES = ("wq", "wl", "wkv", "wo", "wg", "wu", "wd")
MADE = ("gf", "da", "db", "ga", "dq", "dk", "dv", "dc")


def backward_kernel(n, chunks, K, counts, *refs):
    it = iter(refs)
    take = lambda names: {name: next(it) for name in names}
    cot, gains, bias = next(it), next(it), next(it)
    kept = {layer: take(KEPT) for layer in reversed(range(LAYERS))}
    weights = {layer: take(NAMES) for layer in reversed(range(LAYERS))}
    grad_out = next(it)
    outs = [next(it) for _ in range(counts)]
    made = {layer: take(MADE) for layer in reversed(range(LAYERS))}
    bufs = [next(it) for _ in range(9)]
    gain_rows = next(it)
    v = take(("gf", "da", "db", "ga", "do", "q", "k", "v", "dq", "dk", "dv", "dc", "stats",
              "g", "h", "dm", "ab", "wd", "wgu", "wo", "wkv", "wq", "wl"))
    sems = [next(it) for _ in range(10)]
    insem, outsem, asem, wsem = [next(it) for _ in range(4)]

    jobs = []
    for layer in reversed(range(LAYERS)):
        s, m = kept[layer], made[layer]
        need = lambda *names: [(layer, name) for name in names]
        jobs += [
            {"left": m["gf"], "right": [s["z"]], "needs": need("gf")},
            {"left": s["n2"], "right": [m["da"]], "needs": need("da")},
            {"left": s["n2"], "right": [m["db"]], "needs": need("db")},
            {"left": m["ga"], "right": [s["o"]], "needs": need("ga")},
            {"left": s["n1"], "right": [m["dq"]], "needs": need("dq")},
            {"left": s["n1"], "right": [m["dc"]], "needs": need("dc")},
        ]
        half = m["dk"].shape[1] // GROUPS
        rights = [m[name].at[:, g * half : (g + 1) * half] for name in ("dk", "dv") for g in range(GROUPS)]
        jobs += [{"left": s["cp"], "right": rights, "needs": need("dk", "dv")}]
    jobs += [{"left": None, "right": None, "needs": [(0, "end")]}]
    scatter = Scatter(n, chunks, jobs, K, outs, bufs, sems, gain_rows)
    slot = scatter.slot

    ff, width = v["da"].shape[1], v["g"].shape[1]
    count = ff // 256
    tokens = v["g"].shape[0]
    gain_rows[...] = jnp.zeros_like(gain_rows)
    greeted = []

    for layer in reversed(range(LAYERS)):
        s, w, m = kept[layer], weights[layer], made[layer]
        first = layer == LAYERS - 1
        copies = {}

        def load(name, src, at):
            copies[name] = pltpu.make_async_copy(src, v[name], insem.at[at])
            copies[name].start()

        def tile_ab(j, which):
            src = s["ab"[which]]
            return pltpu.make_async_copy(src.at[:, span(j, 256)], v["ab"].at[which, lax.rem(j, 2)], asem.at[which, lax.rem(j, 2)])

        def tile_wd(j):
            return pltpu.make_async_copy(w["wd"].at[:, span(j, 256)], v["wd"].at[lax.rem(j, 2)], wsem.at[0, lax.rem(j, 2)])

        def tile_gu(j, which):
            src = w["wg"] if which == 0 else w["wu"]
            return pltpu.make_async_copy(src.at[span(j, 256), :], v["wgu"].at[which, j % 2], wsem.at[1 + which, j % 2])

        def publish(name):
            copy = pltpu.make_async_copy(v[name], m[name], outsem.at[MADE.index(name)])
            copy.start()
            return copy

        if first:
            load("g", cot, 0)
        tile_wd(0).start()
        tile_ab(0, 0).start()
        tile_ab(0, 1).start()
        load("h", s["h1"], 1)
        for at, name in enumerate(("q", "k", "v", "stats")):
            load(name, s[name], 2 + at)
        for at, name in enumerate(("wo", "wkv", "wq", "wl")):
            load(name, w[name], 6 + at)
        for j in range(2):
            tile_gu(j, 0).start()
            tile_gu(j, 1).start()
        if first:
            z, y, x, c = place(n)
            greet(n, z, y, x, c)
            copies["g"].wait()

        @tiles(tokens, 64)
        def _(at):
            v["gf"][at, :] = v["g"][at, :].astype(bf16)

        publish("gf").wait()
        scatter.ready.add((layer, "gf"))
        slot()

        def dz_step(j):
            at = span(j, 256)
            tile_wd(j).wait()
            tile_ab(j, 0).wait()
            tile_ab(j, 1).wait()

            @pl.when(j + 1 < count)
            def _():
                tile_wd(j + 1).start()
                tile_ab(j + 1, 0).start()
                tile_ab(j + 1, 1).start()

            dz = dot(v["gf"][...], v["wd"][lax.rem(j, 2)])
            a, b = v["ab"][0, lax.rem(j, 2)], v["ab"][1, lax.rem(j, 2)]
            sig = 1.0 / (1.0 + jnp.exp(-a))
            v["da"][:, at] = (dz * b * sig * (1.0 + a * (1.0 - sig))).astype(bf16)
            v["db"][:, at] = (dz * a * sig).astype(bf16)

        cuts = [0, count // 3, 2 * count // 3, count]
        for lo, hi in zip(cuts, cuts[1:]):
            loop(lo, hi, dz_step)
            slot()
        out_da, out_db = publish("da"), publish("db")
        for j in range(width // 256):
            tile_gu(j, 0).wait()
            tile_gu(j, 1).wait()
            at = slice(j * 256, (j + 1) * 256)
            v["dm"][:, at] = dot_nt(v["da"][...], v["wgu"][0, j % 2]) + dot_nt(v["db"][...], v["wgu"][1, j % 2])
            if j + 2 < width // 256:
                tile_gu(j + 2, 0).start()
                tile_gu(j + 2, 1).start()
            if j == 0:
                out_da.wait()
                out_db.wait()
                scatter.ready |= {(layer, "da"), (layer, "db")}
            if j % 2:
                slot()
        copies["h"].wait()
        norm_back_to(v["g"], v["g"], v["dm"], v["h"], gains[2 * layer + 1 : 2 * layer + 2, :],
                     gain_rows.at[2 * layer + 1 : 2 * layer + 2, :], low=v["ga"])
        copies["h"] = pltpu.make_async_copy(s["h"], v["h"], insem.at[1])
        copies["h"].start()
        out_ga = publish("ga")
        slot()
        copies["wo"].wait()

        @tiles(width, 512)
        def _(at):
            v["do"][:, at] = dot(v["ga"][...], v["wo"][:, at]).astype(bf16)

        out_ga.wait()
        scatter.ready.add((layer, "ga"))
        for name in ("q", "k", "v", "stats"):
            copies[name].wait()
        pairs = bias.shape[0] * v["q"].shape[1] // 128
        step = attention_backward_step(v["q"], v["k"], v["v"], v["do"], bias, v["stats"], v["dq"], v["dk"], v["dv"])
        for part in range(4):
            loop(part * pairs // 4, (part + 1) * pairs // 4, step)
            slot()
        out_q = [publish(name) for name in ("dq", "dk", "dv")]
        copies["wkv"].wait()
        half = v["wkv"].shape[2]
        for g in range(GROUPS):
            at = slice(g * half, (g + 1) * half)
            both = dot_nt(v["dk"][:, at], v["wkv"][g]) + dot_nt(v["dv"][:, at], v["wkv"][GROUPS + g])
            v["dc"][:, g * LAT : (g + 1) * LAT] = both.astype(bf16)
        for copy in out_q:
            copy.wait()
        scatter.ready |= {(layer, "dq"), (layer, "dk"), (layer, "dv")}
        out_dc = publish("dc")
        copies["wq"].wait()
        copies["wl"].wait()

        @tiles(width, 512)
        def _(at):
            v["dm"][:, at] = dot_nt(v["dq"][...], v["wq"][at, :]) + dot_nt(v["dc"][...], v["wl"][at, :])

        out_dc.wait()
        scatter.ready.add((layer, "dc"))
        slot()
        copies["h"].wait()
        norm_back_to(v["g"], v["g"], v["dm"], v["h"], gains[2 * layer : 2 * layer + 1, :],
                     gain_rows.at[2 * layer : 2 * layer + 1, :])
        scatter.ready.add((layer, "end"))
        slot()
    last = pltpu.make_async_copy(v["g"], grad_out, insem.at[0])
    last.start()
    scatter.drain()
    last.wait()


def backward(n, cot, gains, bias, kept, weights, target, cid):
    Z, Y, X = dims_of(n)
    tokens, width = cot.shape
    rows = width // n
    ff = weights[0][4].shape[1]
    wide, lat = weights[0][0].shape[1], weights[0][1].shape[1]
    half = weights[0][2].shape[2]
    widths = [ff, ff, ff, wide, wide, lat, half] * LAYERS + [128]
    chunks = cut(widths, target)
    K = 2 * LAG + 1
    most = max(X, Y)
    sides, ends = max(most, 2) - 1, max(Z - 1, 1)
    most_wide = max(hi - lo for a, lo, mid, hi in chunks)
    ring = lambda *shape: pltpu.VMEM((K,) + shape + (rows, most_wide), bf16)
    tok = lambda w, t=bf16: pltpu.VMEM((tokens, w), t)
    made = dict(gf=width, da=ff, db=ff, ga=width, dq=wide, dk=wide, dv=wide, dc=lat)
    layers = list(reversed(range(LAYERS)))
    operands = [cot, gains, bias]
    for layer in layers:
        operands += [kept[layer][name] for name in KEPT]
    for layer in layers:
        operands += list(weights[layer])
    shapes = [jax.ShapeDtypeStruct((tokens, width), f32)]
    shapes += [jax.ShapeDtypeStruct((rows, w), f32) for w in widths]
    shapes += [jax.ShapeDtypeStruct((tokens, made[name]), bf16) for layer in layers for name in MADE]
    got = pl.pallas_call(
        functools.partial(backward_kernel, n, chunks, K, len(widths)),
        out_shape=shapes,
        in_specs=[ANY, VM, VM] + [ANY] * (len(operands) - 3),
        out_specs=[ANY] + [VM] * len(widths) + [ANY] * (LAYERS * len(MADE)),
        scratch_shapes=[
            pltpu.VMEM((2, tokens, width), bf16),
            pltpu.VMEM((2, tokens, most_wide), bf16),
            ring(Z, Y, X, 2),
            ring(Z, Y, X),
            ring(Z, most),
            ring(sides, Z, most),
            ring(Z),
            ring(sides, Z),
            ring(ends),
            pltpu.VMEM((8, width), f32),
            tok(width), tok(ff), tok(ff), tok(width), tok(wide), tok(wide), tok(wide), tok(wide),
            tok(wide), tok(wide), tok(wide), tok(lat), tok(128, f32),
            tok(width, f32), tok(width, f32), tok(width, f32),
            pltpu.VMEM((2, 2, tokens, 256), f32),
            pltpu.VMEM((2, width, 256), bf16),
            pltpu.VMEM((2, 2, 256, ff), bf16),
        ]
        + [pltpu.VMEM(weights[0][i].shape, bf16) for i in (3, 2, 0, 1)]
        + [DMA((2,)), DMA((2,)), DMA((K,)), DMA((K,))]
        + [DMA((K, 2, sides))] * 4
        + [DMA((K, ends))] * 2
        + [DMA((10,)), DMA((len(MADE),)), DMA((2, 2)), DMA((3, 2))],
        compiler_params=pltpu.CompilerParams(
            collective_id=cid, has_side_effects=True, vmem_limit_bytes=63 << 20
        ),
    )(*operands)
    return got[0], got[1 : 1 + len(widths)]


class Gather:
    def __init__(self, n, chunks, ins, outs, sems):
        self.n, self.chunks, self.ins, self.outs = n, chunks, ins, outs
        self.own_sem, self.zs, self.zr, self.as_, self.ar, self.bs, self.br, self.cs, self.cr = sems
        self.stages = [self.along_z, self.first_side, self.second_side, self.to_partner, lambda i: []]
        self.held = [None] * len(chunks)
        self.at = 0
        self.total = len(chunks) + LAG * (len(self.stages) - 1)

    def slot(self, times=1):
        for _ in range(times):
            if self.at >= self.total:
                return
            last = len(self.stages) - 1
            for s in range(last, -1, -1):
                j = self.at - LAG * s
                if 0 <= j < len(self.chunks):
                    if s > 0:
                        for copy in self.held[j]:
                            copy.wait()
                    self.held[j] = self.stages[s](j)
            self.at += 1

    def until(self, a, column):
        need = max(i for i, (b, lo, mid, hi) in enumerate(self.chunks) if b == a and lo < column)
        while self.at < need + LAG * (len(self.stages) - 1) + 1:
            self.slot()

    def to_x(self, o):
        Z, Y, X = dims_of(self.n)
        z, y, x, c = place(self.n)
        return index(self.n, z, y, lax.rem(x + o, X), c)

    def to_y(self, o):
        Z, Y, X = dims_of(self.n)
        z, y, x, c = place(self.n)
        return index(self.n, z, lax.rem(y + o, Y), x, c)

    def along_z(self, i):
        n = self.n
        Z, Y, X = dims_of(n)
        z, y, x, c = place(n)
        a, lo, mid, hi = self.chunks[i]
        src, dst = self.ins[a].at[:, lo:hi], self.outs[a].at[z, y, x, c, :, lo:hi]
        own = pltpu.make_async_copy(src, dst, self.own_sem.at[i])
        own.start()
        return [own] + [
            remote(src, dst, self.zs.at[i, o - 1], self.zr.at[i, o - 1], index(n, lax.rem(z + o, Z), y, x, c))
            for o in range(1, Z)
        ]

    def first_side(self, i):
        Z, Y, X = dims_of(self.n)
        z, y, x, c = place(self.n)
        a, lo, mid, hi = self.chunks[i]
        copies = []
        for h, (start, end, size, to) in enumerate(((lo, mid, X, self.to_x), (mid, hi, Y, self.to_y))):
            part = self.outs[a].at[:, y, x, c, :, start:end]
            for o in range(1, size if end > start else 1):
                copies.append(remote(part, part, self.as_.at[i, h, o - 1], self.ar.at[i, h, o - 1], to(o)))
        return copies

    def second_side(self, i):
        Z, Y, X = dims_of(self.n)
        z, y, x, c = place(self.n)
        a, lo, mid, hi = self.chunks[i]
        copies = []
        for o in range(1, Y if mid > lo else 1):
            part = self.outs[a].at[:, y, :, c, :, lo:mid]
            copies.append(remote(part, part, self.bs.at[i, 0, o - 1], self.br.at[i, 0, o - 1], self.to_y(o)))
        for o in range(1, X):
            part = self.outs[a].at[:, :, x, c, :, mid:hi]
            copies.append(remote(part, part, self.bs.at[i, 1, o - 1], self.br.at[i, 1, o - 1], self.to_x(o)))
        return copies

    def to_partner(self, i):
        z, y, x, c = place(self.n)
        a, lo, mid, hi = self.chunks[i]
        part = self.outs[a].at[:, :, :, c, :, lo:hi]
        return [remote(part, part, self.cs.at[i], self.cr.at[i], index(self.n, z, y, x, 1 - c))]


SAVED = ("n1", "q", "k", "v", "o", "stats", "h1", "n2", "cp", "z", "wkv")
PARTS = ("wq", "wl", "kv", "wo", "wg", "wu", "wd")


def fill_picks(n, picks):
    which, lat, width = picks.shape
    quarter = width // n // which
    bits = quarter.bit_length() - 1
    row = lax.broadcasted_iota(jnp.int32, (lat, width), 0)
    col = lax.broadcasted_iota(jnp.int32, (lat, width), 1)
    base = ((row >> bits) * (which * quarter)) + (row & (quarter - 1))
    for i in range(which):
        picks[i] = jnp.where(col == base + i * quarter, 1.0, 0.0).astype(bf16)


def forward_kernel(n, chunks, *refs):
    it = iter(refs)
    take = lambda names: {name: next(it) for name in names}
    parents, lengths, tokens_ref, gain_in = [next(it) for _ in range(4)]
    count = 1 + LAYERS * len(PARTS)
    ins = [gain_in] + [next(it) for _ in range(count - 1)]
    final, bias, gains_out = next(it), next(it), next(it)
    outs = [next(it) for _ in range(count)]
    kept = [take(SAVED + ("a", "b", "h")) for _ in range(LAYERS)]
    v = take(SAVED + ("h", "c", "ab", "picks", "gr", "gt", "wq", "wl", "kv", "wo", "wgu", "wd"))
    gather = Gather(n, chunks, ins, outs, [next(it) for _ in range(9)])
    insem, savesem, absem, gusem, wdsem = [next(it) for _ in range(5)]
    slot = gather.slot
    z, y, x, c = place(n)
    greet(n, z, y, x, c)
    slot(3)

    def rows_of(a):
        return outs[a].reshape(outs[a].shape[0] * outs[a].shape[1] * outs[a].shape[2] * 2 * outs[a].shape[4], outs[a].shape[5])

    gathered = [rows_of(a) for a in range(count)]

    def load(a, name, at):
        gather.until(a, outs[a].shape[5])
        copy = pltpu.make_async_copy(gathered[a], v[name], insem.at[at])
        copy.start()
        return copy

    @tiles(tokens_ref.shape[0], 64)
    def _(at):
        v["h"][at, :] = tokens_ref[at, :].astype(f32)

    build_bias(parents, lengths, bias)
    slot()
    fill_picks(n, v["picks"])
    slot()
    copy = load(0, "gr", 0)
    copy.wait()
    lines = lax.broadcasted_iota(jnp.int32, (8, 128), 0) == lax.broadcasted_iota(jnp.int32, (8, 128), 1)
    v["gt"][...] = dot_nt(lines.astype(bf16), v["gr"][...])
    gains_out[...] = v["gt"][...]
    gains = v["gt"]

    for layer in range(LAYERS):
        s = kept[layer]
        base = 1 + layer * len(PARTS)
        saves = []

        def save(name, src=None):
            copy = pltpu.make_async_copy(v[src or name], s[name], savesem.at[len(saves)])
            copy.start()
            saves.append(copy)

        h, n1, n2, h1 = v["h"], v["n1"], v["n2"], v["h1"]
        save("h")
        norm_to(n1, h, gains[2 * layer : 2 * layer + 1, :])
        save("n1")
        slot()
        load(base, "wq", 0).wait()
        wl_copy = load(base + 1, "wl", 1)

        @tiles(v["wq"].shape[1], 512)
        def _(at):
            v["q"][:, at] = dot(n1[...], v["wq"][:, at]).astype(bf16)

        save("q")
        slot()
        wl_copy.wait()
        kv_copy = load(base + 2, "kv", 2)
        v["c"][...] = dot(n1[...], v["wl"][...]).astype(bf16)
        spread = dot(v["c"][:, 0:LAT], v["picks"][0] + v["picks"][GROUPS])
        for g in range(1, GROUPS):
            spread += dot(v["c"][:, g * LAT : (g + 1) * LAT], v["picks"][g] + v["picks"][GROUPS + g])
        v["cp"][...] = spread.astype(bf16)
        save("cp")
        kv_copy.wait()
        half = v["kv"].shape[1]
        for i in range(2 * GROUPS):
            v["wkv"][i] = dot(v["picks"][i], v["kv"][...]).astype(bf16)
        save("wkv")
        slot()
        for g in range(GROUPS):
            cg = v["c"][:, g * LAT : (g + 1) * LAT]
            v["k"][:, g * half : (g + 1) * half] = dot(cg, v["wkv"][g]).astype(bf16)
            v["v"][:, g * half : (g + 1) * half] = dot(cg, v["wkv"][GROUPS + g]).astype(bf16)
        save("k")
        save("v")
        slot()
        v["stats"][...] = jnp.zeros_like(v["stats"])
        pairs = bias.shape[0] * v["q"].shape[1] // 128
        step = attention_forward_step(v["q"], v["k"], v["v"], bias, v["o"], v["stats"])
        for part in range(4):
            loop(part * pairs // 4, (part + 1) * pairs // 4, step)
            slot()
        save("o")
        save("stats")
        load(base + 3, "wo", 0).wait()

        @tiles(v["wo"].shape[0], 512)
        def _(at):
            h1[:, at] = h[:, at] + dot_nt(v["o"][...], v["wo"][at, :])

        save("h1")
        slot()
        norm_to(n2, h1, gains[2 * layer + 1 : 2 * layer + 2, :])
        save("n2")
        ff = v["z"].shape[1]
        steps = ff // 256

        def tile_gu(j, which):
            src = gathered[base + 4 + which]
            return pltpu.make_async_copy(src.at[:, span(j, 256)], v["wgu"].at[which, lax.rem(j, 2)], gusem.at[which, lax.rem(j, 2)])

        def put(j, which):
            dst = s["ab"[which]]
            return pltpu.make_async_copy(v["ab"].at[which, lax.rem(j, 2)], dst.at[:, span(j, 256)], absem.at[which, lax.rem(j, 2)])

        cuts = [i * steps // 5 for i in range(6)]
        for lo, hi in zip(cuts, cuts[1:]):
            gather.until(base + 4, hi * 256)
            gather.until(base + 5, hi * 256)
            tile_gu(lo, 0).start()
            tile_gu(lo, 1).start()

            def gate_step(j):
                at = span(j, 256)
                tile_gu(j, 0).wait()
                tile_gu(j, 1).wait()

                @pl.when(j + 1 < hi)
                def _():
                    tile_gu(j + 1, 0).start()
                    tile_gu(j + 1, 1).start()

                @pl.when(j >= 2)
                def _():
                    put(j - 2, 0).wait()
                    put(j - 2, 1).wait()

                a = dot(n2[...], v["wgu"][0, lax.rem(j, 2)])
                b = dot(n2[...], v["wgu"][1, lax.rem(j, 2)])
                v["ab"][0, lax.rem(j, 2)] = a
                v["ab"][1, lax.rem(j, 2)] = b
                put(j, 0).start()
                put(j, 1).start()
                v["z"][:, at] = (a / (1.0 + jnp.exp(-a)) * b).astype(bf16)

            loop(lo, hi, gate_step)
            slot()
        save("z")
        for copy in saves:
            copy.wait()
        for j in (steps - 2, steps - 1):
            put(j, 0).wait()
            put(j, 1).wait()
        downs = [(lo, hi) for a, lo, mid, hi in chunks if a == base + 6]

        def tile_wd(i):
            lo, hi = downs[i]
            gather.until(base + 6, hi)
            copy = pltpu.make_async_copy(gathered[base + 6].at[:, lo:hi], v["wd"].at[i % 2, :, 0 : hi - lo], wdsem.at[i % 2])
            copy.start()
            return copy

        coming = tile_wd(0)
        for i, (lo, hi) in enumerate(downs):
            coming.wait()
            if i + 1 < len(downs):
                coming = tile_wd(i + 1)

            @tiles(h.shape[1], 512)
            def _(at):
                add = dot_nt(v["z"][:, lo:hi], v["wd"][i % 2, at, 0 : hi - lo])
                h[:, at] = (h1[:, at] if i == 0 else h[:, at]) + add

            slot()
    last = pltpu.make_async_copy(v["h"], final, insem.at[0])
    last.start()
    slot(gather.total)
    last.wait()


def forward(n, tokens, parents, lengths, trees, shards, target, cid):
    Z, Y, X = dims_of(n)
    rows, width = tokens.shape
    shapes = {name: shards[1 + i].shape for i, name in enumerate(PARTS)}
    wide, lat, half, ff = shapes["wq"][1], shapes["wl"][1], shapes["kv"][1], shapes["wg"][1]
    chunks = cut([s.shape[1] for s in shards], target)
    order = []
    for a in range(len(shards)):
        mine = [ch for ch in chunks if ch[0] == a]
        part = PARTS[(a - 1) % len(PARTS)] if a else None
        if part == "wg":
            both = [ch for ch in chunks if ch[0] == a + 1]
            mine = [ch for pair in zip(mine, both) for ch in pair]
        elif part == "wu":
            mine = []
        order += mine
    N, ends, sides = len(order), max(Z - 1, 1), max(X, Y, 2) - 1
    tok = lambda w, t=bf16: jax.ShapeDtypeStruct((rows, w), t)
    saved = dict(
        n1=tok(width), q=tok(wide), k=tok(wide), v=tok(wide), o=tok(wide), stats=tok(128, f32),
        h1=tok(width, f32), n2=tok(width), cp=tok(width), z=tok(ff),
        wkv=jax.ShapeDtypeStruct((2 * GROUPS, LAT, half), bf16), a=tok(ff, f32), b=tok(ff, f32), h=tok(width, f32),
    )
    names = SAVED + ("a", "b", "h")
    tree = rows // trees
    out_shape = [tok(width, f32), jax.ShapeDtypeStruct((trees, tree, tree), f32), jax.ShapeDtypeStruct((8, width), f32)]
    out_shape += [jax.ShapeDtypeStruct((Z, Y, X, 2) + s.shape, s.dtype) for s in shards]
    out_shape += [saved[name] for layer in range(LAYERS) for name in names]
    vmem = lambda s: pltpu.VMEM(s.shape, s.dtype)
    down = max(hi - lo for a, lo, mid, hi in order)
    got = pl.pallas_call(
        functools.partial(forward_kernel, n, order),
        out_shape=out_shape,
        in_specs=[SM, SM, VM] + [ANY] * len(shards),
        out_specs=[ANY, VM, VM] + [ANY] * (len(out_shape) - 3),
        scratch_shapes=[vmem(saved[name]) for name in SAVED]
        + [
            pltpu.VMEM((rows, width), f32),
            pltpu.VMEM((rows, lat), bf16),
            pltpu.VMEM((2, 2, rows, 256), f32),
            pltpu.VMEM((2 * GROUPS, LAT, width), bf16),
            pltpu.VMEM((width, 128), bf16),
            pltpu.VMEM((8, width), f32),
            pltpu.VMEM((width, wide), bf16),
            pltpu.VMEM((width, lat), bf16),
            pltpu.VMEM((width, half), bf16),
            pltpu.VMEM((width, wide), bf16),
            pltpu.VMEM((2, 2, width, 256), bf16),
            pltpu.VMEM((2, width, down), bf16),
        ]
        + [DMA((N,)), DMA((N, ends)), DMA((N, ends))]
        + [DMA((N, 2, sides))] * 4
        + [DMA((N,)), DMA((N,))]
        + [DMA((3,)), DMA((len(SAVED) + 1,)), DMA((2, 2)), DMA((2, 2)), DMA((2,))],
        compiler_params=pltpu.CompilerParams(
            collective_id=cid, has_side_effects=True, vmem_limit_bytes=63 << 20
        ),
    )(parents, lengths, tokens, *shards)
    final, bias, gains = got[:3]
    gathered = [g.reshape(n * s.shape[0], s.shape[1]) for g, s in zip(got[3:], shards)]
    rest = got[3 + len(shards) :]
    kept = [dict(zip(names, rest[i * len(names) : (i + 1) * len(names)])) for i in range(LAYERS)]
    weights = []
    for layer in range(LAYERS):
        q, l, kv, o, g, u, d = gathered[1 + layer * len(PARTS) : 1 + (layer + 1) * len(PARTS)]
        weights.append((q, l, kept[layer]["wkv"], o, g, u, d))
    return final, bias, gains, kept, weights


def body(inputs, cotangent, parents, lengths, g1, wq, wl, wk, wv, wo, g2, wg, wu, wd, *, n):
    trees, tree, width = inputs.shape
    rows = wq.shape[1]
    latr = wk.shape[2]

    def packed(layer):
        cast = lambda w: w[layer].astype(bf16)
        kv = jnp.stack([wk[layer], wv[layer]]).astype(bf16).reshape(-1, wk.shape[3])
        return [cast(wq), cast(wl), kv, cast(wo).T, cast(wg), cast(wu), cast(wd).T]

    gain_rows = jnp.stack([g1[0], g2[0], g1[1], g2[1]], axis=1).astype(bf16)
    gain_rows = jnp.pad(gain_rows, ((0, 0), (0, 128 - 2 * LAYERS)))
    shards = [gain_rows] + packed(0) + packed(1)
    out, bias, gains, kept, weights = forward(
        n, inputs.reshape(trees * tree, width), parents, lengths, trees, shards, 576, 0
    )
    outputs = out.reshape(inputs.shape)
    cot = cotangent.reshape(trees * tree, width)
    grad, summed = backward(n, cot, gains, bias, kept, weights, 576, 1)
    out = []
    for layer in range(LAYERS):
        dd, dg, du, do, dq, dl, kv = summed[(1 - layer) * 7 : (1 - layer) * 7 + 7]
        kv = kv.reshape(2, GROUPS, latr, -1)
        gain = summed[14]
        out.append(
            (gain[:, 2 * layer], dq, dl, kv[0], kv[1], do.T, gain[:, 2 * layer + 1], dg, du, dd.T)
        )
    stacked = tuple(jnp.stack([out[layer][slot] for layer in range(LAYERS)]) for slot in range(10))
    return (outputs, grad.reshape(inputs.shape)) + stacked


def solution(mesh):
    n = mesh.shape["fsdp"]
    by_one, by_two = P(None, "fsdp"), P(None, "fsdp", None)
    by_lat, by_last = P(None, None, "fsdp", None), P(None, None, "fsdp")
    params = (by_one, by_two, by_two, by_lat, by_lat, by_last, by_one, by_two, by_two, by_last)
    trees = P("fsdp", None, None)
    return jax.shard_map(
        functools.partial(body, n=n),
        mesh=mesh,
        in_specs=(trees, trees, P("fsdp", None), P("fsdp", None)) + params,
        out_specs=(trees, trees) + params,
        check_vma=False,
    )
```

```python
import functools
import math

import jax
import jax.numpy as jnp
from jax import lax
from jax.experimental import pallas as pl
from jax.experimental.pallas import tpu as pltpu
from jax.sharding import PartitionSpec as P

HEADS = 16
HD = 64
GROUPS = 2
LAT = 256
LAYERS = 2
LAG = 2
RING = 16
KZ = 3 * LAG + 2
epsilon = 1e-05

MESH = pl.DeviceIdType.MESH
ANY = pl.BlockSpec(memory_space=pltpu.HBM)
DMA = pltpu.SemaphoreType.DMA
bf16 = jnp.bfloat16
f32 = jnp.float32


def dims_of(n):
    chips = n // 2
    side = 1
    if chips & (chips - 1) == 0:
        side = 2 ** ((chips.bit_length() - 1) // 3)
    return chips // (side * side), side, side


def index(n, z, y, x, c):
    Z, Y, X = dims_of(n)
    return ((z * Y + y) * X + x) * 2 + c


def place(n):
    Z, Y, X = dims_of(n)
    me = lax.axis_index("fsdp")
    return me // (2 * X * Y), lax.rem(me // (2 * X), Y), lax.rem(me // 2, X), lax.rem(me, 2)


def greet(n, z, y, x, c):
    Z, Y, X = dims_of(n)
    peers = [index(n, lax.rem(z + o, Z), y, x, c) for o in range(1, Z)]
    peers += [index(n, z, lax.rem(y + o, Y), x, c) for o in range(1, Y)]
    peers += [index(n, z, y, lax.rem(x + o, X), c) for o in range(1, X)]
    peers += [index(n, z, y, x, 1 - c)]
    bar = pltpu.get_barrier_semaphore()
    for peer in peers:
        pl.semaphore_signal(bar, inc=1, device_id=(peer,), device_id_type=MESH)
    pl.semaphore_wait(bar, len(peers))


def remote(src, dst, send, recv, device):
    copy = describe(src, dst, send, recv, device)
    copy.start()
    return copy


def cut(widths, target):
    out = []
    for a, w in enumerate(widths):
        k, u = max(1, round(w / target)), w // 128
        edges = [round(j * u / k) for j in range(k + 1)]
        for lo, hi in zip(edges, edges[1:]):
            size = hi - lo
            inner = max(1, round(size / 6)) if size > 1 else 0
            outer = size - 2 * inner
            left = outer // 2 if len(out) % 2 else (outer + 1) // 2
            out.append((a,) + tuple(128 * e for e in (lo, lo + left, lo + left + inner, hi - (outer - left), hi)))
    return out


def relays(Z):
    return Z == 4


class Sometimes:
    def __init__(self, copy, sends, receives):
        self.copy, self.sends, self.receives = copy, sends, receives
        pl.when(sends)(copy.start)

    def wait(self):
        pl.when(self.sends)(self.copy.wait_send)
        pl.when(self.receives)(self.copy.wait_recv)


def describe(src, dst, send, recv, device):
    return pltpu.make_async_remote_copy(
        src_ref=src, dst_ref=dst, send_sem=send, recv_sem=recv, device_id=(device,), device_id_type=MESH
    )


NT = (((1,), (1,)), ((), ()))
TN = (((0,), (0,)), ((), ()))


def dot(a, b):
    return jnp.dot(a, b, preferred_element_type=f32)


def dot_nt(a, b):
    return lax.dot_general(a, b, NT, preferred_element_type=f32)


def dot_tn(a, b):
    return lax.dot_general(a, b, TN, preferred_element_type=f32)


def tiles(size, tile):
    def run(body):
        def step(j, carry):
            body(pl.ds(pl.multiple_of(j * tile, tile), tile))
            return carry

        lax.fori_loop(0, size // tile, step, 0)

    return run


def build_bias(parents, lengths, bias):
    trees, tree = bias.shape[0], bias.shape[1]
    count = parents.shape[1]
    key = lax.broadcasted_iota(jnp.int32, (1, tree), 1)
    row = lax.broadcasted_iota(jnp.int32, (tree, 1), 0)
    for t in range(trees):
        start = jnp.int32(0)
        reach, total = [], jnp.zeros((tree, tree), f32)
        for s in range(count):
            end = start + lengths[t, s]
            line = jnp.where((key >= start) & (key < end), 1.0, 0.0)
            for u in range(s):
                line = line + jnp.where(parents[t, s] == u, reach[u], 0.0)
            reach.append(line)
            total = total + jnp.where((row >= start) & (row < end), 1.0, 0.0) * line
            start = end
        seen = (total > 0.5) & (key <= row)
        bias[t] = jnp.where(seen, 0.0, -1e30)


def norm_to(dst, src, gain, rows=64):
    @tiles(src.shape[0], rows)
    def _(at):
        h = src[at, :]
        r = lax.rsqrt(jnp.mean(h * h, axis=-1, keepdims=True) + epsilon)
        dst[at, :] = (h * r * gain).astype(bf16)


def attention_forward_step(q, k, v, bias, o, stats):
    trees, tree = bias.shape[0], bias.shape[1]
    pairs = q.shape[1] // 128
    scale = 1.0 / math.sqrt(HD)
    lane = lax.broadcasted_iota(jnp.int32, (tree, 128), 1)

    def step(j):
        t, pair = j // pairs, lax.rem(j, pairs)
        rows = pl.ds(pl.multiple_of(t * tree, tree), tree)
        cols = pl.ds(pl.multiple_of(pair * 128, 128), 128)
        q2, k2, v2 = q[rows, cols], k[rows, cols], v[rows, cols]
        mixed, log_total = [], stats[rows, :]
        for half in range(2):
            mine = (lane >= HD) if half else (lane < HD)
            s = dot_nt(jnp.where(mine, q2 * jnp.asarray(scale, bf16), jnp.zeros_like(q2)), k2) + bias[t]
            top = jnp.max(s, axis=-1, keepdims=True)
            e = jnp.exp(s - top)
            total = jnp.sum(e, axis=-1, keepdims=True)
            p = (e * (1.0 / total)).astype(bf16)
            mixed.append(dot(p, v2))
            log_total = jnp.where(lane == pair * 2 + half, top + jnp.log(total), log_total)
        stats[rows, :] = log_total
        o[rows, cols] = jnp.where(lane < HD, mixed[0], mixed[1]).astype(bf16)

    return step


VM = pl.BlockSpec(memory_space=pltpu.VMEM)
SM = pl.BlockSpec(memory_space=pltpu.SMEM)


def norm_back_to(dst, carry_in, dn, h_ref, gain, gain_grad, low=None, rows=64):
    gain_grad[...] = jnp.zeros_like(gain_grad)

    @tiles(h_ref.shape[0], rows)
    def _(at):
        h, d = h_ref[at, :], dn[at, :]
        r = lax.rsqrt(jnp.mean(h * h, axis=-1, keepdims=True) + epsilon)
        gain_grad[...] += jnp.sum(d * h * r, axis=0, keepdims=True)
        weighted = d * gain
        inner = jnp.mean(weighted * h, axis=-1, keepdims=True)
        total = carry_in[at, :] + (r * weighted - h * (r * r * r) * inner)
        dst[at, :] = total
        if low is not None:
            low[at, :] = total.astype(bf16)


def attention_backward_step(q, k, v, do, bias, stats, dq, dk, dv):
    trees, tree = bias.shape[0], bias.shape[1]
    pairs = q.shape[1] // 128
    scale = 1.0 / math.sqrt(HD)
    lane = lax.broadcasted_iota(jnp.int32, (tree, 128), 1)

    def step(j):
        t, pair = j // pairs, lax.rem(j, pairs)
        rows = pl.ds(pl.multiple_of(t * tree, tree), tree)
        cols = pl.ds(pl.multiple_of(pair * 128, 128), 128)
        q2, k2, v2, do2 = q[rows, cols], k[rows, cols], v[rows, cols], do[rows, cols]
        logs = stats[rows, :]
        zero = jnp.zeros_like(q2)
        got = []
        for half in range(2):
            mine = (lane >= HD) if half else (lane < HD)
            log_total = jnp.sum(jnp.where(lane == pair * 2 + half, logs, 0.0), axis=-1, keepdims=True)
            s = dot_nt(jnp.where(mine, q2 * jnp.asarray(scale, bf16), zero), k2) + bias[t]
            p = jnp.exp(s - log_total)
            dp = dot_nt(jnp.where(mine, do2, zero), v2)
            inner = jnp.sum(p * dp, axis=-1, keepdims=True)
            ds = (p * (dp - inner)).astype(bf16)
            got.append((dot(ds, k2), dot_tn(ds, q2), dot_tn(p.astype(bf16), do2)))
        low = lane < HD
        dq[rows, cols] = (jnp.where(low, got[0][0], got[1][0]) * scale).astype(bf16)
        dk[rows, cols] = (jnp.where(low, got[0][1], got[1][1]) * scale).astype(bf16)
        dv[rows, cols] = jnp.where(low, got[0][2], got[1][2]).astype(bf16)

    return step


def plus(*terms):
    if len(terms) < 3:
        return sum(terms[1:], terms[0])
    return sum((t.astype(f32) for t in terms[1:]), terms[0].astype(f32)).astype(bf16)


class Scatter:
    def __init__(self, n, chunks, jobs, K, outs, bufs, sems, gain_rows):
        self.n, self.chunks, self.jobs, self.K, self.outs = n, chunks, jobs, K, outs
        self.LB, self.RB, self.G, self.R0, self.P1, self.R1, self.P2, self.R2, self.RZ, self.R3, self.P3, self.R4 = bufs
        self.lsem, self.ls, self.cs, self.cr, self.ss, self.sr, self.zs, self.zr = sems
        self.gain_rows = gain_rows
        self.ready = set()
        self.stages = [self.from_partner, self.second, self.third, self.fourth, self.fifth, self.finish]
        self.held = [None] * len(chunks)
        self.at = 0
        self.started = False
        turns, last = [], None
        for a, *_ in chunks:
            left = jobs[a]["left"]
            if left is not last and left is not None:
                turns.append(a)
                last = left
            turns_now = len(turns) - 1
            self.turn = getattr(self, "turn", []) + [turns_now]
        self.turns = turns

    def left_copy(self, t):
        return pltpu.make_async_copy(self.jobs[self.turns[t]]["left"], self.LB.at[t % 2], self.lsem.at[t % 2])

    def first_of(self, i):
        return self.jobs[self.chunks[i][0]]["left"] is not None and (i == 0 or self.turn[i] != self.turn[i - 1])

    def right_copy(self, i, which=0):
        a, lo, e1, e2, e3, hi = self.chunks[i]
        return pltpu.make_async_copy(
            self.jobs[a]["right"][which].at[:, lo:hi], self.RB.at[i % 2, :, 0 : hi - lo], self.ls.at[i % 2]
        )

    def fetch(self, i):
        if self.first_of(i):
            self.left_copy(self.turn[i]).start()
        if self.jobs[self.chunks[i][0]]["left"] is not None:
            self.right_copy(i).start()

    def has(self, i):
        return i >= len(self.chunks) or all(w in self.ready for w in self.jobs[self.chunks[i][0]]["needs"])

    def slot(self, times=1):
        for _ in range(times):
            i = self.at
            if i < len(self.chunks) and not (self.has(i) and self.has(i + 1)):
                return
            if not self.started:
                self.fetch(0)
                self.started = True
            last = len(self.stages) - 1
            if i >= len(self.chunks) + LAG * last:
                return
            for s in range(last, -1, -1):
                j = i - LAG * s
                if 0 <= j < len(self.chunks):
                    if s > 0:
                        for copy in self.held[j]:
                            copy.wait()
                    self.held[j] = self.stages[s](j)
            self.at += 1

    def drain(self):
        while self.at < len(self.chunks) + LAG * (len(self.stages) - 1):
            before = self.at
            self.slot()
            assert self.at > before

    def from_partner(self, i):
        Z, Y, X = dims_of(self.n)
        z, y, x, c = place(self.n)
        a, lo, e1, e2, e3, hi = self.chunks[i]
        k, w = i % self.K, hi - lo
        G, LB, RB = self.G, self.LB, self.RB
        rows = G.shape[6 - 1]
        job = self.jobs[a]
        t = self.turn[i]
        depth = LB.shape[2] // Z
        if job["left"] is not None:
            if self.first_of(i):
                self.left_copy(t).wait()
            self.right_copy(i).wait()
        if i + 1 < len(self.chunks):
            self.fetch(i + 1)
        if job["left"] is None:
            lines = self.gain_rows[...].astype(bf16)
            pick = lax.broadcasted_iota(jnp.int32, (lines.shape[0], w), 0)
            pick = (pick == lax.broadcasted_iota(jnp.int32, (lines.shape[0], w), 1)).astype(bf16)
            for zz in range(Z):
                part = dot_tn(lines[:, zz * depth : (zz + 1) * depth], pick)
                G[k, zz, :, :, :, :, 0:w] = part.astype(bf16).reshape(Y, X, 2, rows, w)
        elif len(job["right"]) == 1:

            step = 2 if Z % 2 == 0 else 1

            def block(zz):
                part = dot_tn(LB[t % 2, :, span(zz, step * depth)], RB[i % 2, :, 0:w])
                G[k, pl.ds(zz * step, step), :, :, :, :, 0:w] = part.astype(bf16).reshape(step, Y, X, 2, rows, w)

            loop(0, Z // step, block)
        else:
            quarter = rows // 4
            group = lax.broadcasted_iota(jnp.int32, (rows, w), 0) >> (quarter.bit_length() - 1)
            for which in range(4):
                if which:
                    copy = self.right_copy(i, which)
                    copy.start()
                    copy.wait()

                def block(zz, carry):
                    at = pl.ds(pl.multiple_of(zz * depth, depth), depth)
                    part = dot_tn(LB[t % 2, :, at], RB[i % 2, :, 0:w]).reshape(Y, X, 2, rows, w)
                    if which:
                        part = jnp.where(group == which, part, G[k, zz, :, :, :, :, 0:w].astype(f32))
                    G[k, zz, :, :, :, :, 0:w] = part.astype(bf16)
                    return carry

                lax.fori_loop(0, Z, block, 0)
        copy = remote(
            G.at[k, :, :, :, 1 - c, :, 0:w],
            self.R0.at[k, :, :, :, :, 0:w],
            self.cs.at[k],
            self.cr.at[k],
            index(self.n, z, y, x, 1 - c),
        )
        return [copy]

    def along(self, axis, i, flow, src, dst):
        n, k = self.n, i % self.K
        Z, Y, X = dims_of(n)
        z, y, x, c = place(n)
        copies = []
        for o in range(1, X if axis == "x" else Y):
            p = lax.rem(x + o, X) if axis == "x" else lax.rem(y + o, Y)
            to = index(n, z, y, p, c) if axis == "x" else index(n, z, p, x, c)
            copies.append(remote(src(p), dst(o - 1), self.ss.at[k, flow, o - 1], self.sr.at[k, flow, o - 1], to))
        return copies

    def along_z(self, i, flow, src, dst):
        n, k = self.n, i % KZ
        Z, Y, X = dims_of(n)
        z, y, x, c = place(n)
        copies = []
        for o in range(1, Z):
            p = lax.rem(z + o, Z)
            to = index(n, p, y, x, c)
            sems = self.zs.at[k, flow, o - 1], self.zr.at[k, flow, o - 1]
            if not relays(Z):
                copies.append(remote(src(p), dst(o - 1), *sems, to))
            elif o == 2:
                direct = describe(src(p), dst(o - 1), *sems, to)
                copies.append(Sometimes(direct, (z == 0) | (z == 3), (z == 1) | (z == 2)))
            else:
                ends = (3, 0) if o == 1 else (0, 3)
                copies.append(Sometimes(describe(src(p), dst(o - 1), *sems, to), z != ends[0], z != ends[1]))
        if relays(Z):
            for which, end, via in ((0, 3, 2), (1, 0, 1)):
                sems = self.zs.at[k, flow, Z - 1 + which], self.zr.at[k, flow, Z - 1 + which]
                relay = describe(src(3 - end), dst(Z - 1), *sems, index(n, via, y, x, c))
                copies.append(Sometimes(relay, z == end, z == via))
        return copies

    def relay_z(self, i, flow, src, dst, add):
        n, k = self.n, i % KZ
        Z, Y, X = dims_of(n)
        z, y, x, c = place(n)
        copies = []
        if relays(Z):
            for via, end in ((2, 0), (1, 3)):
                sems = self.zs.at[k, flow, 1], self.zr.at[k, flow, 1]
                pl.when(z == via)(functools.partial(add, end))
                copy = describe(src(end), dst(1), *sems, index(n, end, y, x, c))
                copies.append(Sometimes(copy, z == via, z == end))
        return copies

    def total_z(self, mine, got):
        Z, Y, X = dims_of(self.n)
        z, y, x, c = place(self.n)
        total = mine.astype(f32)
        for o in range(1, Z):
            term = got(o - 1).astype(f32)
            if relays(Z) and o != 2:
                term = jnp.where(z == (0 if o == 1 else 3), 0.0, term)
            total = total + term
        return total

    def second(self, i):
        G, R0, R1 = self.G, self.R0, self.R1
        Z, Y, X = dims_of(self.n)
        z, y, x, c = place(self.n)
        a, lo, e1, e2, e3, hi = self.chunks[i]
        k, w, h = i % self.K, hi - lo, e2 - lo

        def add(zz):
            G[k, zz, :, :, c, :, 0:w] = plus(G[k, zz, :, :, c, :, 0:w], R0[k, zz, :, :, :, 0:w])

        loop(0, Z, add)
        copies = []
        if h > 0:
            copies += self.along(
                "y", i, 0, lambda p: G.at[k, :, p, :, c, :, 0:h], lambda o: R1.at[k, o, :, 0:X, :, 0:h]
            )
        if w > h:
            copies += self.along(
                "x", i, 1, lambda p: G.at[k, :, :, p, c, :, h:w], lambda o: R1.at[k, o, :, 0:Y, :, h:w]
            )
        return copies

    def third(self, i):
        G, P1, R1, R2, RZ = self.G, self.P1, self.R1, self.R2, self.RZ
        Z, Y, X = dims_of(self.n)
        z, y, x, c = place(self.n)
        a, lo, e1, e2, e3, hi = self.chunks[i]
        k, kz, w, h = i % self.K, i % KZ, hi - lo, e2 - lo
        if h > 0:
            others = [R1[k, o, :, 0:X, :, 0:h] for o in range(Y - 1)]
            P1[k, :, 0:X, :, 0:h] = plus(G[k, :, y, :, c, :, 0:h], *others)
        if w > h:
            others = [R1[k, o, :, 0:Y, :, h:w] for o in range(X - 1)]
            P1[k, :, 0:Y, :, h:w] = plus(G[k, :, :, x, c, :, h:w], *others)
        f1, f3 = e1 - lo, e3 - lo
        copies = []
        if h > f1:
            copies += self.along("x", i, 2, lambda p: P1.at[k, :, p, :, f1:h], lambda o: R2.at[k, o, :, :, f1:h])
        if f3 > h:
            copies += self.along("y", i, 3, lambda p: P1.at[k, :, p, :, h:f3], lambda o: R2.at[k, o, :, :, h:f3])
        if f1 > 0:
            copies += self.along_z(
                i, 0, lambda p: P1.at[k, p, 0:X, :, 0:f1], lambda o: RZ.at[kz, o, 0:X, :, 0:f1]
            )
        if w > f3:
            copies += self.along_z(
                i, 1, lambda p: P1.at[k, p, 0:Y, :, f3:w], lambda o: RZ.at[kz, o, 0:Y, :, f3:w]
            )
        return copies

    def fourth(self, i):
        P1, P2, R2, RZ, R3 = self.P1, self.P2, self.R2, self.RZ, self.R3
        Z, Y, X = dims_of(self.n)
        z, y, x, c = place(self.n)
        a, lo, e1, e2, e3, hi = self.chunks[i]
        k, kz, w, h, f1, f3 = i % self.K, i % KZ, hi - lo, e2 - lo, e1 - lo, e3 - lo
        copies = []
        for start, end, size, flow in ((0, f1, X, 0), (f3, w, Y, 1)):
            if end > start:
                src = lambda p: P1.at[k, p, 0:size, :, start:end]
                dst = lambda o: RZ.at[kz, o, 0:size, :, start:end]

                def add(p):
                    P1[k, p, 0:size, :, start:end] = plus(
                        P1[k, p, 0:size, :, start:end], RZ[kz, Z - 1, 0:size, :, start:end]
                    )

                copies += self.relay_z(i, flow, src, dst, add)
        if h > f1:
            P2[k, :, :, f1:h] = plus(P1[k, :, x, :, f1:h], *[R2[k, o, :, :, f1:h] for o in range(X - 1)])
        if f3 > h:
            P2[k, :, :, h:f3] = plus(P1[k, :, y, :, h:f3], *[R2[k, o, :, :, h:f3] for o in range(Y - 1)])
        if f3 > f1:
            copies += self.along_z(i, 2, lambda p: P2.at[k, p, :, f1:f3], lambda o: R3.at[kz, o, :, f1:f3])
        return copies

    def fifth(self, i):
        P1, P2, RZ, R3, P3, R4 = self.P1, self.P2, self.RZ, self.R3, self.P3, self.R4
        Z, Y, X = dims_of(self.n)
        z, y, x, c = place(self.n)
        a, lo, e1, e2, e3, hi = self.chunks[i]
        k, kz, w, f1, f3 = i % self.K, i % KZ, hi - lo, e1 - lo, e3 - lo
        copies = []
        if f3 > f1:

            def add(p):
                P2[k, p, :, f1:f3] = plus(P2[k, p, :, f1:f3], R3[kz, Z - 1, :, f1:f3])

            copies += self.relay_z(i, 2, lambda p: P2.at[k, p, :, f1:f3], lambda o: R3.at[kz, o, :, f1:f3], add)
        for start, end, size, axis, flow in ((0, f1, X, "x", 4), (f3, w, Y, "y", 5)):
            if end > start:
                total = self.total_z(
                    P1[k, z, 0:size, :, start:end], lambda o: RZ[kz, o, 0:size, :, start:end]
                )
                P3[k, 0:size, :, start:end] = total.astype(bf16)
                copies += self.along(
                    axis, i, flow, lambda p: P3.at[k, p, :, start:end], lambda o: R4.at[k, o, :, start:end]
                )
        return copies

    def finish(self, i):
        P2, R3, P3, R4 = self.P2, self.R3, self.P3, self.R4
        Z, Y, X = dims_of(self.n)
        z, y, x, c = place(self.n)
        a, lo, e1, e2, e3, hi = self.chunks[i]
        k, kz, w, f1, f3 = i % self.K, i % KZ, hi - lo, e1 - lo, e3 - lo
        if f3 > f1:
            self.outs[a][:, e1:e3] = self.total_z(P2[k, z, :, f1:f3], lambda o: R3[kz, o, :, f1:f3])
        for start, end, size, mine in ((0, f1, X, x), (f3, w, Y, y)):
            if end > start:
                total = P3[k, mine, :, start:end].astype(f32)
                for o in range(size - 1):
                    total = total + R4[k, o, :, start:end].astype(f32)
                self.outs[a][:, lo + start : lo + end] = total
        return []


def loop(lo, hi, body, unroll=1):
    def step(j, carry):
        body(j)
        return carry

    lax.fori_loop(lo, hi, step, 0, unroll=unroll)


def span(j, size):
    return pl.ds(pl.multiple_of(j * size, size), size)


KEPT = ("h", "n1", "q", "k", "v", "o", "stats", "h1", "n2", "a", "b", "z", "cp")
NAMES = ("wq", "wl", "wkv", "wo", "wg", "wu", "wd")
MADE = ("gf", "da", "db", "ga", "dq", "dk", "dv", "dc")


def backward_kernel(n, chunks, K, counts, *refs):
    it = iter(refs)
    take = lambda names: {name: next(it) for name in names}
    cot, gains, bias = next(it), next(it), next(it)
    kept = {layer: take(KEPT) for layer in reversed(range(LAYERS))}
    weights = {layer: take(NAMES) for layer in reversed(range(LAYERS))}
    grad_out = next(it)
    outs = [next(it) for _ in range(counts)]
    made = {layer: take(MADE) for layer in reversed(range(LAYERS))}
    bufs = [next(it) for _ in range(12)]
    gain_rows = next(it)
    v = take(("gf", "da", "db", "ga", "do", "q", "k", "v", "dq", "dk", "dv", "dc", "stats",
              "g", "h", "dm", "ab", "wd", "wgu", "wo", "wkv", "wq", "wl"))
    sems = [next(it) for _ in range(8)]
    insem, outsem, asem, wsem = [next(it) for _ in range(4)]

    jobs = []
    for layer in reversed(range(LAYERS)):
        s, m = kept[layer], made[layer]
        need = lambda *names: [(layer, name) for name in names]
        jobs += [
            {"left": m["gf"], "right": [s["z"]], "needs": need("gf")},
            {"left": s["n2"], "right": [m["da"]], "needs": need("da")},
            {"left": s["n2"], "right": [m["db"]], "needs": need("db")},
            {"left": m["ga"], "right": [s["o"]], "needs": need("ga")},
            {"left": s["n1"], "right": [m["dq"]], "needs": need("dq")},
            {"left": s["n1"], "right": [m["dc"]], "needs": need("dc")},
        ]
        half = m["dk"].shape[1] // GROUPS
        rights = [m[name].at[:, g * half : (g + 1) * half] for name in ("dk", "dv") for g in range(GROUPS)]
        jobs += [{"left": s["cp"], "right": rights, "needs": need("dk", "dv")}]
    jobs += [{"left": None, "right": None, "needs": [(0, "end")]}]
    scatter = Scatter(n, chunks, jobs, K, outs, bufs, sems, gain_rows)
    slot = scatter.slot

    ff, width = v["da"].shape[1], v["g"].shape[1]
    count = ff // 256
    tokens = v["g"].shape[0]
    gain_rows[...] = jnp.zeros_like(gain_rows)
    greeted = []

    for layer in reversed(range(LAYERS)):
        s, w, m = kept[layer], weights[layer], made[layer]
        first = layer == LAYERS - 1
        copies = {}

        def load(name, src, at):
            copies[name] = pltpu.make_async_copy(src, v[name], insem.at[at])
            copies[name].start()

        def tile_ab(j, which):
            src = s["ab"[which]]
            return pltpu.make_async_copy(src.at[:, span(j, 256)], v["ab"].at[which, lax.rem(j, 2)], asem.at[which, lax.rem(j, 2)])

        def tile_wd(j):
            return pltpu.make_async_copy(w["wd"].at[:, span(j, 256)], v["wd"].at[lax.rem(j, 2)], wsem.at[0, lax.rem(j, 2)])

        def tile_gu(j, which):
            src = w["wg"] if which == 0 else w["wu"]
            return pltpu.make_async_copy(src.at[span(j, 256), :], v["wgu"].at[which, j % 2], wsem.at[1 + which, j % 2])

        def publish(name):
            copy = pltpu.make_async_copy(v[name], m[name], outsem.at[MADE.index(name)])
            copy.start()
            return copy

        if first:
            load("g", cot, 0)
        tile_wd(0).start()
        tile_ab(0, 0).start()
        tile_ab(0, 1).start()
        load("h", s["h1"], 1)
        for at, name in enumerate(("q", "k", "v", "stats")):
            load(name, s[name], 2 + at)
        for at, name in enumerate(("wo", "wkv", "wq", "wl")):
            load(name, w[name], 6 + at)
        for j in range(2):
            tile_gu(j, 0).start()
            tile_gu(j, 1).start()
        if first:
            z, y, x, c = place(n)
            greet(n, z, y, x, c)
            copies["g"].wait()

        @tiles(tokens, 64)
        def _(at):
            v["gf"][at, :] = v["g"][at, :].astype(bf16)

        publish("gf").wait()
        scatter.ready.add((layer, "gf"))
        slot()

        def dz_step(j):
            at = span(j, 256)
            tile_wd(j).wait()
            tile_ab(j, 0).wait()
            tile_ab(j, 1).wait()

            @pl.when(j + 1 < count)
            def _():
                tile_wd(j + 1).start()
                tile_ab(j + 1, 0).start()
                tile_ab(j + 1, 1).start()

            dz = dot(v["gf"][...], v["wd"][lax.rem(j, 2)])
            a, b = v["ab"][0, lax.rem(j, 2)], v["ab"][1, lax.rem(j, 2)]
            sig = 1.0 / (1.0 + jnp.exp(-a))
            v["da"][:, at] = (dz * b * sig * (1.0 + a * (1.0 - sig))).astype(bf16)
            v["db"][:, at] = (dz * a * sig).astype(bf16)

        cuts = [0, count // 3, 2 * count // 3, count]
        for lo, hi in zip(cuts, cuts[1:]):
            loop(lo, hi, dz_step)
            slot(1 + (lo > 0 and hi < count))
        out_da, out_db = publish("da"), publish("db")
        for j in range(width // 256):
            tile_gu(j, 0).wait()
            tile_gu(j, 1).wait()
            at = slice(j * 256, (j + 1) * 256)
            v["dm"][:, at] = dot_nt(v["da"][...], v["wgu"][0, j % 2]) + dot_nt(v["db"][...], v["wgu"][1, j % 2])
            if j + 2 < width // 256:
                tile_gu(j + 2, 0).start()
                tile_gu(j + 2, 1).start()
            if j == 0:
                out_da.wait()
                out_db.wait()
                scatter.ready |= {(layer, "da"), (layer, "db")}
            slot()
        copies["h"].wait()
        norm_back_to(v["g"], v["g"], v["dm"], v["h"], gains[2 * layer + 1 : 2 * layer + 2, :],
                     gain_rows.at[2 * layer + 1 : 2 * layer + 2, :], low=v["ga"])
        copies["h"] = pltpu.make_async_copy(s["h"], v["h"], insem.at[1])
        copies["h"].start()
        out_ga = publish("ga")
        slot()
        copies["wo"].wait()

        @tiles(width, 512)
        def _(at):
            v["do"][:, at] = dot(v["ga"][...], v["wo"][:, at]).astype(bf16)

        out_ga.wait()
        scatter.ready.add((layer, "ga"))
        slot()
        for name in ("q", "k", "v", "stats"):
            copies[name].wait()
        pairs = bias.shape[0] * v["q"].shape[1] // 128
        step = attention_backward_step(v["q"], v["k"], v["v"], v["do"], bias, v["stats"], v["dq"], v["dk"], v["dv"])
        for part in range(4):
            loop(part * pairs // 4, (part + 1) * pairs // 4, step, 2)
            slot(2 - part % 2)
        out_q = [publish(name) for name in ("dq", "dk", "dv")]
        copies["wkv"].wait()
        half = v["wkv"].shape[2]
        for g in range(GROUPS):
            at = slice(g * half, (g + 1) * half)
            both = dot_nt(v["dk"][:, at], v["wkv"][g]) + dot_nt(v["dv"][:, at], v["wkv"][GROUPS + g])
            v["dc"][:, g * LAT : (g + 1) * LAT] = both.astype(bf16)
        for copy in out_q:
            copy.wait()
        scatter.ready |= {(layer, "dq"), (layer, "dk"), (layer, "dv")}
        out_dc = publish("dc")
        slot()
        copies["wq"].wait()
        copies["wl"].wait()

        @tiles(width, 512)
        def _(at):
            v["dm"][:, at] = dot_nt(v["dq"][...], v["wq"][at, :]) + dot_nt(v["dc"][...], v["wl"][at, :])

        out_dc.wait()
        scatter.ready.add((layer, "dc"))
        slot()
        copies["h"].wait()
        norm_back_to(v["g"], v["g"], v["dm"], v["h"], gains[2 * layer : 2 * layer + 1, :],
                     gain_rows.at[2 * layer : 2 * layer + 1, :])
        scatter.ready.add((layer, "end"))
        slot()
    last = pltpu.make_async_copy(v["g"], grad_out, insem.at[0])
    last.start()
    scatter.drain()
    last.wait()


def backward(n, cot, gains, bias, kept, weights, target, cid):
    Z, Y, X = dims_of(n)
    tokens, width = cot.shape
    rows = width // n
    ff = weights[0][4].shape[1]
    wide, lat = weights[0][0].shape[1], weights[0][1].shape[1]
    half = weights[0][2].shape[2]
    widths = [ff, ff, ff, wide, wide, lat, half] * LAYERS + [128]
    chunks = cut(widths, target)
    K = 2 * LAG + 1
    most = max(X, Y)
    sides, ends = max(most, 2) - 1, max(Z - 1, 1)
    most_wide = max(ch[5] - ch[1] for ch in chunks)
    ring = lambda *shape, deep=K: pltpu.VMEM((deep,) + shape + (rows, most_wide), bf16)
    tok = lambda w, t=bf16: pltpu.VMEM((tokens, w), t)
    made = dict(gf=width, da=ff, db=ff, ga=width, dq=wide, dk=wide, dv=wide, dc=lat)
    layers = list(reversed(range(LAYERS)))
    operands = [cot, gains, bias]
    for layer in layers:
        operands += [kept[layer][name] for name in KEPT]
    for layer in layers:
        operands += list(weights[layer])
    shapes = [jax.ShapeDtypeStruct((tokens, width), f32)]
    shapes += [jax.ShapeDtypeStruct((rows, w), f32) for w in widths]
    shapes += [jax.ShapeDtypeStruct((tokens, made[name]), bf16) for layer in layers for name in MADE]
    got = pl.pallas_call(
        functools.partial(backward_kernel, n, chunks, K, len(widths)),
        out_shape=shapes,
        in_specs=[ANY, VM, VM] + [ANY] * (len(operands) - 3),
        out_specs=[ANY] + [VM] * len(widths) + [ANY] * (LAYERS * len(MADE)),
        scratch_shapes=[
            pltpu.VMEM((2, tokens, width), bf16),
            pltpu.VMEM((2, tokens, most_wide), bf16),
            ring(Z, Y, X, 2),
            ring(Z, Y, X),
            ring(Z, most),
            ring(sides, Z, most),
            ring(Z),
            ring(sides, Z),
            ring(Z, most, deep=KZ),
            ring(Z, deep=KZ),
            ring(most),
            ring(sides),
            pltpu.VMEM((8, width), f32),
            tok(width), tok(ff), tok(ff), tok(width), tok(wide), tok(wide), tok(wide), tok(wide),
            tok(wide), tok(wide), tok(wide), tok(lat), tok(128, f32),
            tok(width, f32), tok(width, f32), tok(width, f32),
            pltpu.VMEM((2, 2, tokens, 256), f32),
            pltpu.VMEM((2, width, 256), bf16),
            pltpu.VMEM((2, 2, 256, ff), bf16),
        ]
        + [pltpu.VMEM(weights[0][i].shape, bf16) for i in (3, 2, 0, 1)]
        + [DMA((2,)), DMA((2,)), DMA((K,)), DMA((K,))]
        + [DMA((K, 6, sides))] * 2
        + [DMA((KZ, 3, ends + 2))] * 2
        + [DMA((10,)), DMA((len(MADE),)), DMA((2, 2)), DMA((3, 2))],
        compiler_params=pltpu.CompilerParams(
            collective_id=cid, has_side_effects=True, vmem_limit_bytes=67043328
        ),
    )(*operands)
    return got[0], got[1 : 1 + len(widths)]


class Gather:
    def __init__(self, n, chunks, ins, outs, sems):
        self.n, self.chunks, self.ins, self.outs = n, chunks, ins, outs
        self.own_sem, self.zs, self.zr, self.ss, self.sr, self.cs, self.cr = sems
        self.stages = [self.first, self.second, self.third, self.fourth, self.to_partner, lambda i: []]
        self.held = [None] * len(chunks)
        self.at = 0
        self.total = len(chunks) + LAG * (len(self.stages) - 1)

    def slot(self, times=1):
        for _ in range(times):
            if self.at >= self.total:
                return
            last = len(self.stages) - 1
            for s in range(last, -1, -1):
                j = self.at - LAG * s
                if 0 <= j < len(self.chunks):
                    if s > 0:
                        for copy in self.held[j]:
                            copy.wait()
                    self.held[j] = self.stages[s](j)
            self.at += 1

    def until(self, a, column):
        need = max(i for i, ch in enumerate(self.chunks) if ch[0] == a and ch[1] < column)
        while self.at < need + LAG * (len(self.stages) - 1) + 1:
            self.slot()

    def along(self, axis, i, flow, src, dst):
        n, k = self.n, i % RING
        Z, Y, X = dims_of(n)
        z, y, x, c = place(n)
        copies = []
        for o in range(1, X if axis == "x" else Y):
            to = index(n, z, y, lax.rem(x + o, X), c) if axis == "x" else index(n, z, lax.rem(y + o, Y), x, c)
            copies.append(remote(src, dst, self.ss.at[k, flow, o - 1], self.sr.at[k, flow, o - 1], to))
        return copies

    def along_z(self, i, flow, src, dst):
        n, k = self.n, i % RING
        Z, Y, X = dims_of(n)
        z, y, x, c = place(n)
        copies = []
        for o in range(1, Z):
            to = index(n, lax.rem(z + o, Z), y, x, c)
            sems = self.zs.at[k, flow, o - 1], self.zr.at[k, flow, o - 1]
            if relays(Z) and o != 2:
                ends = (Z - 1, 0) if o == 1 else (0, Z - 1)
                copies.append(Sometimes(describe(src, dst, *sems, to), z != ends[0], z != ends[1]))
            else:
                copies.append(remote(src, dst, *sems, to))
        return copies

    def relay_z(self, i, flow, part):
        n, k = self.n, i % RING
        Z, Y, X = dims_of(n)
        z, y, x, c = place(n)
        copies = []
        if relays(Z):
            for o, via, end in ((1, 1, 0), (3, 2, 3)):
                block = part(3 - end)
                sems = self.zs.at[k, flow, o - 1], self.zr.at[k, flow, o - 1]
                copies.append(Sometimes(describe(block, block, *sems, index(n, end, y, x, c)), z == via, z == end))
        return copies

    def views(self, i):
        z, y, x, c = place(self.n)
        a, lo, e1, e2, e3, hi = self.chunks[i]
        out = self.outs[a]
        inner = lambda zz: out.at[zz, y, x, c, :, e1:e3]
        left = lambda zz: out.at[zz, y, :, c, :, lo:e1]
        right = lambda zz: out.at[zz, :, x, c, :, e3:hi]
        return z, y, x, c, out, inner, left, right

    def first(self, i):
        z, y, x, c, out, inner, left, right = self.views(i)
        a, lo, e1, e2, e3, hi = self.chunks[i]
        src = self.ins[a]
        own = pltpu.make_async_copy(src.at[:, lo:hi], out.at[z, y, x, c, :, lo:hi], self.own_sem.at[i % RING])
        own.start()
        copies = [own]
        if e3 > e1:
            copies += self.along_z(i, 0, src.at[:, e1:e3], inner(z))
        if e1 > lo:
            copies += self.along("x", i, 0, src.at[:, lo:e1], out.at[z, y, x, c, :, lo:e1])
        if hi > e3:
            copies += self.along("y", i, 1, src.at[:, e3:hi], out.at[z, y, x, c, :, e3:hi])
        return copies

    def second(self, i):
        z, y, x, c, out, inner, left, right = self.views(i)
        a, lo, e1, e2, e3, hi = self.chunks[i]
        copies = self.relay_z(i, 0, inner) if e3 > e1 else []
        if e1 > lo:
            copies += self.along_z(i, 1, left(z), left(z))
        if hi > e3:
            copies += self.along_z(i, 2, right(z), right(z))
        return copies

    def third(self, i):
        z, y, x, c, out, inner, left, right = self.views(i)
        a, lo, e1, e2, e3, hi = self.chunks[i]
        copies = []
        if e1 > lo:
            copies += self.relay_z(i, 1, left)
        if hi > e3:
            copies += self.relay_z(i, 2, right)
        if e3 > e1:
            part = out.at[:, y, x, c, :, e1:e2]
            copies += self.along("x", i, 2, part, part)
            part = out.at[:, y, x, c, :, e2:e3]
            copies += self.along("y", i, 3, part, part)
        return copies

    def fourth(self, i):
        z, y, x, c, out, inner, left, right = self.views(i)
        a, lo, e1, e2, e3, hi = self.chunks[i]
        copies = []
        if e2 > lo:
            part = out.at[:, y, :, c, :, lo:e2]
            copies += self.along("y", i, 4, part, part)
        if hi > e2:
            part = out.at[:, :, x, c, :, e2:hi]
            copies += self.along("x", i, 5, part, part)
        return copies

    def to_partner(self, i):
        z, y, x, c, out, inner, left, right = self.views(i)
        a, lo, e1, e2, e3, hi = self.chunks[i]
        part = out.at[:, :, :, c, :, lo:hi]
        return [remote(part, part, self.cs.at[i % RING], self.cr.at[i % RING], index(self.n, z, y, x, 1 - c))]


SAVED = ("n1", "q", "k", "v", "o", "stats", "h1", "n2", "cp", "z", "wkv")
PARTS = ("wq", "wl", "kv", "wo", "wg", "wu", "wd")


def fill_picks(n, picks):
    which, lat, width = picks.shape
    quarter = width // n // which
    bits = quarter.bit_length() - 1
    row = lax.broadcasted_iota(jnp.int32, (lat, width), 0)
    col = lax.broadcasted_iota(jnp.int32, (lat, width), 1)
    base = ((row >> bits) * (which * quarter)) + (row & (quarter - 1))
    for i in range(which):
        picks[i] = jnp.where(col == base + i * quarter, 1.0, 0.0).astype(bf16)


def forward_kernel(n, chunks, *refs):
    it = iter(refs)
    take = lambda names: {name: next(it) for name in names}
    parents, lengths, tokens_ref, gain_in = [next(it) for _ in range(4)]
    count = 1 + LAYERS * len(PARTS)
    ins = [gain_in] + [next(it) for _ in range(count - 1)]
    final, bias, gains_out = next(it), next(it), next(it)
    outs = [next(it) for _ in range(count)]
    kept = [take(SAVED + ("a", "b", "h")) for _ in range(LAYERS)]
    v = take(SAVED + ("h", "c", "ab", "picks", "gr", "gt", "wq", "wl", "kv", "wo", "wgu", "wd"))
    gather = Gather(n, chunks, ins, outs, [next(it) for _ in range(7)])
    insem, savesem, absem, gusem, wdsem = [next(it) for _ in range(5)]
    slot = gather.slot
    z, y, x, c = place(n)
    greet(n, z, y, x, c)
    slot(3)

    def rows_of(a):
        return outs[a].reshape(outs[a].shape[0] * outs[a].shape[1] * outs[a].shape[2] * 2 * outs[a].shape[4], outs[a].shape[5])

    gathered = [rows_of(a) for a in range(count)]

    def load(a, name, at):
        gather.until(a, outs[a].shape[5])
        copy = pltpu.make_async_copy(gathered[a], v[name], insem.at[at])
        copy.start()
        return copy

    @tiles(tokens_ref.shape[0], 64)
    def _(at):
        v["h"][at, :] = tokens_ref[at, :].astype(f32)

    build_bias(parents, lengths, bias)
    slot()
    fill_picks(n, v["picks"])
    slot()
    copy = load(0, "gr", 0)
    copy.wait()
    lines = lax.broadcasted_iota(jnp.int32, (8, 128), 0) == lax.broadcasted_iota(jnp.int32, (8, 128), 1)
    v["gt"][...] = dot_nt(lines.astype(bf16), v["gr"][...])
    gains_out[...] = v["gt"][...]
    gains = v["gt"]

    for layer in range(LAYERS):
        s = kept[layer]
        base = 1 + layer * len(PARTS)
        saves = []

        def save(name, src=None):
            copy = pltpu.make_async_copy(v[src or name], s[name], savesem.at[len(saves)])
            copy.start()
            saves.append(copy)

        h, n1, n2, h1 = v["h"], v["n1"], v["n2"], v["h1"]
        save("h")
        norm_to(n1, h, gains[2 * layer : 2 * layer + 1, :])
        save("n1")
        slot()
        load(base, "wq", 0).wait()
        wl_copy = load(base + 1, "wl", 1)

        @tiles(v["wq"].shape[1], 512)
        def _(at):
            v["q"][:, at] = dot(n1[...], v["wq"][:, at]).astype(bf16)

        save("q")
        slot()
        wl_copy.wait()
        kv_copy = load(base + 2, "kv", 2)
        v["c"][...] = dot(n1[...], v["wl"][...]).astype(bf16)
        spread = dot(v["c"][:, 0:LAT], v["picks"][0] + v["picks"][GROUPS])
        for g in range(1, GROUPS):
            spread += dot(v["c"][:, g * LAT : (g + 1) * LAT], v["picks"][g] + v["picks"][GROUPS + g])
        v["cp"][...] = spread.astype(bf16)
        save("cp")
        kv_copy.wait()
        half = v["kv"].shape[1]
        for i in range(2 * GROUPS):
            v["wkv"][i] = dot(v["picks"][i], v["kv"][...]).astype(bf16)
        save("wkv")
        slot()
        for g in range(GROUPS):
            cg = v["c"][:, g * LAT : (g + 1) * LAT]
            v["k"][:, g * half : (g + 1) * half] = dot(cg, v["wkv"][g]).astype(bf16)
            v["v"][:, g * half : (g + 1) * half] = dot(cg, v["wkv"][GROUPS + g]).astype(bf16)
        save("k")
        save("v")
        slot()
        v["stats"][...] = jnp.zeros_like(v["stats"])
        pairs = bias.shape[0] * v["q"].shape[1] // 128
        step = attention_forward_step(v["q"], v["k"], v["v"], bias, v["o"], v["stats"])
        for part in range(4):
            loop(part * pairs // 4, (part + 1) * pairs // 4, step, 2)
            slot()
        save("o")
        save("stats")
        load(base + 3, "wo", 0).wait()

        @tiles(v["wo"].shape[0], 512)
        def _(at):
            h1[:, at] = h[:, at] + dot_nt(v["o"][...], v["wo"][at, :])

        save("h1")
        slot()
        norm_to(n2, h1, gains[2 * layer + 1 : 2 * layer + 2, :])
        save("n2")
        ff = v["z"].shape[1]
        steps = ff // 256

        def tile_gu(j, which):
            src = gathered[base + 4 + which]
            return pltpu.make_async_copy(src.at[:, span(j, 256)], v["wgu"].at[which, lax.rem(j, 2)], gusem.at[which, lax.rem(j, 2)])

        def put(j, which):
            dst = s["ab"[which]]
            return pltpu.make_async_copy(v["ab"].at[which, lax.rem(j, 2)], dst.at[:, span(j, 256)], absem.at[which, lax.rem(j, 2)])

        cuts = [i * steps // 5 for i in range(6)]
        for lo, hi in zip(cuts, cuts[1:]):
            gather.until(base + 4, hi * 256)
            gather.until(base + 5, hi * 256)
            tile_gu(lo, 0).start()
            tile_gu(lo, 1).start()

            def gate_step(j):
                at = span(j, 256)
                tile_gu(j, 0).wait()
                tile_gu(j, 1).wait()

                @pl.when(j + 1 < hi)
                def _():
                    tile_gu(j + 1, 0).start()
                    tile_gu(j + 1, 1).start()

                @pl.when(j >= 2)
                def _():
                    put(j - 2, 0).wait()
                    put(j - 2, 1).wait()

                a = dot(n2[...], v["wgu"][0, lax.rem(j, 2)])
                b = dot(n2[...], v["wgu"][1, lax.rem(j, 2)])
                v["ab"][0, lax.rem(j, 2)] = a
                v["ab"][1, lax.rem(j, 2)] = b
                put(j, 0).start()
                put(j, 1).start()
                v["z"][:, at] = (a / (1.0 + jnp.exp(-a)) * b).astype(bf16)

            loop(lo, hi, gate_step)
            slot()
        save("z")
        for copy in saves:
            copy.wait()
        for j in (steps - 2, steps - 1):
            put(j, 0).wait()
            put(j, 1).wait()
        downs = [(ch[1], ch[5]) for ch in chunks if ch[0] == base + 6]

        def tile_wd(i):
            lo, hi = downs[i]
            gather.until(base + 6, hi)
            copy = pltpu.make_async_copy(gathered[base + 6].at[:, lo:hi], v["wd"].at[i % 2, :, 0 : hi - lo], wdsem.at[i % 2])
            copy.start()
            return copy

        coming = tile_wd(0)
        for i, (lo, hi) in enumerate(downs):
            coming.wait()
            if i + 1 < len(downs):
                coming = tile_wd(i + 1)

            @tiles(h.shape[1], 512)
            def _(at):
                add = dot_nt(v["z"][:, lo:hi], v["wd"][i % 2, at, 0 : hi - lo])
                h[:, at] = (h1[:, at] if i == 0 else h[:, at]) + add

            slot()
    last = pltpu.make_async_copy(v["h"], final, insem.at[0])
    last.start()
    slot(gather.total)
    last.wait()


def forward(n, tokens, parents, lengths, trees, shards, target, cid):
    Z, Y, X = dims_of(n)
    rows, width = tokens.shape
    shapes = {name: shards[1 + i].shape for i, name in enumerate(PARTS)}
    wide, lat, half, ff = shapes["wq"][1], shapes["wl"][1], shapes["kv"][1], shapes["wg"][1]
    chunks = cut([s.shape[1] for s in shards], target)
    order = []
    for a in range(len(shards)):
        mine = [ch for ch in chunks if ch[0] == a]
        part = PARTS[(a - 1) % len(PARTS)] if a else None
        if part == "wg":
            both = [ch for ch in chunks if ch[0] == a + 1]
            mine = [ch for pair in zip(mine, both) for ch in pair]
        elif part == "wu":
            mine = []
        order += mine
    ends, sides = max(Z - 1, 1), max(X, Y, 2) - 1
    tok = lambda w, t=bf16: jax.ShapeDtypeStruct((rows, w), t)
    saved = dict(
        n1=tok(width), q=tok(wide), k=tok(wide), v=tok(wide), o=tok(wide), stats=tok(128, f32),
        h1=tok(width, f32), n2=tok(width), cp=tok(width), z=tok(ff),
        wkv=jax.ShapeDtypeStruct((2 * GROUPS, LAT, half), bf16), a=tok(ff, f32), b=tok(ff, f32), h=tok(width, f32),
    )
    names = SAVED + ("a", "b", "h")
    tree = rows // trees
    out_shape = [tok(width, f32), jax.ShapeDtypeStruct((trees, tree, tree), f32), jax.ShapeDtypeStruct((8, width), f32)]
    out_shape += [jax.ShapeDtypeStruct((Z, Y, X, 2) + s.shape, s.dtype) for s in shards]
    out_shape += [saved[name] for layer in range(LAYERS) for name in names]
    vmem = lambda s: pltpu.VMEM(s.shape, s.dtype)
    down = max(ch[5] - ch[1] for ch in order)
    got = pl.pallas_call(
        functools.partial(forward_kernel, n, order),
        out_shape=out_shape,
        in_specs=[SM, SM, VM] + [ANY] * len(shards),
        out_specs=[ANY, VM, VM] + [ANY] * (len(out_shape) - 3),
        scratch_shapes=[vmem(saved[name]) for name in SAVED]
        + [
            pltpu.VMEM((rows, width), f32),
            pltpu.VMEM((rows, lat), bf16),
            pltpu.VMEM((2, 2, rows, 256), f32),
            pltpu.VMEM((2 * GROUPS, LAT, width), bf16),
            pltpu.VMEM((width, 128), bf16),
            pltpu.VMEM((8, width), f32),
            pltpu.VMEM((width, wide), bf16),
            pltpu.VMEM((width, lat), bf16),
            pltpu.VMEM((width, half), bf16),
            pltpu.VMEM((width, wide), bf16),
            pltpu.VMEM((2, 2, width, 256), bf16),
            pltpu.VMEM((2, width, down), bf16),
        ]
        + [DMA((RING,))]
        + [DMA((RING, 3, ends))] * 2
        + [DMA((RING, 6, sides))] * 2
        + [DMA((RING,))] * 2
        + [DMA((3,)), DMA((len(SAVED) + 1,)), DMA((2, 2)), DMA((2, 2)), DMA((2,))],
        compiler_params=pltpu.CompilerParams(
            collective_id=cid, has_side_effects=True, vmem_limit_bytes=67043328
        ),
    )(parents, lengths, tokens, *shards)
    final, bias, gains = got[:3]
    gathered = [g.reshape(n * s.shape[0], s.shape[1]) for g, s in zip(got[3:], shards)]
    rest = got[3 + len(shards) :]
    kept = [dict(zip(names, rest[i * len(names) : (i + 1) * len(names)])) for i in range(LAYERS)]
    weights = []
    for layer in range(LAYERS):
        q, l, kv, o, g, u, d = gathered[1 + layer * len(PARTS) : 1 + (layer + 1) * len(PARTS)]
        weights.append((q, l, kept[layer]["wkv"], o, g, u, d))
    return final, bias, gains, kept, weights


def body(inputs, cotangent, parents, lengths, g1, wq, wl, wk, wv, wo, g2, wg, wu, wd, *, n):
    trees, tree, width = inputs.shape
    rows = wq.shape[1]
    latr = wk.shape[2]

    def packed(layer):
        cast = lambda w: w[layer].astype(bf16)
        kv = jnp.stack([wk[layer], wv[layer]]).astype(bf16).reshape(-1, wk.shape[3])
        return [cast(wq), cast(wl), kv, cast(wo).T, cast(wg), cast(wu), cast(wd).T]

    gain_rows = jnp.stack([g1[0], g2[0], g1[1], g2[1]], axis=1).astype(bf16)
    gain_rows = jnp.pad(gain_rows, ((0, 0), (0, 128 - 2 * LAYERS)))
    shards = [gain_rows] + packed(0) + packed(1)
    out, bias, gains, kept, weights = forward(
        n, inputs.reshape(trees * tree, width), parents, lengths, trees, shards, 576, 0
    )
    outputs = out.reshape(inputs.shape)
    cot = cotangent.reshape(trees * tree, width)
    grad, summed = backward(n, cot, gains, bias, kept, weights, 576, 1)
    out = []
    for layer in range(LAYERS):
        dd, dg, du, do, dq, dl, kv = summed[(1 - layer) * 7 : (1 - layer) * 7 + 7]
        kv = kv.reshape(2, GROUPS, latr, -1)
        gain = summed[14]
        out.append(
            (gain[:, 2 * layer], dq, dl, kv[0], kv[1], do.T, gain[:, 2 * layer + 1], dg, du, dd.T)
        )
    stacked = tuple(jnp.stack([out[layer][slot] for layer in range(LAYERS)]) for slot in range(10))
    return (outputs, grad.reshape(inputs.shape)) + stacked


def solution(mesh):
    n = mesh.shape["fsdp"]
    by_one, by_two = P(None, "fsdp"), P(None, "fsdp", None)
    by_lat, by_last = P(None, None, "fsdp", None), P(None, None, "fsdp")
    params = (by_one, by_two, by_two, by_lat, by_lat, by_last, by_one, by_two, by_two, by_last)
    trees = P("fsdp", None, None)
    return jax.shard_map(
        functools.partial(body, n=n),
        mesh=mesh,
        in_specs=(trees, trees, P("fsdp", None), P("fsdp", None)) + params,
        out_specs=(trees, trees) + params,
        check_vma=False,
    )
```

```python
import functools
import math

import jax
import jax.numpy as jnp
from jax import lax
from jax.experimental import pallas as pl
from jax.experimental.pallas import tpu as pltpu
from jax.sharding import PartitionSpec as P

HEADS = 16
HD = 64
GROUPS = 2
LAT = 256
LAYERS = 2
LAG = 2
RING = 16
KZ = 3 * LAG + 2
epsilon = 1e-05

MESH = pl.DeviceIdType.MESH
ANY = pl.BlockSpec(memory_space=pltpu.HBM)
DMA = pltpu.SemaphoreType.DMA
bf16 = jnp.bfloat16
f32 = jnp.float32


def dims_of(n):
    chips = n // 2
    side = 1
    if chips & (chips - 1) == 0:
        side = 2 ** ((chips.bit_length() - 1) // 3)
    return chips // (side * side), side, side


def index(n, z, y, x, c):
    Z, Y, X = dims_of(n)
    return ((z * Y + y) * X + x) * 2 + c


def place(n):
    Z, Y, X = dims_of(n)
    me = lax.axis_index("fsdp")
    return me // (2 * X * Y), lax.rem(me // (2 * X), Y), lax.rem(me // 2, X), lax.rem(me, 2)


def greet(n, z, y, x, c):
    Z, Y, X = dims_of(n)
    peers = [index(n, lax.rem(z + o, Z), y, x, c) for o in range(1, Z)]
    peers += [index(n, z, lax.rem(y + o, Y), x, c) for o in range(1, Y)]
    peers += [index(n, z, y, lax.rem(x + o, X), c) for o in range(1, X)]
    peers += [index(n, z, y, x, 1 - c)]
    bar = pltpu.get_barrier_semaphore()
    for peer in peers:
        pl.semaphore_signal(bar, inc=1, device_id=(peer,), device_id_type=MESH)
    pl.semaphore_wait(bar, len(peers))


def remote(src, dst, send, recv, device):
    copy = describe(src, dst, send, recv, device)
    copy.start()
    return copy


def cut(widths, target):
    out = []
    for a, w in enumerate(widths):
        k, u = max(1, round(w / target)), w // 128
        edges = [round(j * u / k) for j in range(k + 1)]
        for lo, hi in zip(edges, edges[1:]):
            size = hi - lo
            inner = max(1, round(size / 6)) if size > 1 else 0
            outer = size - 2 * inner
            left = outer // 2 if len(out) % 2 else (outer + 1) // 2
            out.append((a,) + tuple(128 * e for e in (lo, lo + left, lo + left + inner, hi - (outer - left), hi)))
    return out


def relays(Z):
    return Z == 4


class Sometimes:
    def __init__(self, copy, sends, receives):
        self.copy, self.sends, self.receives = copy, sends, receives
        pl.when(sends)(copy.start)

    def wait(self):
        pl.when(self.sends)(self.copy.wait_send)
        pl.when(self.receives)(self.copy.wait_recv)


def describe(src, dst, send, recv, device):
    return pltpu.make_async_remote_copy(
        src_ref=src, dst_ref=dst, send_sem=send, recv_sem=recv, device_id=(device,), device_id_type=MESH
    )


NT = (((1,), (1,)), ((), ()))
TN = (((0,), (0,)), ((), ()))


def dot(a, b):
    return jnp.dot(a, b, preferred_element_type=f32)


def dot_nt(a, b):
    return lax.dot_general(a, b, NT, preferred_element_type=f32)


def dot_tn(a, b):
    return lax.dot_general(a, b, TN, preferred_element_type=f32)


def tiles(size, tile):
    def run(body):
        def step(j, carry):
            body(pl.ds(pl.multiple_of(j * tile, tile), tile))
            return carry

        lax.fori_loop(0, size // tile, step, 0)

    return run


def build_bias(parents, lengths, bias):
    trees, tree = bias.shape[0], bias.shape[1]
    count = parents.shape[1]
    key = lax.broadcasted_iota(jnp.int32, (1, tree), 1)
    row = lax.broadcasted_iota(jnp.int32, (tree, 1), 0)
    for t in range(trees):
        start = jnp.int32(0)
        reach, total = [], jnp.zeros((tree, tree), f32)
        for s in range(count):
            end = start + lengths[t, s]
            line = jnp.where((key >= start) & (key < end), 1.0, 0.0)
            for u in range(s):
                line = line + jnp.where(parents[t, s] == u, reach[u], 0.0)
            reach.append(line)
            total = total + jnp.where((row >= start) & (row < end), 1.0, 0.0) * line
            start = end
        seen = (total > 0.5) & (key <= row)
        bias[t] = jnp.where(seen, 0.0, -1e30)


def norm_to(dst, src, gain, rows=64):
    @tiles(src.shape[0], rows)
    def _(at):
        h = src[at, :]
        r = lax.rsqrt(jnp.mean(h * h, axis=-1, keepdims=True) + epsilon)
        dst[at, :] = (h * r * gain).astype(bf16)


def attention_forward_step(q, k, v, bias, o, stats):
    trees, tree = bias.shape[0], bias.shape[1]
    pairs = q.shape[1] // 128
    scale = 1.0 / math.sqrt(HD)
    lane = lax.broadcasted_iota(jnp.int32, (tree, 128), 1)

    def step(j):
        t, pair = j // pairs, lax.rem(j, pairs)
        rows = pl.ds(pl.multiple_of(t * tree, tree), tree)
        cols = pl.ds(pl.multiple_of(pair * 128, 128), 128)
        q2, k2, v2 = q[rows, cols], k[rows, cols], v[rows, cols]
        mixed, log_total = [], stats[rows, :]
        for half in range(2):
            mine = (lane >= HD) if half else (lane < HD)
            s = dot_nt(jnp.where(mine, q2 * jnp.asarray(scale, bf16), jnp.zeros_like(q2)), k2) + bias[t]
            top = jnp.max(s, axis=-1, keepdims=True)
            e = jnp.exp(s - top)
            total = jnp.sum(e, axis=-1, keepdims=True)
            p = (e * (1.0 / total)).astype(bf16)
            mixed.append(dot(p, v2))
            log_total = jnp.where(lane == pair * 2 + half, top + jnp.log(total), log_total)
        stats[rows, :] = log_total
        o[rows, cols] = jnp.where(lane < HD, mixed[0], mixed[1]).astype(bf16)

    return step


VM = pl.BlockSpec(memory_space=pltpu.VMEM)
SM = pl.BlockSpec(memory_space=pltpu.SMEM)


def norm_back_to(dst, carry_in, dn, h_ref, gain, gain_grad, low=None, rows=64):
    gain_grad[...] = jnp.zeros_like(gain_grad)

    @tiles(h_ref.shape[0], rows)
    def _(at):
        h, d = h_ref[at, :], dn[at, :]
        r = lax.rsqrt(jnp.mean(h * h, axis=-1, keepdims=True) + epsilon)
        gain_grad[...] += jnp.sum(d * h * r, axis=0, keepdims=True)
        weighted = d * gain
        inner = jnp.mean(weighted * h, axis=-1, keepdims=True)
        total = carry_in[at, :] + (r * weighted - h * (r * r * r) * inner)
        dst[at, :] = total
        if low is not None:
            low[at, :] = total.astype(bf16)


def attention_backward_step(q, k, v, do, bias, stats, dq, dk, dv):
    trees, tree = bias.shape[0], bias.shape[1]
    pairs = q.shape[1] // 128
    scale = 1.0 / math.sqrt(HD)
    lane = lax.broadcasted_iota(jnp.int32, (tree, 128), 1)

    def step(j):
        t, pair = j // pairs, lax.rem(j, pairs)
        rows = pl.ds(pl.multiple_of(t * tree, tree), tree)
        cols = pl.ds(pl.multiple_of(pair * 128, 128), 128)
        q2, k2, v2, do2 = q[rows, cols], k[rows, cols], v[rows, cols], do[rows, cols]
        logs = stats[rows, :]
        zero = jnp.zeros_like(q2)
        got = []
        for half in range(2):
            mine = (lane >= HD) if half else (lane < HD)
            log_total = jnp.sum(jnp.where(lane == pair * 2 + half, logs, 0.0), axis=-1, keepdims=True)
            s = dot_nt(jnp.where(mine, q2 * jnp.asarray(scale, bf16), zero), k2) + bias[t]
            p = jnp.exp(s - log_total)
            dp = dot_nt(jnp.where(mine, do2, zero), v2)
            inner = jnp.sum(p * dp, axis=-1, keepdims=True)
            ds = (p * (dp - inner)).astype(bf16)
            got.append((dot(ds, k2), dot_tn(ds, q2), dot_tn(p.astype(bf16), do2)))
        low = lane < HD
        dq[rows, cols] = (jnp.where(low, got[0][0], got[1][0]) * scale).astype(bf16)
        dk[rows, cols] = (jnp.where(low, got[0][1], got[1][1]) * scale).astype(bf16)
        dv[rows, cols] = jnp.where(low, got[0][2], got[1][2]).astype(bf16)

    return step


def plus(*terms):
    if len(terms) < 3:
        return sum(terms[1:], terms[0])
    return sum((t.astype(f32) for t in terms[1:]), terms[0].astype(f32)).astype(bf16)


class Scatter:
    def __init__(self, n, chunks, jobs, K, outs, bufs, sems, gain_rows):
        self.n, self.chunks, self.jobs, self.K, self.outs = n, chunks, jobs, K, outs
        self.LB, self.RB, self.G, self.R0, self.P1, self.R1, self.P2, self.R2, self.RZ, self.R3, self.P3, self.R4 = bufs
        self.lsem, self.ls, self.cs, self.cr, self.ss, self.sr, self.zs, self.zr = sems
        self.gain_rows = gain_rows
        self.ready = set()
        self.stages = [self.from_partner, self.second, self.third, self.fourth, self.fifth, self.finish]
        self.held = [None] * len(chunks)
        self.at = 0
        self.started = False
        turns, last = [], None
        for a, *_ in chunks:
            left = jobs[a]["left"]
            if left is not last and left is not None:
                turns.append(a)
                last = left
            turns_now = len(turns) - 1
            self.turn = getattr(self, "turn", []) + [turns_now]
        self.turns = turns

    def left_copy(self, t):
        return pltpu.make_async_copy(self.jobs[self.turns[t]]["left"], self.LB.at[t % 2], self.lsem.at[t % 2])

    def first_of(self, i):
        return self.jobs[self.chunks[i][0]]["left"] is not None and (i == 0 or self.turn[i] != self.turn[i - 1])

    def right_copy(self, i, which=0):
        a, lo, e1, e2, e3, hi = self.chunks[i]
        return pltpu.make_async_copy(
            self.jobs[a]["right"][which].at[:, lo:hi], self.RB.at[i % 2, :, 0 : hi - lo], self.ls.at[i % 2]
        )

    def fetch(self, i):
        if self.first_of(i):
            self.left_copy(self.turn[i]).start()
        if self.jobs[self.chunks[i][0]]["left"] is not None:
            self.right_copy(i).start()

    def has(self, i):
        return i >= len(self.chunks) or all(w in self.ready for w in self.jobs[self.chunks[i][0]]["needs"])

    def slot(self, times=1):
        for _ in range(times):
            i = self.at
            if i < len(self.chunks) and not (self.has(i) and self.has(i + 1)):
                return
            if not self.started:
                self.fetch(0)
                self.started = True
            last = len(self.stages) - 1
            if i >= len(self.chunks) + LAG * last:
                return
            for s in range(last, -1, -1):
                j = i - LAG * s
                if 0 <= j < len(self.chunks):
                    if s > 0:
                        for copy in self.held[j]:
                            copy.wait()
                    self.held[j] = self.stages[s](j)
            self.at += 1

    def drain(self):
        while self.at < len(self.chunks) + LAG * (len(self.stages) - 1):
            before = self.at
            self.slot()
            assert self.at > before

    def from_partner(self, i):
        Z, Y, X = dims_of(self.n)
        z, y, x, c = place(self.n)
        a, lo, e1, e2, e3, hi = self.chunks[i]
        k, w = i % self.K, hi - lo
        G, LB, RB = self.G, self.LB, self.RB
        rows = G.shape[6 - 1]
        job = self.jobs[a]
        t = self.turn[i]
        depth = LB.shape[2] // Z
        if job["left"] is not None:
            if self.first_of(i):
                self.left_copy(t).wait()
            self.right_copy(i).wait()
        if i + 1 < len(self.chunks):
            self.fetch(i + 1)
        if job["left"] is None:
            lines = self.gain_rows[...].astype(bf16)
            pick = lax.broadcasted_iota(jnp.int32, (lines.shape[0], w), 0)
            pick = (pick == lax.broadcasted_iota(jnp.int32, (lines.shape[0], w), 1)).astype(bf16)
            for zz in range(Z):
                part = dot_tn(lines[:, zz * depth : (zz + 1) * depth], pick)
                G[k, zz, :, :, :, :, 0:w] = part.astype(bf16).reshape(Y, X, 2, rows, w)
        elif len(job["right"]) == 1:

            step = 2 if Z % 2 == 0 else 1

            def block(zz):
                part = dot_tn(LB[t % 2, :, span(zz, step * depth)], RB[i % 2, :, 0:w])
                G[k, pl.ds(zz * step, step), :, :, :, :, 0:w] = part.astype(bf16).reshape(step, Y, X, 2, rows, w)

            loop(0, Z // step, block)
        else:
            quarter = rows // 4
            group = lax.broadcasted_iota(jnp.int32, (rows, w), 0) >> (quarter.bit_length() - 1)
            for which in range(4):
                if which:
                    copy = self.right_copy(i, which)
                    copy.start()
                    copy.wait()

                def block(zz, carry):
                    at = pl.ds(pl.multiple_of(zz * depth, depth), depth)
                    part = dot_tn(LB[t % 2, :, at], RB[i % 2, :, 0:w]).reshape(Y, X, 2, rows, w)
                    if which:
                        part = jnp.where(group == which, part, G[k, zz, :, :, :, :, 0:w].astype(f32))
                    G[k, zz, :, :, :, :, 0:w] = part.astype(bf16)
                    return carry

                lax.fori_loop(0, Z, block, 0)
        copy = remote(
            G.at[k, :, :, :, 1 - c, :, 0:w],
            self.R0.at[k, :, :, :, :, 0:w],
            self.cs.at[k],
            self.cr.at[k],
            index(self.n, z, y, x, 1 - c),
        )
        return [copy]

    def along(self, axis, i, flow, src, dst):
        n, k = self.n, i % self.K
        Z, Y, X = dims_of(n)
        z, y, x, c = place(n)
        copies = []
        for o in range(1, X if axis == "x" else Y):
            p = lax.rem(x + o, X) if axis == "x" else lax.rem(y + o, Y)
            to = index(n, z, y, p, c) if axis == "x" else index(n, z, p, x, c)
            copies.append(remote(src(p), dst(o - 1), self.ss.at[k, flow, o - 1], self.sr.at[k, flow, o - 1], to))
        return copies

    def along_z(self, i, flow, src, dst):
        n, k = self.n, i % KZ
        Z, Y, X = dims_of(n)
        z, y, x, c = place(n)
        copies = []
        for o in range(1, Z):
            p = lax.rem(z + o, Z)
            to = index(n, p, y, x, c)
            sems = self.zs.at[k, flow, o - 1], self.zr.at[k, flow, o - 1]
            if not relays(Z):
                copies.append(remote(src(p), dst(o - 1), *sems, to))
            elif o == 2:
                direct = describe(src(p), dst(o - 1), *sems, to)
                copies.append(Sometimes(direct, (z == 0) | (z == 3), (z == 1) | (z == 2)))
            else:
                ends = (3, 0) if o == 1 else (0, 3)
                copies.append(Sometimes(describe(src(p), dst(o - 1), *sems, to), z != ends[0], z != ends[1]))
        if relays(Z):
            for which, end, via in ((0, 3, 2), (1, 0, 1)):
                sems = self.zs.at[k, flow, Z - 1 + which], self.zr.at[k, flow, Z - 1 + which]
                relay = describe(src(3 - end), dst(Z - 1), *sems, index(n, via, y, x, c))
                copies.append(Sometimes(relay, z == end, z == via))
        return copies

    def relay_z(self, i, flow, src, dst, add):
        n, k = self.n, i % KZ
        Z, Y, X = dims_of(n)
        z, y, x, c = place(n)
        copies = []
        if relays(Z):
            for via, end in ((2, 0), (1, 3)):
                sems = self.zs.at[k, flow, 1], self.zr.at[k, flow, 1]
                pl.when(z == via)(functools.partial(add, end))
                copy = describe(src(end), dst(1), *sems, index(n, end, y, x, c))
                copies.append(Sometimes(copy, z == via, z == end))
        return copies

    def total_z(self, mine, got):
        Z, Y, X = dims_of(self.n)
        z, y, x, c = place(self.n)
        total = mine.astype(f32)
        for o in range(1, Z):
            term = got(o - 1).astype(f32)
            if relays(Z) and o != 2:
                term = jnp.where(z == (0 if o == 1 else 3), 0.0, term)
            total = total + term
        return total

    def second(self, i):
        G, R0, R1 = self.G, self.R0, self.R1
        Z, Y, X = dims_of(self.n)
        z, y, x, c = place(self.n)
        a, lo, e1, e2, e3, hi = self.chunks[i]
        k, w, h = i % self.K, hi - lo, e2 - lo

        def add(zz):
            G[k, zz, :, :, c, :, 0:w] = plus(G[k, zz, :, :, c, :, 0:w], R0[k, zz, :, :, :, 0:w])

        loop(0, Z, add)
        copies = []
        if h > 0:
            copies += self.along(
                "y", i, 0, lambda p: G.at[k, :, p, :, c, :, 0:h], lambda o: R1.at[k, o, :, 0:X, :, 0:h]
            )
        if w > h:
            copies += self.along(
                "x", i, 1, lambda p: G.at[k, :, :, p, c, :, h:w], lambda o: R1.at[k, o, :, 0:Y, :, h:w]
            )
        return copies

    def third(self, i):
        G, P1, R1, R2, RZ = self.G, self.P1, self.R1, self.R2, self.RZ
        Z, Y, X = dims_of(self.n)
        z, y, x, c = place(self.n)
        a, lo, e1, e2, e3, hi = self.chunks[i]
        k, kz, w, h = i % self.K, i % KZ, hi - lo, e2 - lo
        if h > 0:
            others = [R1[k, o, :, 0:X, :, 0:h] for o in range(Y - 1)]
            P1[k, :, 0:X, :, 0:h] = plus(G[k, :, y, :, c, :, 0:h], *others)
        if w > h:
            others = [R1[k, o, :, 0:Y, :, h:w] for o in range(X - 1)]
            P1[k, :, 0:Y, :, h:w] = plus(G[k, :, :, x, c, :, h:w], *others)
        f1, f3 = e1 - lo, e3 - lo
        copies = []
        if h > f1:
            copies += self.along("x", i, 2, lambda p: P1.at[k, :, p, :, f1:h], lambda o: R2.at[k, o, :, :, f1:h])
        if f3 > h:
            copies += self.along("y", i, 3, lambda p: P1.at[k, :, p, :, h:f3], lambda o: R2.at[k, o, :, :, h:f3])
        if f1 > 0:
            copies += self.along_z(
                i, 0, lambda p: P1.at[k, p, 0:X, :, 0:f1], lambda o: RZ.at[kz, o, 0:X, :, 0:f1]
            )
        if w > f3:
            copies += self.along_z(
                i, 1, lambda p: P1.at[k, p, 0:Y, :, f3:w], lambda o: RZ.at[kz, o, 0:Y, :, f3:w]
            )
        return copies

    def fourth(self, i):
        P1, P2, R2, RZ, R3 = self.P1, self.P2, self.R2, self.RZ, self.R3
        Z, Y, X = dims_of(self.n)
        z, y, x, c = place(self.n)
        a, lo, e1, e2, e3, hi = self.chunks[i]
        k, kz, w, h, f1, f3 = i % self.K, i % KZ, hi - lo, e2 - lo, e1 - lo, e3 - lo
        copies = []
        for start, end, size, flow in ((0, f1, X, 0), (f3, w, Y, 1)):
            if end > start:
                src = lambda p: P1.at[k, p, 0:size, :, start:end]
                dst = lambda o: RZ.at[kz, o, 0:size, :, start:end]

                def add(p):
                    P1[k, p, 0:size, :, start:end] = plus(
                        P1[k, p, 0:size, :, start:end], RZ[kz, Z - 1, 0:size, :, start:end]
                    )

                copies += self.relay_z(i, flow, src, dst, add)
        if h > f1:
            P2[k, :, :, f1:h] = plus(P1[k, :, x, :, f1:h], *[R2[k, o, :, :, f1:h] for o in range(X - 1)])
        if f3 > h:
            P2[k, :, :, h:f3] = plus(P1[k, :, y, :, h:f3], *[R2[k, o, :, :, h:f3] for o in range(Y - 1)])
        if f3 > f1:
            copies += self.along_z(i, 2, lambda p: P2.at[k, p, :, f1:f3], lambda o: R3.at[kz, o, :, f1:f3])
        return copies

    def fifth(self, i):
        P1, P2, RZ, R3, P3, R4 = self.P1, self.P2, self.RZ, self.R3, self.P3, self.R4
        Z, Y, X = dims_of(self.n)
        z, y, x, c = place(self.n)
        a, lo, e1, e2, e3, hi = self.chunks[i]
        k, kz, w, f1, f3 = i % self.K, i % KZ, hi - lo, e1 - lo, e3 - lo
        copies = []
        if f3 > f1:

            def add(p):
                P2[k, p, :, f1:f3] = plus(P2[k, p, :, f1:f3], R3[kz, Z - 1, :, f1:f3])

            copies += self.relay_z(i, 2, lambda p: P2.at[k, p, :, f1:f3], lambda o: R3.at[kz, o, :, f1:f3], add)
        for start, end, size, axis, flow in ((0, f1, X, "x", 4), (f3, w, Y, "y", 5)):
            if end > start:
                total = self.total_z(
                    P1[k, z, 0:size, :, start:end], lambda o: RZ[kz, o, 0:size, :, start:end]
                )
                P3[k, 0:size, :, start:end] = total.astype(bf16)
                copies += self.along(
                    axis, i, flow, lambda p: P3.at[k, p, :, start:end], lambda o: R4.at[k, o, :, start:end]
                )
        return copies

    def finish(self, i):
        P2, R3, P3, R4 = self.P2, self.R3, self.P3, self.R4
        Z, Y, X = dims_of(self.n)
        z, y, x, c = place(self.n)
        a, lo, e1, e2, e3, hi = self.chunks[i]
        k, kz, w, f1, f3 = i % self.K, i % KZ, hi - lo, e1 - lo, e3 - lo
        if f3 > f1:
            self.outs[a][:, e1:e3] = self.total_z(P2[k, z, :, f1:f3], lambda o: R3[kz, o, :, f1:f3])
        for start, end, size, mine in ((0, f1, X, x), (f3, w, Y, y)):
            if end > start:
                total = P3[k, mine, :, start:end].astype(f32)
                for o in range(size - 1):
                    total = total + R4[k, o, :, start:end].astype(f32)
                self.outs[a][:, lo + start : lo + end] = total
        return []


def loop(lo, hi, body, unroll=1):
    def step(j, carry):
        body(j)
        return carry

    lax.fori_loop(lo, hi, step, 0, unroll=unroll)


def span(j, size):
    return pl.ds(pl.multiple_of(j * size, size), size)


KEPT = ("h", "n1", "q", "k", "v", "o", "stats", "h1", "n2", "a", "b", "z", "cp")
NAMES = ("wq", "wl", "wkv", "wo", "wg", "wu", "wd")
MADE = ("gf", "da", "db", "ga", "dq", "dk", "dv", "dc")


def backward_kernel(n, chunks, K, counts, *refs):
    it = iter(refs)
    take = lambda names: {name: next(it) for name in names}
    cot, gains, bias = next(it), next(it), next(it)
    kept = {layer: take(KEPT) for layer in reversed(range(LAYERS))}
    weights = {layer: take(NAMES) for layer in reversed(range(LAYERS))}
    grad_out = next(it)
    stacks = [next(it) for _ in range(counts)]
    outs = [stack.at[layer] for layer in reversed(range(LAYERS)) for stack in stacks[:-1]] + [stacks[-1]]
    made = {layer: take(MADE) for layer in reversed(range(LAYERS))}
    bufs = [next(it) for _ in range(12)]
    gain_rows = next(it)
    v = take(("gf", "da", "db", "ga", "do", "q", "k", "v", "dq", "dk", "dv", "dc", "stats",
              "g", "h", "dm", "ab", "wd", "wgu", "wo", "wkv", "wq", "wl"))
    sems = [next(it) for _ in range(8)]
    insem, outsem, asem, wsem = [next(it) for _ in range(4)]

    jobs = []
    for layer in reversed(range(LAYERS)):
        s, m = kept[layer], made[layer]
        need = lambda *names: [(layer, name) for name in names]
        jobs += [
            {"left": m["gf"], "right": [s["z"]], "needs": need("gf")},
            {"left": s["n2"], "right": [m["da"]], "needs": need("da")},
            {"left": s["n2"], "right": [m["db"]], "needs": need("db")},
            {"left": m["ga"], "right": [s["o"]], "needs": need("ga")},
            {"left": s["n1"], "right": [m["dq"]], "needs": need("dq")},
            {"left": s["n1"], "right": [m["dc"]], "needs": need("dc")},
        ]
        half = m["dk"].shape[1] // GROUPS
        rights = [m[name].at[:, g * half : (g + 1) * half] for name in ("dk", "dv") for g in range(GROUPS)]
        jobs += [{"left": s["cp"], "right": rights, "needs": need("dk", "dv")}]
    jobs += [{"left": None, "right": None, "needs": [(0, "end")]}]
    scatter = Scatter(n, chunks, jobs, K, outs, bufs, sems, gain_rows)
    slot = scatter.slot

    ff, width = v["da"].shape[1], v["g"].shape[1]
    count = ff // 256
    tokens = v["g"].shape[0]
    gain_rows[...] = jnp.zeros_like(gain_rows)
    greeted = []

    for layer in reversed(range(LAYERS)):
        s, w, m = kept[layer], weights[layer], made[layer]
        first = layer == LAYERS - 1
        copies = {}

        def load(name, src, at):
            copies[name] = pltpu.make_async_copy(src, v[name], insem.at[at])
            copies[name].start()

        def tile_ab(j, which):
            src = s["ab"[which]]
            return pltpu.make_async_copy(src.at[:, span(j, 256)], v["ab"].at[which, lax.rem(j, 2)], asem.at[which, lax.rem(j, 2)])

        def tile_wd(j):
            return pltpu.make_async_copy(w["wd"].at[:, span(j, 256)], v["wd"].at[lax.rem(j, 2)], wsem.at[0, lax.rem(j, 2)])

        def tile_gu(j, which):
            src = w["wg"] if which == 0 else w["wu"]
            return pltpu.make_async_copy(src.at[span(j, 256), :], v["wgu"].at[which, j % 2], wsem.at[1 + which, j % 2])

        def publish(name):
            copy = pltpu.make_async_copy(v[name], m[name], outsem.at[MADE.index(name)])
            copy.start()
            return copy

        if first:
            load("g", cot, 0)
        tile_wd(0).start()
        tile_ab(0, 0).start()
        tile_ab(0, 1).start()
        load("h", s["h1"], 1)
        for at, name in enumerate(("q", "k", "v", "stats")):
            load(name, s[name], 2 + at)
        for at, name in enumerate(("wo", "wkv", "wq", "wl")):
            load(name, w[name], 6 + at)
        for j in range(2):
            tile_gu(j, 0).start()
            tile_gu(j, 1).start()
        if first:
            z, y, x, c = place(n)
            greet(n, z, y, x, c)
            copies["g"].wait()

        @tiles(tokens, 64)
        def _(at):
            v["gf"][at, :] = v["g"][at, :].astype(bf16)

        publish("gf").wait()
        scatter.ready.add((layer, "gf"))
        slot()

        def dz_step(j):
            at = span(j, 256)
            tile_wd(j).wait()
            tile_ab(j, 0).wait()
            tile_ab(j, 1).wait()

            @pl.when(j + 1 < count)
            def _():
                tile_wd(j + 1).start()
                tile_ab(j + 1, 0).start()
                tile_ab(j + 1, 1).start()

            dz = dot(v["gf"][...], v["wd"][lax.rem(j, 2)])
            v["da"][:, at] = (dz * v["ab"][0, lax.rem(j, 2)]).astype(bf16)
            v["db"][:, at] = (dz * v["ab"][1, lax.rem(j, 2)]).astype(bf16)

        cuts = [0, count // 3, 2 * count // 3, count]
        for lo, hi in zip(cuts, cuts[1:]):
            loop(lo, hi, dz_step)
            slot(1 + (lo > 0 and hi < count))
        out_da, out_db = publish("da"), publish("db")
        for j in range(width // 256):
            tile_gu(j, 0).wait()
            tile_gu(j, 1).wait()
            at = slice(j * 256, (j + 1) * 256)
            v["dm"][:, at] = dot_nt(v["da"][...], v["wgu"][0, j % 2]) + dot_nt(v["db"][...], v["wgu"][1, j % 2])
            if j + 2 < width // 256:
                tile_gu(j + 2, 0).start()
                tile_gu(j + 2, 1).start()
            if j == 0:
                out_da.wait()
                out_db.wait()
                scatter.ready |= {(layer, "da"), (layer, "db")}
            slot()
        copies["h"].wait()
        norm_back_to(v["g"], v["g"], v["dm"], v["h"], gains[2 * layer + 1 : 2 * layer + 2, :],
                     gain_rows.at[2 * layer + 1 : 2 * layer + 2, :], low=v["ga"])
        copies["h"] = pltpu.make_async_copy(s["h"], v["h"], insem.at[1])
        copies["h"].start()
        out_ga = publish("ga")
        slot()
        copies["wo"].wait()

        @tiles(width, 512)
        def _(at):
            v["do"][:, at] = dot(v["ga"][...], v["wo"][:, at]).astype(bf16)

        out_ga.wait()
        scatter.ready.add((layer, "ga"))
        slot()
        for name in ("q", "k", "v", "stats"):
            copies[name].wait()
        pairs = bias.shape[0] * v["q"].shape[1] // 128
        step = attention_backward_step(v["q"], v["k"], v["v"], v["do"], bias, v["stats"], v["dq"], v["dk"], v["dv"])
        for part in range(4):
            loop(part * pairs // 4, (part + 1) * pairs // 4, step, 2)
            slot(2)
        out_q = [publish(name) for name in ("dq", "dk", "dv")]
        copies["wkv"].wait()
        half = v["wkv"].shape[2]
        for g in range(GROUPS):
            at = slice(g * half, (g + 1) * half)
            both = dot_nt(v["dk"][:, at], v["wkv"][g]) + dot_nt(v["dv"][:, at], v["wkv"][GROUPS + g])
            v["dc"][:, g * LAT : (g + 1) * LAT] = both.astype(bf16)
        for copy in out_q:
            copy.wait()
        scatter.ready |= {(layer, "dq"), (layer, "dk"), (layer, "dv")}
        out_dc = publish("dc")
        slot()
        copies["wq"].wait()
        copies["wl"].wait()

        @tiles(width, 512)
        def _(at):
            v["dm"][:, at] = dot_nt(v["dq"][...], v["wq"][at, :]) + dot_nt(v["dc"][...], v["wl"][at, :])

        out_dc.wait()
        scatter.ready.add((layer, "dc"))
        slot()
        copies["h"].wait()
        norm_back_to(v["g"], v["g"], v["dm"], v["h"], gains[2 * layer : 2 * layer + 1, :],
                     gain_rows.at[2 * layer : 2 * layer + 1, :])
        scatter.ready.add((layer, "end"))
        slot()
    last = pltpu.make_async_copy(v["g"], grad_out, insem.at[0])
    last.start()
    scatter.drain()
    last.wait()


def backward(n, cot, gains, bias, kept, weights, target, cid):
    Z, Y, X = dims_of(n)
    tokens, width = cot.shape
    rows = width // n
    ff = weights[0][4].shape[1]
    wide, lat = weights[0][0].shape[1], weights[0][1].shape[1]
    half = weights[0][2].shape[2]
    each = [ff, ff, ff, wide, wide, lat, half]
    widths = each * LAYERS + [128]
    chunks = cut(widths, target)
    K = 2 * LAG + 1
    most = max(X, Y)
    sides, ends = max(most, 2) - 1, max(Z - 1, 1)
    most_wide = max(ch[5] - ch[1] for ch in chunks)
    ring = lambda *shape, deep=K: pltpu.VMEM((deep,) + shape + (rows, most_wide), bf16)
    tok = lambda w, t=bf16: pltpu.VMEM((tokens, w), t)
    made = dict(gf=width, da=ff, db=ff, ga=width, dq=wide, dk=wide, dv=wide, dc=lat)
    layers = list(reversed(range(LAYERS)))
    operands = [cot, gains, bias]
    for layer in layers:
        operands += [kept[layer][name] for name in KEPT]
    for layer in layers:
        operands += list(weights[layer])
    shapes = [jax.ShapeDtypeStruct((tokens, width), f32)]
    shapes += [jax.ShapeDtypeStruct((LAYERS, rows, w), f32) for w in each] + [jax.ShapeDtypeStruct((rows, 128), f32)]
    count = len(each) + 1
    shapes += [jax.ShapeDtypeStruct((tokens, made[name]), bf16) for layer in layers for name in MADE]
    got = pl.pallas_call(
        functools.partial(backward_kernel, n, chunks, K, count),
        out_shape=shapes,
        in_specs=[ANY, VM, VM] + [ANY] * (len(operands) - 3),
        out_specs=[ANY] + [VM] * count + [ANY] * (LAYERS * len(MADE)),
        scratch_shapes=[
            pltpu.VMEM((2, tokens, width), bf16),
            pltpu.VMEM((2, tokens, most_wide), bf16),
            ring(Z, Y, X, 2),
            ring(Z, Y, X),
            ring(Z, most),
            ring(sides, Z, most),
            ring(Z),
            ring(sides, Z),
            ring(Z, most, deep=KZ),
            ring(Z, deep=KZ),
            ring(most),
            ring(sides),
            pltpu.VMEM((8, width), f32),
            tok(width), tok(ff), tok(ff), tok(width), tok(wide), tok(wide), tok(wide), tok(wide),
            tok(wide), tok(wide), tok(wide), tok(lat), tok(128, f32),
            tok(width, f32), tok(width, f32), tok(width, f32),
            pltpu.VMEM((2, 2, tokens, 256), f32),
            pltpu.VMEM((2, width, 256), bf16),
            pltpu.VMEM((2, 2, 256, ff), bf16),
        ]
        + [pltpu.VMEM(weights[0][i].shape, bf16) for i in (3, 2, 0, 1)]
        + [DMA((2,)), DMA((2,)), DMA((K,)), DMA((K,))]
        + [DMA((K, 6, sides))] * 2
        + [DMA((KZ, 3, ends + 2))] * 2
        + [DMA((10,)), DMA((len(MADE),)), DMA((2, 2)), DMA((3, 2))],
        compiler_params=pltpu.CompilerParams(
            collective_id=cid, has_side_effects=True, vmem_limit_bytes=67043328
        ),
    )(*operands)
    return got[0], got[1 : 1 + count]


class Gather:
    def __init__(self, n, chunks, ins, outs, sems):
        self.n, self.chunks, self.ins, self.outs = n, chunks, ins, outs
        self.own_sem, self.zs, self.zr, self.ss, self.sr, self.cs, self.cr = sems
        self.stages = [self.first, self.second, self.third, self.fourth, self.to_partner, lambda i: []]
        self.held = [None] * len(chunks)
        self.at = 0
        self.total = len(chunks) + LAG * (len(self.stages) - 1)

    def slot(self, times=1):
        for _ in range(times):
            if self.at >= self.total:
                return
            last = len(self.stages) - 1
            for s in range(last, -1, -1):
                j = self.at - LAG * s
                if 0 <= j < len(self.chunks):
                    if s > 0:
                        for copy in self.held[j]:
                            copy.wait()
                    self.held[j] = self.stages[s](j)
            self.at += 1

    def until(self, a, column):
        need = max(i for i, ch in enumerate(self.chunks) if ch[0] == a and ch[1] < column)
        while self.at < need + LAG * (len(self.stages) - 1) + 1:
            self.slot()

    def along(self, axis, i, flow, src, dst):
        n, k = self.n, i % RING
        Z, Y, X = dims_of(n)
        z, y, x, c = place(n)
        copies = []
        for o in range(1, X if axis == "x" else Y):
            to = index(n, z, y, lax.rem(x + o, X), c) if axis == "x" else index(n, z, lax.rem(y + o, Y), x, c)
            copies.append(remote(src, dst, self.ss.at[k, flow, o - 1], self.sr.at[k, flow, o - 1], to))
        return copies

    def along_z(self, i, flow, src, dst):
        n, k = self.n, i % RING
        Z, Y, X = dims_of(n)
        z, y, x, c = place(n)
        copies = []
        for o in range(1, Z):
            to = index(n, lax.rem(z + o, Z), y, x, c)
            sems = self.zs.at[k, flow, o - 1], self.zr.at[k, flow, o - 1]
            if relays(Z) and o != 2:
                ends = (Z - 1, 0) if o == 1 else (0, Z - 1)
                copies.append(Sometimes(describe(src, dst, *sems, to), z != ends[0], z != ends[1]))
            else:
                copies.append(remote(src, dst, *sems, to))
        return copies

    def relay_z(self, i, flow, part):
        n, k = self.n, i % RING
        Z, Y, X = dims_of(n)
        z, y, x, c = place(n)
        copies = []
        if relays(Z):
            for o, via, end in ((1, 1, 0), (3, 2, 3)):
                block = part(3 - end)
                sems = self.zs.at[k, flow, o - 1], self.zr.at[k, flow, o - 1]
                copies.append(Sometimes(describe(block, block, *sems, index(n, end, y, x, c)), z == via, z == end))
        return copies

    def views(self, i):
        z, y, x, c = place(self.n)
        a, lo, e1, e2, e3, hi = self.chunks[i]
        out = self.outs[a]
        inner = lambda zz: out.at[zz, y, x, c, :, e1:e3]
        left = lambda zz: out.at[zz, y, :, c, :, lo:e1]
        right = lambda zz: out.at[zz, :, x, c, :, e3:hi]
        return z, y, x, c, out, inner, left, right

    def first(self, i):
        z, y, x, c, out, inner, left, right = self.views(i)
        a, lo, e1, e2, e3, hi = self.chunks[i]
        src = self.ins[a]
        own = pltpu.make_async_copy(src.at[:, lo:hi], out.at[z, y, x, c, :, lo:hi], self.own_sem.at[i % RING])
        own.start()
        copies = [own]
        if e3 > e1:
            copies += self.along_z(i, 0, src.at[:, e1:e3], inner(z))
        if e1 > lo:
            copies += self.along("x", i, 0, src.at[:, lo:e1], out.at[z, y, x, c, :, lo:e1])
        if hi > e3:
            copies += self.along("y", i, 1, src.at[:, e3:hi], out.at[z, y, x, c, :, e3:hi])
        return copies

    def second(self, i):
        z, y, x, c, out, inner, left, right = self.views(i)
        a, lo, e1, e2, e3, hi = self.chunks[i]
        copies = self.relay_z(i, 0, inner) if e3 > e1 else []
        if e1 > lo:
            copies += self.along_z(i, 1, left(z), left(z))
        if hi > e3:
            copies += self.along_z(i, 2, right(z), right(z))
        return copies

    def third(self, i):
        z, y, x, c, out, inner, left, right = self.views(i)
        a, lo, e1, e2, e3, hi = self.chunks[i]
        copies = []
        if e1 > lo:
            copies += self.relay_z(i, 1, left)
        if hi > e3:
            copies += self.relay_z(i, 2, right)
        if e3 > e1:
            part = out.at[:, y, x, c, :, e1:e2]
            copies += self.along("x", i, 2, part, part)
            part = out.at[:, y, x, c, :, e2:e3]
            copies += self.along("y", i, 3, part, part)
        return copies

    def fourth(self, i):
        z, y, x, c, out, inner, left, right = self.views(i)
        a, lo, e1, e2, e3, hi = self.chunks[i]
        copies = []
        if e2 > lo:
            part = out.at[:, y, :, c, :, lo:e2]
            copies += self.along("y", i, 4, part, part)
        if hi > e2:
            part = out.at[:, :, x, c, :, e2:hi]
            copies += self.along("x", i, 5, part, part)
        return copies

    def to_partner(self, i):
        z, y, x, c, out, inner, left, right = self.views(i)
        a, lo, e1, e2, e3, hi = self.chunks[i]
        part = out.at[:, :, :, c, :, lo:hi]
        return [remote(part, part, self.cs.at[i % RING], self.cr.at[i % RING], index(self.n, z, y, x, 1 - c))]


SAVED = ("n1", "q", "k", "v", "o", "stats", "h1", "n2", "cp", "z", "wkv")
PARTS = ("wq", "wl", "kv", "wo", "wg", "wu", "wd")
CAST = ("wq", "wl", "wg", "wu")


def fill_picks(n, picks):
    which, lat, width = picks.shape
    quarter = width // n // which
    bits = quarter.bit_length() - 1
    row = lax.broadcasted_iota(jnp.int32, (lat, width), 0)
    col = lax.broadcasted_iota(jnp.int32, (lat, width), 1)
    base = ((row >> bits) * (which * quarter)) + (row & (quarter - 1))
    for i in range(which):
        picks[i] = jnp.where(col == base + i * quarter, 1.0, 0.0).astype(bf16)


def forward_kernel(n, chunks, *refs):
    it = iter(refs)
    take = lambda names: {name: next(it) for name in names}
    parents, lengths, tokens_ref, gain_in = [next(it) for _ in range(4)]
    count = 1 + LAYERS * len(PARTS)
    raw = take(PARTS)
    final, bias, gains_out = next(it), next(it), next(it)
    outs = [next(it) for _ in range(count)]
    kept = [take(SAVED + ("a", "b", "h")) for _ in range(LAYERS)]
    v = take(SAVED + ("h", "c", "ab", "picks", "gr", "gt", "wq", "wl", "kv", "wo", "wgu", "wd"))
    low = take(CAST)
    send = {name: low.get(name, raw[name]) for name in PARTS}
    ins = [gain_in] + [send[name].at[layer] for layer in range(LAYERS) for name in PARTS]
    gather = Gather(n, chunks, ins, outs, [next(it) for _ in range(7)])
    insem, savesem, absem, gusem, wdsem = [next(it) for _ in range(5)]
    slot = gather.slot
    z, y, x, c = place(n)
    for name in CAST:
        low[name][...] = raw[name][...].astype(bf16)
    greet(n, z, y, x, c)
    slot(3)

    def rows_of(a):
        return outs[a].reshape(outs[a].shape[0] * outs[a].shape[1] * outs[a].shape[2] * 2 * outs[a].shape[4], outs[a].shape[5])

    gathered = [rows_of(a) for a in range(count)]

    def load(a, name, at):
        gather.until(a, outs[a].shape[5])
        copy = pltpu.make_async_copy(gathered[a], v[name], insem.at[at])
        copy.start()
        return copy

    @tiles(tokens_ref.shape[0], 64)
    def _(at):
        v["h"][at, :] = tokens_ref[at, :].astype(f32)

    build_bias(parents, lengths, bias)
    slot()
    fill_picks(n, v["picks"])
    slot()
    copy = load(0, "gr", 0)
    copy.wait()
    lines = lax.broadcasted_iota(jnp.int32, (8, 128), 0) == lax.broadcasted_iota(jnp.int32, (8, 128), 1)
    v["gt"][...] = dot_nt(lines.astype(bf16), v["gr"][...])
    gains_out[...] = v["gt"][...]
    gains = v["gt"]

    for layer in range(LAYERS):
        s = kept[layer]
        base = 1 + layer * len(PARTS)
        saves = []

        def save(name, src=None):
            copy = pltpu.make_async_copy(v[src or name], s[name], savesem.at[len(saves)])
            copy.start()
            saves.append(copy)

        h, n1, n2, h1 = v["h"], v["n1"], v["n2"], v["h1"]
        save("h")
        norm_to(n1, h, gains[2 * layer : 2 * layer + 1, :])
        save("n1")
        slot()
        load(base, "wq", 0).wait()
        wl_copy = load(base + 1, "wl", 1)

        @tiles(v["wq"].shape[1], 512)
        def _(at):
            v["q"][:, at] = dot(n1[...], v["wq"][:, at]).astype(bf16)

        save("q")
        slot()
        wl_copy.wait()
        kv_copy = load(base + 2, "kv", 2)
        v["c"][...] = dot(n1[...], v["wl"][...]).astype(bf16)
        spread = dot(v["c"][:, 0:LAT], v["picks"][0] + v["picks"][GROUPS])
        for g in range(1, GROUPS):
            spread += dot(v["c"][:, g * LAT : (g + 1) * LAT], v["picks"][g] + v["picks"][GROUPS + g])
        v["cp"][...] = spread.astype(bf16)
        save("cp")
        kv_copy.wait()
        half = v["kv"].shape[1]
        for i in range(2 * GROUPS):
            v["wkv"][i] = dot(v["picks"][i], v["kv"][...]).astype(bf16)
        save("wkv")
        slot()
        for g in range(GROUPS):
            cg = v["c"][:, g * LAT : (g + 1) * LAT]
            v["k"][:, g * half : (g + 1) * half] = dot(cg, v["wkv"][g]).astype(bf16)
            v["v"][:, g * half : (g + 1) * half] = dot(cg, v["wkv"][GROUPS + g]).astype(bf16)
        save("k")
        save("v")
        slot()
        v["stats"][...] = jnp.zeros_like(v["stats"])
        pairs = bias.shape[0] * v["q"].shape[1] // 128
        step = attention_forward_step(v["q"], v["k"], v["v"], bias, v["o"], v["stats"])
        for part in range(4):
            loop(part * pairs // 4, (part + 1) * pairs // 4, step, 2)
            slot()
        save("o")
        save("stats")
        load(base + 3, "wo", 0).wait()

        @tiles(v["wo"].shape[0], 512)
        def _(at):
            h1[:, at] = h[:, at] + dot_nt(v["o"][...], v["wo"][at, :])

        save("h1")
        slot()
        norm_to(n2, h1, gains[2 * layer + 1 : 2 * layer + 2, :])
        save("n2")
        ff = v["z"].shape[1]
        steps = ff // 256

        def tile_gu(j, which):
            src = gathered[base + 4 + which]
            return pltpu.make_async_copy(src.at[:, span(j, 256)], v["wgu"].at[which, lax.rem(j, 2)], gusem.at[which, lax.rem(j, 2)])

        def put(j, which):
            dst = s["ab"[which]]
            return pltpu.make_async_copy(v["ab"].at[which, lax.rem(j, 2)], dst.at[:, span(j, 256)], absem.at[which, lax.rem(j, 2)])

        cuts = [i * steps // 5 for i in range(6)]
        for lo, hi in zip(cuts, cuts[1:]):
            gather.until(base + 4, hi * 256)
            gather.until(base + 5, hi * 256)
            tile_gu(lo, 0).start()
            tile_gu(lo, 1).start()

            def gate_step(j):
                at = span(j, 256)
                tile_gu(j, 0).wait()
                tile_gu(j, 1).wait()

                @pl.when(j + 1 < hi)
                def _():
                    tile_gu(j + 1, 0).start()
                    tile_gu(j + 1, 1).start()

                @pl.when(j >= 2)
                def _():
                    put(j - 2, 0).wait()
                    put(j - 2, 1).wait()

                a = dot(n2[...], v["wgu"][0, lax.rem(j, 2)])
                b = dot(n2[...], v["wgu"][1, lax.rem(j, 2)])
                sig = 1.0 / (1.0 + jnp.exp(-a))
                silu = a * sig
                v["ab"][0, lax.rem(j, 2)] = b * sig * (1.0 + a * (1.0 - sig))
                v["ab"][1, lax.rem(j, 2)] = silu
                put(j, 0).start()
                put(j, 1).start()
                v["z"][:, at] = (silu * b).astype(bf16)

            loop(lo, hi, gate_step)
            slot()
        save("z")
        for copy in saves:
            copy.wait()
        for j in (steps - 2, steps - 1):
            put(j, 0).wait()
            put(j, 1).wait()
        downs = [(ch[1], ch[5]) for ch in chunks if ch[0] == base + 6]

        def tile_wd(i):
            lo, hi = downs[i]
            gather.until(base + 6, hi)
            copy = pltpu.make_async_copy(gathered[base + 6].at[:, lo:hi], v["wd"].at[i % 2, :, 0 : hi - lo], wdsem.at[i % 2])
            copy.start()
            return copy

        coming = tile_wd(0)
        for i, (lo, hi) in enumerate(downs):
            coming.wait()
            if i + 1 < len(downs):
                coming = tile_wd(i + 1)

            @tiles(h.shape[1], 512)
            def _(at):
                add = dot_nt(v["z"][:, lo:hi], v["wd"][i % 2, at, 0 : hi - lo])
                h[:, at] = (h1[:, at] if i == 0 else h[:, at]) + add

            slot()
    last = pltpu.make_async_copy(v["h"], final, insem.at[0])
    last.start()
    slot(gather.total)
    last.wait()


def forward(n, tokens, parents, lengths, trees, gain_rows, parts, target, cid):
    Z, Y, X = dims_of(n)
    rows, width = tokens.shape
    shapes = {name: part.shape[1:] for name, part in zip(PARTS, parts)}
    shards = [jax.ShapeDtypeStruct(gain_rows.shape, bf16)]
    shards += [jax.ShapeDtypeStruct(shapes[name], bf16) for layer in range(LAYERS) for name in PARTS]
    wide, lat, half, ff = shapes["wq"][1], shapes["wl"][1], shapes["kv"][1], shapes["wg"][1]
    chunks = cut([s.shape[1] for s in shards], target)
    order = []
    for a in range(len(shards)):
        mine = [ch for ch in chunks if ch[0] == a]
        part = PARTS[(a - 1) % len(PARTS)] if a else None
        if part == "wg":
            both = [ch for ch in chunks if ch[0] == a + 1]
            mine = [ch for pair in zip(mine, both) for ch in pair]
        elif part == "wu":
            mine = []
        order += mine
    ends, sides = max(Z - 1, 1), max(X, Y, 2) - 1
    tok = lambda w, t=bf16: jax.ShapeDtypeStruct((rows, w), t)
    saved = dict(
        n1=tok(width), q=tok(wide), k=tok(wide), v=tok(wide), o=tok(wide), stats=tok(128, f32),
        h1=tok(width, f32), n2=tok(width), cp=tok(width), z=tok(ff),
        wkv=jax.ShapeDtypeStruct((2 * GROUPS, LAT, half), bf16), a=tok(ff, f32), b=tok(ff, f32), h=tok(width, f32),
    )
    names = SAVED + ("a", "b", "h")
    tree = rows // trees
    out_shape = [tok(width, f32), jax.ShapeDtypeStruct((trees, tree, tree), f32), jax.ShapeDtypeStruct((8, width), f32)]
    out_shape += [jax.ShapeDtypeStruct((Z, Y, X, 2) + s.shape, s.dtype) for s in shards]
    out_shape += [saved[name] for layer in range(LAYERS) for name in names]
    vmem = lambda s: pltpu.VMEM(s.shape, s.dtype)
    down = max(ch[5] - ch[1] for ch in order)
    got = pl.pallas_call(
        functools.partial(forward_kernel, n, order),
        out_shape=out_shape,
        in_specs=[SM, SM, VM, ANY] + [VM if name in CAST else ANY for name in PARTS],
        out_specs=[ANY, VM, VM] + [ANY] * (len(out_shape) - 3),
        scratch_shapes=[vmem(saved[name]) for name in SAVED]
        + [
            pltpu.VMEM((rows, width), f32),
            pltpu.VMEM((rows, lat), bf16),
            pltpu.VMEM((2, 2, rows, 256), f32),
            pltpu.VMEM((2 * GROUPS, LAT, width), bf16),
            pltpu.VMEM((width, 128), bf16),
            pltpu.VMEM((8, width), f32),
            pltpu.VMEM((width, wide), bf16),
            pltpu.VMEM((width, lat), bf16),
            pltpu.VMEM((width, half), bf16),
            pltpu.VMEM((width, wide), bf16),
            pltpu.VMEM((2, 2, width, 256), bf16),
            pltpu.VMEM((2, width, down), bf16),
        ]
        + [pltpu.VMEM((LAYERS,) + shapes[name], bf16) for name in CAST]
        + [DMA((RING,))]
        + [DMA((RING, 3, ends))] * 2
        + [DMA((RING, 6, sides))] * 2
        + [DMA((RING,))] * 2
        + [DMA((3,)), DMA((len(SAVED) + 1,)), DMA((2, 2)), DMA((2, 2)), DMA((2,))],
        compiler_params=pltpu.CompilerParams(
            collective_id=cid, has_side_effects=True, vmem_limit_bytes=67043328
        ),
    )(parents, lengths, tokens, gain_rows, *parts)
    final, bias, gains = got[:3]
    gathered = [g.reshape(n * s.shape[0], s.shape[1]) for g, s in zip(got[3:], shards)]
    rest = got[3 + len(shards) :]
    kept = [dict(zip(names, rest[i * len(names) : (i + 1) * len(names)])) for i in range(LAYERS)]
    weights = []
    for layer in range(LAYERS):
        q, l, kv, o, g, u, d = gathered[1 + layer * len(PARTS) : 1 + (layer + 1) * len(PARTS)]
        weights.append((q, l, kept[layer]["wkv"], o, g, u, d))
    return final, bias, gains, kept, weights


def body(inputs, cotangent, parents, lengths, g1, wq, wl, wk, wv, wo, g2, wg, wu, wd, *, n):
    trees, tree, width = inputs.shape
    rows = wq.shape[1]
    latr = wk.shape[2]

    kv = jnp.stack([wk, wv], axis=1).astype(bf16).reshape(LAYERS, 4 * latr, wk.shape[3])
    gain_rows = jnp.stack([g1[0], g2[0], g1[1], g2[1]], axis=1).astype(bf16)
    gain_rows = jnp.pad(gain_rows, ((0, 0), (0, 128 - 2 * LAYERS)))
    parts = [wq, wl, kv, wo.astype(bf16).transpose(0, 2, 1), wg, wu, wd.astype(bf16).transpose(0, 2, 1)]
    out, bias, gains, kept, weights = forward(
        n, inputs.reshape(trees * tree, width), parents, lengths, trees, gain_rows, parts, 576, 0
    )
    outputs = out.reshape(inputs.shape)
    cot = cotangent.reshape(trees * tree, width)
    grad, summed = backward(n, cot, gains, bias, kept, weights, 576, 1)
    dd, dg, du, do, dq, dl, kv, gain = summed
    kv = kv.reshape(LAYERS, 2, GROUPS, latr, -1)
    gain = gain.T[: 2 * LAYERS].reshape(LAYERS, 2, rows)
    flip = lambda d: d.transpose(0, 2, 1)
    grads = (gain[:, 0], dq, dl, kv[:, 0], kv[:, 1], flip(do), gain[:, 1], dg, du, flip(dd))
    return (outputs, grad.reshape(inputs.shape)) + grads


def solution(mesh):
    n = mesh.shape["fsdp"]
    by_one, by_two = P(None, "fsdp"), P(None, "fsdp", None)
    by_lat, by_last = P(None, None, "fsdp", None), P(None, None, "fsdp")
    params = (by_one, by_two, by_two, by_lat, by_lat, by_last, by_one, by_two, by_two, by_last)
    trees = P("fsdp", None, None)
    return jax.shard_map(
        functools.partial(body, n=n),
        mesh=mesh,
        in_specs=(trees, trees, P("fsdp", None), P("fsdp", None)) + params,
        out_specs=(trees, trees) + params,
        check_vma=False,
    )
```

```python
import functools
import math

import jax
import jax.numpy as jnp
from jax import lax
from jax.experimental import pallas as pl
from jax.experimental.pallas import tpu as pltpu
from jax.sharding import PartitionSpec as P

HEADS = 16
HD = 64
GROUPS = 2
LAT = 256
LAYERS = 2
LAG = 2
RING = 16
KZ = 3 * LAG + 2
epsilon = 1e-05

MESH = pl.DeviceIdType.MESH
ANY = pl.BlockSpec(memory_space=pltpu.HBM)
DMA = pltpu.SemaphoreType.DMA
bf16 = jnp.bfloat16
f32 = jnp.float32


def dims_of(n):
    chips = n // 2
    side = 1
    if chips & (chips - 1) == 0:
        side = 2 ** ((chips.bit_length() - 1) // 3)
    return chips // (side * side), side, side


def index(n, z, y, x, c):
    Z, Y, X = dims_of(n)
    return ((z * Y + y) * X + x) * 2 + c


def place(n):
    Z, Y, X = dims_of(n)
    me = lax.axis_index("fsdp")
    return me // (2 * X * Y), lax.rem(me // (2 * X), Y), lax.rem(me // 2, X), lax.rem(me, 2)


def greet(n, z, y, x, c):
    Z, Y, X = dims_of(n)
    peers = [index(n, lax.rem(z + o, Z), y, x, c) for o in range(1, Z)]
    peers += [index(n, z, lax.rem(y + o, Y), x, c) for o in range(1, Y)]
    peers += [index(n, z, y, lax.rem(x + o, X), c) for o in range(1, X)]
    peers += [index(n, z, y, x, 1 - c)]
    bar = pltpu.get_barrier_semaphore()
    for peer in peers:
        pl.semaphore_signal(bar, inc=1, device_id=(peer,), device_id_type=MESH)
    pl.semaphore_wait(bar, len(peers))


def remote(src, dst, send, recv, device):
    copy = describe(src, dst, send, recv, device)
    copy.start()
    return copy


def cut(widths, target):
    out = []
    for a, w in enumerate(widths):
        k, u = max(1, round(w / target)), w // 128
        edges = [round(j * u / k) for j in range(k + 1)]
        for lo, hi in zip(edges, edges[1:]):
            size = hi - lo
            inner = max(1, round(size / 6)) if size > 1 else 0
            outer = size - 2 * inner
            left = outer // 2 if len(out) % 2 else (outer + 1) // 2
            out.append((a,) + tuple(128 * e for e in (lo, lo + left, lo + left + inner, hi - (outer - left), hi)))
    return out


def relays(Z):
    return Z == 4


class Sometimes:
    def __init__(self, copy, sends, receives):
        self.copy, self.sends, self.receives = copy, sends, receives
        pl.when(sends)(copy.start)

    def wait(self):
        pl.when(self.sends)(self.copy.wait_send)
        pl.when(self.receives)(self.copy.wait_recv)


def describe(src, dst, send, recv, device):
    return pltpu.make_async_remote_copy(
        src_ref=src, dst_ref=dst, send_sem=send, recv_sem=recv, device_id=(device,), device_id_type=MESH
    )


NT = (((1,), (1,)), ((), ()))
TN = (((0,), (0,)), ((), ()))


def dot(a, b):
    return jnp.dot(a, b, preferred_element_type=f32)


def dot_nt(a, b):
    return lax.dot_general(a, b, NT, preferred_element_type=f32)


def dot_tn(a, b):
    return lax.dot_general(a, b, TN, preferred_element_type=f32)


def tiles(size, tile):
    def run(body):
        def step(j, carry):
            body(pl.ds(pl.multiple_of(j * tile, tile), tile))
            return carry

        lax.fori_loop(0, size // tile, step, 0)

    return run


def build_bias(parents, lengths, bias):
    trees, tree = bias.shape[0], bias.shape[1]
    count = parents.shape[1]
    key = lax.broadcasted_iota(jnp.int32, (1, tree), 1)
    row = lax.broadcasted_iota(jnp.int32, (tree, 1), 0)
    for t in range(trees):
        start = jnp.int32(0)
        reach, total = [], jnp.zeros((tree, tree), f32)
        for s in range(count):
            end = start + lengths[t, s]
            line = jnp.where((key >= start) & (key < end), 1.0, 0.0)
            for u in range(s):
                line = line + jnp.where(parents[t, s] == u, reach[u], 0.0)
            reach.append(line)
            total = total + jnp.where((row >= start) & (row < end), 1.0, 0.0) * line
            start = end
        seen = (total > 0.5) & (key <= row)
        bias[t] = jnp.where(seen, 0.0, -1e30)


def norm_to(dst, src, gain, rows=64):
    @tiles(src.shape[0], rows)
    def _(at):
        h = src[at, :]
        r = lax.rsqrt(jnp.mean(h * h, axis=-1, keepdims=True) + epsilon)
        dst[at, :] = (h * r * gain).astype(bf16)


def attention_forward_step(q, k, v, bias, o, probs, put):
    tree = bias.shape[1]
    pairs = q.shape[1] // 128
    scale = 1.0 / math.sqrt(HD)
    lane = lax.broadcasted_iota(jnp.int32, (tree, 128), 1)

    def step(j):
        t, pair = j // pairs, lax.rem(j, pairs)
        rows = pl.ds(pl.multiple_of(t * tree, tree), tree)
        cols = pl.ds(pl.multiple_of(pair * 128, 128), 128)
        q2, k2, v2 = q[rows, cols], k[rows, cols], v[rows, cols]
        mixed = []

        @pl.when(j >= 2)
        def _():
            put(j - 2).wait()

        for half in range(2):
            mine = (lane >= HD) if half else (lane < HD)
            s = dot_nt(jnp.where(mine, q2 * jnp.asarray(scale, bf16), jnp.zeros_like(q2)), k2) + bias[t]
            top = jnp.max(s, axis=-1, keepdims=True)
            e = jnp.exp(s - top)
            total = jnp.sum(e, axis=-1, keepdims=True)
            p = (e * (1.0 / total)).astype(bf16)
            probs[lax.rem(j, 2), half] = p
            mixed.append(dot(p, v2))
        put(j).start()
        o[rows, cols] = jnp.where(lane < HD, mixed[0], mixed[1]).astype(bf16)

    return step


VM = pl.BlockSpec(memory_space=pltpu.VMEM)
SM = pl.BlockSpec(memory_space=pltpu.SMEM)


def norm_back_to(dst, carry_in, dn, h_ref, gain, gain_grad, low=None, rows=64):
    gain_grad[...] = jnp.zeros_like(gain_grad)

    @tiles(h_ref.shape[0], rows)
    def _(at):
        h, d = h_ref[at, :], dn[at, :]
        r = lax.rsqrt(jnp.mean(h * h, axis=-1, keepdims=True) + epsilon)
        gain_grad[...] += jnp.sum(d * h * r, axis=0, keepdims=True)
        weighted = d * gain
        inner = jnp.mean(weighted * h, axis=-1, keepdims=True)
        total = carry_in[at, :] + (r * weighted - h * (r * r * r) * inner)
        dst[at, :] = total
        if low is not None:
            low[at, :] = total.astype(bf16)


def attention_backward_step(q, k, v, do, probs, get, count, dq, dk, dv):
    tree = probs.shape[2]
    pairs = q.shape[1] // 128
    scale = 1.0 / math.sqrt(HD)
    lane = lax.broadcasted_iota(jnp.int32, (tree, 128), 1)

    def step(j):
        t, pair = j // pairs, lax.rem(j, pairs)
        rows = pl.ds(pl.multiple_of(t * tree, tree), tree)
        cols = pl.ds(pl.multiple_of(pair * 128, 128), 128)
        get(j).wait()

        @pl.when(j + 3 < count)
        def _():
            get(j + 3).start()

        q2, k2, v2, do2 = q[rows, cols], k[rows, cols], v[rows, cols], do[rows, cols]
        zero = jnp.zeros_like(q2)
        got = []
        for half in range(2):
            mine = (lane >= HD) if half else (lane < HD)
            low = probs[lax.rem(j, 4), half]
            p = low.astype(f32)
            dp = dot_nt(jnp.where(mine, do2, zero), v2)
            inner = jnp.sum(p * dp, axis=-1, keepdims=True)
            ds = (p * (dp - inner)).astype(bf16)
            got.append((dot(ds, k2), dot_tn(ds, q2), dot_tn(low, do2)))
        low = lane < HD
        dq[rows, cols] = (jnp.where(low, got[0][0], got[1][0]) * scale).astype(bf16)
        dk[rows, cols] = (jnp.where(low, got[0][1], got[1][1]) * scale).astype(bf16)
        dv[rows, cols] = jnp.where(low, got[0][2], got[1][2]).astype(bf16)

    return step


def plus(*terms):
    if len(terms) < 3:
        return sum(terms[1:], terms[0])
    return sum((t.astype(f32) for t in terms[1:]), terms[0].astype(f32)).astype(bf16)


class Scatter:
    def __init__(self, n, chunks, jobs, K, outs, bufs, sems, gain_rows):
        self.n, self.chunks, self.jobs, self.K, self.outs = n, chunks, jobs, K, outs
        self.LB, self.RB, self.G, self.R0, self.P1, self.R1, self.P2, self.R2, self.RZ, self.R3, self.P3, self.R4 = bufs
        self.lsem, self.ls, self.cs, self.cr, self.ss, self.sr, self.zs, self.zr = sems
        self.gain_rows = gain_rows
        self.ready = set()
        self.stages = [self.from_partner, self.second, self.third, self.fourth, self.fifth, self.finish]
        self.held = [None] * len(chunks)
        self.at = 0
        self.fetched = 0
        turns, last = [], None
        for a, *_ in chunks:
            left = jobs[a]["left"]
            if left is not last and left is not None:
                turns.append(a)
                last = left
            turns_now = len(turns) - 1
            self.turn = getattr(self, "turn", []) + [turns_now]
        self.turns = turns

    def left_copy(self, t):
        return pltpu.make_async_copy(self.jobs[self.turns[t]]["left"], self.LB.at[t % 2], self.lsem.at[t % 2])

    def first_of(self, i):
        return self.jobs[self.chunks[i][0]]["left"] is not None and (i == 0 or self.turn[i] != self.turn[i - 1])

    def right_copy(self, i, which=0):
        a, lo, e1, e2, e3, hi = self.chunks[i]
        return pltpu.make_async_copy(
            self.jobs[a]["right"][which].at[:, lo:hi], self.RB.at[i % 2, :, 0 : hi - lo], self.ls.at[i % 2]
        )

    def fetch(self, i):
        self.fetched = i + 1
        if self.first_of(i):
            self.left_copy(self.turn[i]).start()
        if self.jobs[self.chunks[i][0]]["left"] is not None:
            self.right_copy(i).start()

    def has(self, i):
        return i >= len(self.chunks) or all(w in self.ready for w in self.jobs[self.chunks[i][0]]["needs"])

    def slot(self, times=1):
        for _ in range(times):
            i = self.at
            if not self.has(i):
                return
            if self.fetched <= i < len(self.chunks):
                self.fetch(i)
            last = len(self.stages) - 1
            if i >= len(self.chunks) + LAG * last:
                return
            for s in range(last, -1, -1):
                j = i - LAG * s
                if 0 <= j < len(self.chunks):
                    if s > 0:
                        for copy in self.held[j]:
                            copy.wait()
                    self.held[j] = self.stages[s](j)
            self.at += 1

    def drain(self):
        while self.at < len(self.chunks) + LAG * (len(self.stages) - 1):
            before = self.at
            self.slot()
            assert self.at > before

    def from_partner(self, i):
        Z, Y, X = dims_of(self.n)
        z, y, x, c = place(self.n)
        a, lo, e1, e2, e3, hi = self.chunks[i]
        k, w = i % self.K, hi - lo
        G, LB, RB = self.G, self.LB, self.RB
        rows = G.shape[6 - 1]
        job = self.jobs[a]
        t = self.turn[i]
        depth = LB.shape[2] // Z
        if job["left"] is not None:
            if self.first_of(i):
                self.left_copy(t).wait()
            self.right_copy(i).wait()
        if i + 1 < len(self.chunks) and self.has(i + 1):
            self.fetch(i + 1)
        if job["left"] is None:
            lines = self.gain_rows[...].astype(bf16)
            pick = lax.broadcasted_iota(jnp.int32, (lines.shape[0], w), 0)
            pick = (pick == lax.broadcasted_iota(jnp.int32, (lines.shape[0], w), 1)).astype(bf16)
            for zz in range(Z):
                part = dot_tn(lines[:, zz * depth : (zz + 1) * depth], pick)
                G[k, zz, :, :, :, :, 0:w] = part.astype(bf16).reshape(Y, X, 2, rows, w)
        elif len(job["right"]) == 1:

            step = 2 if Z % 2 == 0 else 1

            def block(zz):
                part = dot_tn(LB[t % 2, :, span(zz, step * depth)], RB[i % 2, :, 0:w])
                G[k, pl.ds(zz * step, step), :, :, :, :, 0:w] = part.astype(bf16).reshape(step, Y, X, 2, rows, w)

            loop(0, Z // step, block)
        else:
            quarter = rows // 4
            group = lax.broadcasted_iota(jnp.int32, (rows, w), 0) >> (quarter.bit_length() - 1)
            for which in range(4):
                if which:
                    copy = self.right_copy(i, which)
                    copy.start()
                    copy.wait()

                def block(zz, carry):
                    at = pl.ds(pl.multiple_of(zz * depth, depth), depth)
                    part = dot_tn(LB[t % 2, :, at], RB[i % 2, :, 0:w]).reshape(Y, X, 2, rows, w)
                    if which:
                        part = jnp.where(group == which, part, G[k, zz, :, :, :, :, 0:w].astype(f32))
                    G[k, zz, :, :, :, :, 0:w] = part.astype(bf16)
                    return carry

                lax.fori_loop(0, Z, block, 0)
        copy = remote(
            G.at[k, :, :, :, 1 - c, :, 0:w],
            self.R0.at[k, :, :, :, :, 0:w],
            self.cs.at[k],
            self.cr.at[k],
            index(self.n, z, y, x, 1 - c),
        )
        return [copy]

    def along(self, axis, i, flow, src, dst):
        n, k = self.n, i % self.K
        Z, Y, X = dims_of(n)
        z, y, x, c = place(n)
        copies = []
        for o in range(1, X if axis == "x" else Y):
            p = lax.rem(x + o, X) if axis == "x" else lax.rem(y + o, Y)
            to = index(n, z, y, p, c) if axis == "x" else index(n, z, p, x, c)
            copies.append(remote(src(p), dst(o - 1), self.ss.at[k, flow, o - 1], self.sr.at[k, flow, o - 1], to))
        return copies

    def along_z(self, i, flow, src, dst):
        n, k = self.n, i % KZ
        Z, Y, X = dims_of(n)
        z, y, x, c = place(n)
        copies = []
        for o in range(1, Z):
            p = lax.rem(z + o, Z)
            to = index(n, p, y, x, c)
            sems = self.zs.at[k, flow, o - 1], self.zr.at[k, flow, o - 1]
            if not relays(Z):
                copies.append(remote(src(p), dst(o - 1), *sems, to))
            elif o == 2:
                direct = describe(src(p), dst(o - 1), *sems, to)
                copies.append(Sometimes(direct, (z == 0) | (z == 3), (z == 1) | (z == 2)))
            else:
                ends = (3, 0) if o == 1 else (0, 3)
                copies.append(Sometimes(describe(src(p), dst(o - 1), *sems, to), z != ends[0], z != ends[1]))
        if relays(Z):
            for which, end, via in ((0, 3, 2), (1, 0, 1)):
                sems = self.zs.at[k, flow, Z - 1 + which], self.zr.at[k, flow, Z - 1 + which]
                relay = describe(src(3 - end), dst(Z - 1), *sems, index(n, via, y, x, c))
                copies.append(Sometimes(relay, z == end, z == via))
        return copies

    def relay_z(self, i, flow, src, dst, add):
        n, k = self.n, i % KZ
        Z, Y, X = dims_of(n)
        z, y, x, c = place(n)
        copies = []
        if relays(Z):
            for via, end in ((2, 0), (1, 3)):
                sems = self.zs.at[k, flow, 1], self.zr.at[k, flow, 1]
                pl.when(z == via)(functools.partial(add, end))
                copy = describe(src(end), dst(1), *sems, index(n, end, y, x, c))
                copies.append(Sometimes(copy, z == via, z == end))
        return copies

    def total_z(self, mine, got):
        Z, Y, X = dims_of(self.n)
        z, y, x, c = place(self.n)
        total = mine.astype(f32)
        for o in range(1, Z):
            term = got(o - 1).astype(f32)
            if relays(Z) and o != 2:
                term = jnp.where(z == (0 if o == 1 else 3), 0.0, term)
            total = total + term
        return total

    def second(self, i):
        G, R0, R1 = self.G, self.R0, self.R1
        Z, Y, X = dims_of(self.n)
        z, y, x, c = place(self.n)
        a, lo, e1, e2, e3, hi = self.chunks[i]
        k, w, h = i % self.K, hi - lo, e2 - lo

        def add(zz):
            G[k, zz, :, :, c, :, 0:w] = plus(G[k, zz, :, :, c, :, 0:w], R0[k, zz, :, :, :, 0:w])

        loop(0, Z, add)
        copies = []
        if h > 0:
            copies += self.along(
                "y", i, 0, lambda p: G.at[k, :, p, :, c, :, 0:h], lambda o: R1.at[k, o, :, 0:X, :, 0:h]
            )
        if w > h:
            copies += self.along(
                "x", i, 1, lambda p: G.at[k, :, :, p, c, :, h:w], lambda o: R1.at[k, o, :, 0:Y, :, h:w]
            )
        return copies

    def third(self, i):
        G, P1, R1, R2, RZ = self.G, self.P1, self.R1, self.R2, self.RZ
        Z, Y, X = dims_of(self.n)
        z, y, x, c = place(self.n)
        a, lo, e1, e2, e3, hi = self.chunks[i]
        k, kz, w, h = i % self.K, i % KZ, hi - lo, e2 - lo
        if h > 0:
            others = [R1[k, o, :, 0:X, :, 0:h] for o in range(Y - 1)]
            P1[k, :, 0:X, :, 0:h] = plus(G[k, :, y, :, c, :, 0:h], *others)
        if w > h:
            others = [R1[k, o, :, 0:Y, :, h:w] for o in range(X - 1)]
            P1[k, :, 0:Y, :, h:w] = plus(G[k, :, :, x, c, :, h:w], *others)
        f1, f3 = e1 - lo, e3 - lo
        copies = []
        if h > f1:
            copies += self.along("x", i, 2, lambda p: P1.at[k, :, p, :, f1:h], lambda o: R2.at[k, o, :, :, f1:h])
        if f3 > h:
            copies += self.along("y", i, 3, lambda p: P1.at[k, :, p, :, h:f3], lambda o: R2.at[k, o, :, :, h:f3])
        if f1 > 0:
            copies += self.along_z(
                i, 0, lambda p: P1.at[k, p, 0:X, :, 0:f1], lambda o: RZ.at[kz, o, 0:X, :, 0:f1]
            )
        if w > f3:
            copies += self.along_z(
                i, 1, lambda p: P1.at[k, p, 0:Y, :, f3:w], lambda o: RZ.at[kz, o, 0:Y, :, f3:w]
            )
        return copies

    def fourth(self, i):
        P1, P2, R2, RZ, R3 = self.P1, self.P2, self.R2, self.RZ, self.R3
        Z, Y, X = dims_of(self.n)
        z, y, x, c = place(self.n)
        a, lo, e1, e2, e3, hi = self.chunks[i]
        k, kz, w, h, f1, f3 = i % self.K, i % KZ, hi - lo, e2 - lo, e1 - lo, e3 - lo
        copies = []
        for start, end, size, flow in ((0, f1, X, 0), (f3, w, Y, 1)):
            if end > start:
                src = lambda p: P1.at[k, p, 0:size, :, start:end]
                dst = lambda o: RZ.at[kz, o, 0:size, :, start:end]

                def add(p):
                    P1[k, p, 0:size, :, start:end] = plus(
                        P1[k, p, 0:size, :, start:end], RZ[kz, Z - 1, 0:size, :, start:end]
                    )

                copies += self.relay_z(i, flow, src, dst, add)
        if h > f1:
            P2[k, :, :, f1:h] = plus(P1[k, :, x, :, f1:h], *[R2[k, o, :, :, f1:h] for o in range(X - 1)])
        if f3 > h:
            P2[k, :, :, h:f3] = plus(P1[k, :, y, :, h:f3], *[R2[k, o, :, :, h:f3] for o in range(Y - 1)])
        if f3 > f1:
            copies += self.along_z(i, 2, lambda p: P2.at[k, p, :, f1:f3], lambda o: R3.at[kz, o, :, f1:f3])
        return copies

    def fifth(self, i):
        P1, P2, RZ, R3, P3, R4 = self.P1, self.P2, self.RZ, self.R3, self.P3, self.R4
        Z, Y, X = dims_of(self.n)
        z, y, x, c = place(self.n)
        a, lo, e1, e2, e3, hi = self.chunks[i]
        k, kz, w, f1, f3 = i % self.K, i % KZ, hi - lo, e1 - lo, e3 - lo
        copies = []
        if f3 > f1:

            def add(p):
                P2[k, p, :, f1:f3] = plus(P2[k, p, :, f1:f3], R3[kz, Z - 1, :, f1:f3])

            copies += self.relay_z(i, 2, lambda p: P2.at[k, p, :, f1:f3], lambda o: R3.at[kz, o, :, f1:f3], add)
        for start, end, size, axis, flow in ((0, f1, X, "x", 4), (f3, w, Y, "y", 5)):
            if end > start:
                total = self.total_z(
                    P1[k, z, 0:size, :, start:end], lambda o: RZ[kz, o, 0:size, :, start:end]
                )
                P3[k, 0:size, :, start:end] = total.astype(bf16)
                copies += self.along(
                    axis, i, flow, lambda p: P3.at[k, p, :, start:end], lambda o: R4.at[k, o, :, start:end]
                )
        return copies

    def finish(self, i):
        P2, R3, P3, R4 = self.P2, self.R3, self.P3, self.R4
        Z, Y, X = dims_of(self.n)
        z, y, x, c = place(self.n)
        a, lo, e1, e2, e3, hi = self.chunks[i]
        k, kz, w, f1, f3 = i % self.K, i % KZ, hi - lo, e1 - lo, e3 - lo
        if f3 > f1:
            self.outs[a][:, e1:e3] = self.total_z(P2[k, z, :, f1:f3], lambda o: R3[kz, o, :, f1:f3])
        for start, end, size, mine in ((0, f1, X, x), (f3, w, Y, y)):
            if end > start:
                total = P3[k, mine, :, start:end].astype(f32)
                for o in range(size - 1):
                    total = total + R4[k, o, :, start:end].astype(f32)
                self.outs[a][:, lo + start : lo + end] = total
        return []


def loop(lo, hi, body, unroll=1):
    def step(j, carry):
        body(j)
        return carry

    lax.fori_loop(lo, hi, step, 0, unroll=unroll)


def span(j, size):
    return pl.ds(pl.multiple_of(j * size, size), size)


KEPT = ("h", "n1", "q", "k", "v", "o", "p", "h1", "n2", "a", "b", "z", "cp")
NAMES = ("wq", "wl", "wkv", "wo", "wg", "wu", "wd")
MADE = ("gf", "da", "db", "ga", "dq", "dk", "dv", "dc")


def backward_kernel(n, chunks, K, counts, *refs):
    it = iter(refs)
    take = lambda names: {name: next(it) for name in names}
    cot, gains = next(it), next(it)
    kept = {layer: take(KEPT) for layer in reversed(range(LAYERS))}
    weights = {layer: take(NAMES) for layer in reversed(range(LAYERS))}
    grad_out = next(it)
    stacks = [next(it) for _ in range(counts)]
    outs = [stack.at[layer] for layer in reversed(range(LAYERS)) for stack in stacks[:-1]] + [stacks[-1]]
    made = {layer: take(MADE) for layer in reversed(range(LAYERS))}
    bufs = [next(it) for _ in range(12)]
    gain_rows = next(it)
    v = take(("gf", "da", "db", "ga", "do", "q", "k", "v", "dq", "dk", "dv", "dc", "p",
              "g", "h", "dm", "ab", "wd", "wgu", "wo", "wkv", "wq", "wl"))
    sems = [next(it) for _ in range(8)]
    insem, outsem, asem, wsem, psem = [next(it) for _ in range(5)]

    jobs = []
    for layer in reversed(range(LAYERS)):
        s, m = kept[layer], made[layer]
        need = lambda *names: [(layer, name) for name in names]
        jobs += [
            {"left": m["gf"], "right": [s["z"]], "needs": need("gf")},
            {"left": s["n2"], "right": [m["da"]], "needs": need("da")},
            {"left": s["n2"], "right": [m["db"]], "needs": need("db")},
            {"left": m["ga"], "right": [s["o"]], "needs": need("ga")},
            {"left": s["n1"], "right": [m["dq"]], "needs": need("dq")},
        ]
        half = m["dk"].shape[1] // GROUPS
        rights = [m[name].at[:, g * half : (g + 1) * half] for name in ("dk", "dv") for g in range(GROUPS)]
        jobs += [
            {"left": s["cp"], "right": rights, "needs": need("dk", "dv")},
            {"left": s["n1"], "right": [m["dc"]], "needs": need("dc")},
        ]
    jobs += [{"left": None, "right": None, "needs": [(0, "end")]}]
    scatter = Scatter(n, chunks, jobs, K, outs, bufs, sems, gain_rows)
    slot = scatter.slot

    ff, width = v["da"].shape[1], v["g"].shape[1]
    count = ff // 256
    tokens = v["g"].shape[0]
    gain_rows[...] = jnp.zeros_like(gain_rows)
    greeted = []

    for layer in reversed(range(LAYERS)):
        s, w, m = kept[layer], weights[layer], made[layer]
        first = layer == LAYERS - 1
        copies = {}

        def load(name, src, at):
            copies[name] = pltpu.make_async_copy(src, v[name], insem.at[at])
            copies[name].start()

        def tile_ab(j, which):
            src = s["ab"[which]]
            return pltpu.make_async_copy(src.at[:, span(j, 256)], v["ab"].at[which, lax.rem(j, 2)], asem.at[which, lax.rem(j, 2)])

        def tile_wd(j):
            return pltpu.make_async_copy(w["wd"].at[:, span(j, 256)], v["wd"].at[lax.rem(j, 2)], wsem.at[0, lax.rem(j, 2)])

        def tile_gu(j, which):
            src = w["wg"] if which == 0 else w["wu"]
            return pltpu.make_async_copy(src.at[span(j, 256), :], v["wgu"].at[which, j % 2], wsem.at[1 + which, j % 2])

        def tile_p(j):
            return pltpu.make_async_copy(s["p"].at[j], v["p"].at[lax.rem(j, 4)], psem.at[lax.rem(j, 4)])

        def publish(name):
            copy = pltpu.make_async_copy(v[name], m[name], outsem.at[MADE.index(name)])
            copy.start()
            return copy

        if first:
            load("g", cot, 0)
        tile_wd(0).start()
        tile_ab(0, 0).start()
        tile_ab(0, 1).start()
        load("h", s["h1"], 1)
        for at, name in enumerate(("q", "k", "v")):
            load(name, s[name], 2 + at)
        for at, name in enumerate(("wo", "wkv", "wq", "wl")):
            load(name, w[name], 6 + at)
        for j in range(2):
            tile_gu(j, 0).start()
            tile_gu(j, 1).start()
        for j in range(3):
            tile_p(j).start()
        if first:
            z, y, x, c = place(n)
            greet(n, z, y, x, c)
            copies["g"].wait()

        @tiles(tokens, 64)
        def _(at):
            v["gf"][at, :] = v["g"][at, :].astype(bf16)

        publish("gf").wait()
        scatter.ready.add((layer, "gf"))
        slot()

        def dz_step(j):
            at = span(j, 256)
            tile_wd(j).wait()
            tile_ab(j, 0).wait()
            tile_ab(j, 1).wait()

            @pl.when(j + 1 < count)
            def _():
                tile_wd(j + 1).start()
                tile_ab(j + 1, 0).start()
                tile_ab(j + 1, 1).start()

            dz = dot(v["gf"][...], v["wd"][lax.rem(j, 2)])
            v["da"][:, at] = (dz * v["ab"][0, lax.rem(j, 2)]).astype(bf16)
            v["db"][:, at] = (dz * v["ab"][1, lax.rem(j, 2)]).astype(bf16)

        cuts = [0, count // 3, 2 * count // 3, count]
        for lo, hi in zip(cuts, cuts[1:]):
            loop(lo, hi, dz_step)
            slot(1 + (lo > 0 and hi < count))
        out_da, out_db = publish("da"), publish("db")
        for j in range(width // 256):
            tile_gu(j, 0).wait()
            tile_gu(j, 1).wait()
            at = slice(j * 256, (j + 1) * 256)
            v["dm"][:, at] = dot_nt(v["da"][...], v["wgu"][0, j % 2]) + dot_nt(v["db"][...], v["wgu"][1, j % 2])
            if j + 2 < width // 256:
                tile_gu(j + 2, 0).start()
                tile_gu(j + 2, 1).start()
            if j == 0:
                out_da.wait()
                out_db.wait()
                scatter.ready |= {(layer, "da"), (layer, "db")}
            slot()
        copies["h"].wait()
        norm_back_to(v["g"], v["g"], v["dm"], v["h"], gains[2 * layer + 1 : 2 * layer + 2, :],
                     gain_rows.at[2 * layer + 1 : 2 * layer + 2, :], low=v["ga"])
        copies["h"] = pltpu.make_async_copy(s["h"], v["h"], insem.at[1])
        copies["h"].start()
        out_ga = publish("ga")
        slot()
        copies["wo"].wait()

        @tiles(width, 512)
        def _(at):
            v["do"][:, at] = dot(v["ga"][...], v["wo"][:, at]).astype(bf16)

        out_ga.wait()
        scatter.ready.add((layer, "ga"))
        slot()
        for name in ("q", "k", "v"):
            copies[name].wait()
        pairs = s["p"].shape[0]
        step = attention_backward_step(
            v["q"], v["k"], v["v"], v["do"], v["p"], tile_p, pairs, v["dq"], v["dk"], v["dv"]
        )
        for part in range(8):
            loop(part * pairs // 8, (part + 1) * pairs // 8, step)
            slot()
        out_q = [publish(name) for name in ("dq", "dk", "dv")]
        copies["wkv"].wait()
        half = v["wkv"].shape[2]
        for g in range(GROUPS):
            at = slice(g * half, (g + 1) * half)
            both = dot_nt(v["dk"][:, at], v["wkv"][g]) + dot_nt(v["dv"][:, at], v["wkv"][GROUPS + g])
            v["dc"][:, g * LAT : (g + 1) * LAT] = both.astype(bf16)
        for copy in out_q:
            copy.wait()
        scatter.ready |= {(layer, "dq"), (layer, "dk"), (layer, "dv")}
        out_dc = publish("dc")
        slot()
        copies["wq"].wait()
        copies["wl"].wait()

        @tiles(width, 512)
        def _(at):
            v["dm"][:, at] = dot_nt(v["dq"][...], v["wq"][at, :]) + dot_nt(v["dc"][...], v["wl"][at, :])

        out_dc.wait()
        scatter.ready.add((layer, "dc"))
        slot()
        copies["h"].wait()
        norm_back_to(v["g"], v["g"], v["dm"], v["h"], gains[2 * layer : 2 * layer + 1, :],
                     gain_rows.at[2 * layer : 2 * layer + 1, :])
        scatter.ready.add((layer, "end"))
        slot()
    last = pltpu.make_async_copy(v["g"], grad_out, insem.at[0])
    last.start()
    scatter.drain()
    last.wait()


def backward(n, cot, gains, kept, weights, target, cid):
    Z, Y, X = dims_of(n)
    tokens, width = cot.shape
    rows = width // n
    ff = weights[0][4].shape[1]
    wide, lat = weights[0][0].shape[1], weights[0][1].shape[1]
    half = weights[0][2].shape[2]
    each = [ff, ff, ff, wide, wide, half, lat]
    widths = each * LAYERS + [128]
    chunks = cut(widths, target)
    K = 2 * LAG + 1
    most = max(X, Y)
    sides, ends = max(most, 2) - 1, max(Z - 1, 1)
    most_wide = max(ch[5] - ch[1] for ch in chunks)
    ring = lambda *shape, deep=K: pltpu.VMEM((deep,) + shape + (rows, most_wide), bf16)
    tok = lambda w, t=bf16: pltpu.VMEM((tokens, w), t)
    made = dict(gf=width, da=ff, db=ff, ga=width, dq=wide, dk=wide, dv=wide, dc=lat)
    layers = list(reversed(range(LAYERS)))
    operands = [cot, gains]
    for layer in layers:
        operands += [kept[layer][name] for name in KEPT]
    for layer in layers:
        operands += list(weights[layer])
    shapes = [jax.ShapeDtypeStruct((tokens, width), f32)]
    shapes += [jax.ShapeDtypeStruct((LAYERS, rows, w), f32) for w in each] + [jax.ShapeDtypeStruct((rows, 128), f32)]
    count = len(each) + 1
    shapes += [jax.ShapeDtypeStruct((tokens, made[name]), bf16) for layer in layers for name in MADE]
    got = pl.pallas_call(
        functools.partial(backward_kernel, n, chunks, K, count),
        out_shape=shapes,
        in_specs=[ANY, VM] + [ANY] * (len(operands) - 2),
        out_specs=[ANY] + [VM] * count + [ANY] * (LAYERS * len(MADE)),
        scratch_shapes=[
            pltpu.VMEM((2, tokens, width), bf16),
            pltpu.VMEM((2, tokens, most_wide), bf16),
            ring(Z, Y, X, 2),
            ring(Z, Y, X),
            ring(Z, most),
            ring(sides, Z, most),
            ring(Z),
            ring(sides, Z),
            ring(Z, most, deep=KZ),
            ring(Z, deep=KZ),
            ring(most),
            ring(sides),
            pltpu.VMEM((8, width), f32),
            tok(width), tok(ff), tok(ff), tok(width), tok(wide), tok(wide), tok(wide), tok(wide),
            tok(wide), tok(wide), tok(wide), tok(lat),
            pltpu.VMEM((4,) + kept[0]["p"].shape[1:], bf16),
            tok(width, f32), tok(width, f32), tok(width, f32),
            pltpu.VMEM((2, 2, tokens, 256), f32),
            pltpu.VMEM((2, width, 256), bf16),
            pltpu.VMEM((2, 2, 256, ff), bf16),
        ]
        + [pltpu.VMEM(weights[0][i].shape, bf16) for i in (3, 2, 0, 1)]
        + [DMA((2,)), DMA((2,)), DMA((K,)), DMA((K,))]
        + [DMA((K, 6, sides))] * 2
        + [DMA((KZ, 3, ends + 2))] * 2
        + [DMA((10,)), DMA((len(MADE),)), DMA((2, 2)), DMA((3, 2)), DMA((4,))],
        compiler_params=pltpu.CompilerParams(
            collective_id=cid, has_side_effects=True, vmem_limit_bytes=67043328
        ),
    )(*operands)
    return got[0], got[1 : 1 + count]


class Gather:
    def __init__(self, n, chunks, ins, outs, sems):
        self.n, self.chunks, self.ins, self.outs = n, chunks, ins, outs
        self.own_sem, self.zs, self.zr, self.ss, self.sr, self.cs, self.cr = sems
        self.stages = [self.first, self.second, self.third, self.fourth, self.to_partner, lambda i: []]
        self.held = [None] * len(chunks)
        self.at = 0
        self.total = len(chunks) + LAG * (len(self.stages) - 1)

    def slot(self, times=1):
        for _ in range(times):
            if self.at >= self.total:
                return
            last = len(self.stages) - 1
            for s in range(last, -1, -1):
                j = self.at - LAG * s
                if 0 <= j < len(self.chunks):
                    if s > 0:
                        for copy in self.held[j]:
                            copy.wait()
                    self.held[j] = self.stages[s](j)
            self.at += 1

    def until(self, a, column):
        need = max(i for i, ch in enumerate(self.chunks) if ch[0] == a and ch[1] < column)
        while self.at < need + LAG * (len(self.stages) - 1) + 1:
            self.slot()

    def along(self, axis, i, flow, src, dst):
        n, k = self.n, i % RING
        Z, Y, X = dims_of(n)
        z, y, x, c = place(n)
        copies = []
        for o in range(1, X if axis == "x" else Y):
            to = index(n, z, y, lax.rem(x + o, X), c) if axis == "x" else index(n, z, lax.rem(y + o, Y), x, c)
            copies.append(remote(src, dst, self.ss.at[k, flow, o - 1], self.sr.at[k, flow, o - 1], to))
        return copies

    def along_z(self, i, flow, src, dst):
        n, k = self.n, i % RING
        Z, Y, X = dims_of(n)
        z, y, x, c = place(n)
        copies = []
        for o in range(1, Z):
            to = index(n, lax.rem(z + o, Z), y, x, c)
            sems = self.zs.at[k, flow, o - 1], self.zr.at[k, flow, o - 1]
            if relays(Z) and o != 2:
                ends = (Z - 1, 0) if o == 1 else (0, Z - 1)
                copies.append(Sometimes(describe(src, dst, *sems, to), z != ends[0], z != ends[1]))
            else:
                copies.append(remote(src, dst, *sems, to))
        return copies

    def relay_z(self, i, flow, part):
        n, k = self.n, i % RING
        Z, Y, X = dims_of(n)
        z, y, x, c = place(n)
        copies = []
        if relays(Z):
            for o, via, end in ((1, 1, 0), (3, 2, 3)):
                block = part(3 - end)
                sems = self.zs.at[k, flow, o - 1], self.zr.at[k, flow, o - 1]
                copies.append(Sometimes(describe(block, block, *sems, index(n, end, y, x, c)), z == via, z == end))
        return copies

    def views(self, i):
        z, y, x, c = place(self.n)
        a, lo, e1, e2, e3, hi = self.chunks[i]
        out = self.outs[a]
        inner = lambda zz: out.at[zz, y, x, c, :, e1:e3]
        left = lambda zz: out.at[zz, y, :, c, :, lo:e1]
        right = lambda zz: out.at[zz, :, x, c, :, e3:hi]
        return z, y, x, c, out, inner, left, right

    def first(self, i):
        z, y, x, c, out, inner, left, right = self.views(i)
        a, lo, e1, e2, e3, hi = self.chunks[i]
        src = self.ins[a]
        own = pltpu.make_async_copy(src.at[:, lo:hi], out.at[z, y, x, c, :, lo:hi], self.own_sem.at[i % RING])
        own.start()
        copies = [own]
        if e3 > e1:
            copies += self.along_z(i, 0, src.at[:, e1:e3], inner(z))
        if e1 > lo:
            copies += self.along("x", i, 0, src.at[:, lo:e1], out.at[z, y, x, c, :, lo:e1])
        if hi > e3:
            copies += self.along("y", i, 1, src.at[:, e3:hi], out.at[z, y, x, c, :, e3:hi])
        return copies

    def second(self, i):
        z, y, x, c, out, inner, left, right = self.views(i)
        a, lo, e1, e2, e3, hi = self.chunks[i]
        copies = self.relay_z(i, 0, inner) if e3 > e1 else []
        if e1 > lo:
            copies += self.along_z(i, 1, left(z), left(z))
        if hi > e3:
            copies += self.along_z(i, 2, right(z), right(z))
        return copies

    def third(self, i):
        z, y, x, c, out, inner, left, right = self.views(i)
        a, lo, e1, e2, e3, hi = self.chunks[i]
        copies = []
        if e1 > lo:
            copies += self.relay_z(i, 1, left)
        if hi > e3:
            copies += self.relay_z(i, 2, right)
        if e3 > e1:
            part = out.at[:, y, x, c, :, e1:e2]
            copies += self.along("x", i, 2, part, part)
            part = out.at[:, y, x, c, :, e2:e3]
            copies += self.along("y", i, 3, part, part)
        return copies

    def fourth(self, i):
        z, y, x, c, out, inner, left, right = self.views(i)
        a, lo, e1, e2, e3, hi = self.chunks[i]
        copies = []
        if e2 > lo:
            part = out.at[:, y, :, c, :, lo:e2]
            copies += self.along("y", i, 4, part, part)
        if hi > e2:
            part = out.at[:, :, x, c, :, e2:hi]
            copies += self.along("x", i, 5, part, part)
        return copies

    def to_partner(self, i):
        z, y, x, c, out, inner, left, right = self.views(i)
        a, lo, e1, e2, e3, hi = self.chunks[i]
        part = out.at[:, :, :, c, :, lo:hi]
        return [remote(part, part, self.cs.at[i % RING], self.cr.at[i % RING], index(self.n, z, y, x, 1 - c))]


SAVED = ("n1", "q", "k", "v", "o", "h1", "n2", "cp", "z", "wkv")
PARTS = ("wq", "wl", "kv", "wo", "wg", "wu", "wd")
CAST = ("wq", "wl", "wg", "wu")


def fill_picks(n, picks):
    which, lat, width = picks.shape
    quarter = width // n // which
    bits = quarter.bit_length() - 1
    row = lax.broadcasted_iota(jnp.int32, (lat, width), 0)
    col = lax.broadcasted_iota(jnp.int32, (lat, width), 1)
    base = ((row >> bits) * (which * quarter)) + (row & (quarter - 1))
    for i in range(which):
        picks[i] = jnp.where(col == base + i * quarter, 1.0, 0.0).astype(bf16)


def forward_kernel(n, chunks, *refs):
    it = iter(refs)
    take = lambda names: {name: next(it) for name in names}
    parents, lengths, tokens_ref, gain_in = [next(it) for _ in range(4)]
    count = 1 + LAYERS * len(PARTS)
    raw = take(PARTS)
    final, bias, gains_out = next(it), next(it), next(it)
    outs = [next(it) for _ in range(count)]
    kept = [take(SAVED + ("a", "b", "h", "p")) for _ in range(LAYERS)]
    v = take(SAVED + ("h", "p", "c", "ab", "picks", "gr", "gt", "wq", "wl", "kv", "wo", "wgu", "wd"))
    low = take(CAST)
    send = {name: low.get(name, raw[name]) for name in PARTS}
    ins = [gain_in] + [send[name].at[layer] for layer in range(LAYERS) for name in PARTS]
    gather = Gather(n, chunks, ins, outs, [next(it) for _ in range(7)])
    insem, savesem, absem, gusem, wdsem, psem = [next(it) for _ in range(6)]
    slot = gather.slot
    z, y, x, c = place(n)
    for name in CAST:
        low[name][...] = raw[name][...].astype(bf16)
    greet(n, z, y, x, c)
    slot(3)

    def rows_of(a):
        return outs[a].reshape(outs[a].shape[0] * outs[a].shape[1] * outs[a].shape[2] * 2 * outs[a].shape[4], outs[a].shape[5])

    gathered = [rows_of(a) for a in range(count)]

    def load(a, name, at):
        gather.until(a, outs[a].shape[5])
        copy = pltpu.make_async_copy(gathered[a], v[name], insem.at[at])
        copy.start()
        return copy

    @tiles(tokens_ref.shape[0], 64)
    def _(at):
        v["h"][at, :] = tokens_ref[at, :].astype(f32)

    build_bias(parents, lengths, bias)
    slot()
    fill_picks(n, v["picks"])
    slot()
    copy = load(0, "gr", 0)
    copy.wait()
    lines = lax.broadcasted_iota(jnp.int32, (8, 128), 0) == lax.broadcasted_iota(jnp.int32, (8, 128), 1)
    v["gt"][...] = dot_nt(lines.astype(bf16), v["gr"][...])
    gains_out[...] = v["gt"][...]
    gains = v["gt"]

    for layer in range(LAYERS):
        s = kept[layer]
        base = 1 + layer * len(PARTS)
        saves = []

        def save(name, src=None):
            copy = pltpu.make_async_copy(v[src or name], s[name], savesem.at[len(saves)])
            copy.start()
            saves.append(copy)

        h, n1, n2, h1 = v["h"], v["n1"], v["n2"], v["h1"]
        save("h")
        norm_to(n1, h, gains[2 * layer : 2 * layer + 1, :])
        save("n1")
        slot()
        load(base, "wq", 0).wait()
        wl_copy = load(base + 1, "wl", 1)

        @tiles(v["wq"].shape[1], 512)
        def _(at):
            v["q"][:, at] = dot(n1[...], v["wq"][:, at]).astype(bf16)

        save("q")
        slot()
        wl_copy.wait()
        kv_copy = load(base + 2, "kv", 2)
        v["c"][...] = dot(n1[...], v["wl"][...]).astype(bf16)
        spread = dot(v["c"][:, 0:LAT], v["picks"][0] + v["picks"][GROUPS])
        for g in range(1, GROUPS):
            spread += dot(v["c"][:, g * LAT : (g + 1) * LAT], v["picks"][g] + v["picks"][GROUPS + g])
        v["cp"][...] = spread.astype(bf16)
        save("cp")
        kv_copy.wait()
        half = v["kv"].shape[1]
        for i in range(2 * GROUPS):
            v["wkv"][i] = dot(v["picks"][i], v["kv"][...]).astype(bf16)
        save("wkv")
        slot()
        for g in range(GROUPS):
            cg = v["c"][:, g * LAT : (g + 1) * LAT]
            v["k"][:, g * half : (g + 1) * half] = dot(cg, v["wkv"][g]).astype(bf16)
            v["v"][:, g * half : (g + 1) * half] = dot(cg, v["wkv"][GROUPS + g]).astype(bf16)
        save("k")
        save("v")
        slot()
        pairs = s["p"].shape[0]

        def put_p(j):
            return pltpu.make_async_copy(v["p"].at[lax.rem(j, 2)], s["p"].at[j], psem.at[lax.rem(j, 2)])

        step = attention_forward_step(v["q"], v["k"], v["v"], bias, v["o"], v["p"], put_p)
        for part in range(4):
            loop(part * pairs // 4, (part + 1) * pairs // 4, step, 2)
            slot()
        save("o")
        for j in (pairs - 2, pairs - 1):
            put_p(j).wait()
        load(base + 3, "wo", 0).wait()

        @tiles(v["wo"].shape[0], 512)
        def _(at):
            h1[:, at] = h[:, at] + dot_nt(v["o"][...], v["wo"][at, :])

        save("h1")
        slot()
        norm_to(n2, h1, gains[2 * layer + 1 : 2 * layer + 2, :])
        save("n2")
        ff = v["z"].shape[1]
        steps = ff // 256

        def tile_gu(j, which):
            src = gathered[base + 4 + which]
            return pltpu.make_async_copy(src.at[:, span(j, 256)], v["wgu"].at[which, lax.rem(j, 2)], gusem.at[which, lax.rem(j, 2)])

        def put(j, which):
            dst = s["ab"[which]]
            return pltpu.make_async_copy(v["ab"].at[which, lax.rem(j, 2)], dst.at[:, span(j, 256)], absem.at[which, lax.rem(j, 2)])

        cuts = [i * steps // 5 for i in range(6)]
        for lo, hi in zip(cuts, cuts[1:]):
            gather.until(base + 4, hi * 256)
            gather.until(base + 5, hi * 256)
            tile_gu(lo, 0).start()
            tile_gu(lo, 1).start()

            def gate_step(j):
                at = span(j, 256)
                tile_gu(j, 0).wait()
                tile_gu(j, 1).wait()

                @pl.when(j + 1 < hi)
                def _():
                    tile_gu(j + 1, 0).start()
                    tile_gu(j + 1, 1).start()

                @pl.when(j >= 2)
                def _():
                    put(j - 2, 0).wait()
                    put(j - 2, 1).wait()

                a = dot(n2[...], v["wgu"][0, lax.rem(j, 2)])
                b = dot(n2[...], v["wgu"][1, lax.rem(j, 2)])
                sig = 1.0 / (1.0 + jnp.exp(-a))
                silu = a * sig
                v["ab"][0, lax.rem(j, 2)] = b * sig * (1.0 + a * (1.0 - sig))
                v["ab"][1, lax.rem(j, 2)] = silu
                put(j, 0).start()
                put(j, 1).start()
                v["z"][:, at] = (silu * b).astype(bf16)

            loop(lo, hi, gate_step)
            slot()
        save("z")
        for copy in saves:
            copy.wait()
        for j in (steps - 2, steps - 1):
            put(j, 0).wait()
            put(j, 1).wait()
        downs = [(ch[1], ch[5]) for ch in chunks if ch[0] == base + 6]

        def tile_wd(i):
            lo, hi = downs[i]
            gather.until(base + 6, hi)
            copy = pltpu.make_async_copy(gathered[base + 6].at[:, lo:hi], v["wd"].at[i % 2, :, 0 : hi - lo], wdsem.at[i % 2])
            copy.start()
            return copy

        coming = tile_wd(0)
        for i, (lo, hi) in enumerate(downs):
            coming.wait()
            if i + 1 < len(downs):
                coming = tile_wd(i + 1)

            @tiles(h.shape[1], 512)
            def _(at):
                add = dot_nt(v["z"][:, lo:hi], v["wd"][i % 2, at, 0 : hi - lo])
                h[:, at] = (h1[:, at] if i == 0 else h[:, at]) + add

            slot()
    last = pltpu.make_async_copy(v["h"], final, insem.at[0])
    last.start()
    slot(gather.total)
    last.wait()


def forward(n, tokens, parents, lengths, trees, gain_rows, parts, target, cid):
    Z, Y, X = dims_of(n)
    rows, width = tokens.shape
    shapes = {name: part.shape[1:] for name, part in zip(PARTS, parts)}
    shards = [jax.ShapeDtypeStruct(gain_rows.shape, bf16)]
    shards += [jax.ShapeDtypeStruct(shapes[name], bf16) for layer in range(LAYERS) for name in PARTS]
    wide, lat, half, ff = shapes["wq"][1], shapes["wl"][1], shapes["kv"][1], shapes["wg"][1]
    chunks = cut([s.shape[1] for s in shards], target)
    order = []
    for a in range(len(shards)):
        mine = [ch for ch in chunks if ch[0] == a]
        part = PARTS[(a - 1) % len(PARTS)] if a else None
        if part == "wg":
            both = [ch for ch in chunks if ch[0] == a + 1]
            mine = [ch for pair in zip(mine, both) for ch in pair]
        elif part == "wu":
            mine = []
        order += mine
    ends, sides = max(Z - 1, 1), max(X, Y, 2) - 1
    tok = lambda w, t=bf16: jax.ShapeDtypeStruct((rows, w), t)
    saved = dict(
        n1=tok(width), q=tok(wide), k=tok(wide), v=tok(wide), o=tok(wide),
        h1=tok(width, f32), n2=tok(width), cp=tok(width), z=tok(ff),
        wkv=jax.ShapeDtypeStruct((2 * GROUPS, LAT, half), bf16), a=tok(ff, f32), b=tok(ff, f32), h=tok(width, f32),
    )
    tree = rows // trees
    saved["p"] = jax.ShapeDtypeStruct((trees * wide // 128, 2, tree, tree), bf16)
    names = SAVED + ("a", "b", "h", "p")
    out_shape = [tok(width, f32), jax.ShapeDtypeStruct((trees, tree, tree), f32), jax.ShapeDtypeStruct((8, width), f32)]
    out_shape += [jax.ShapeDtypeStruct((Z, Y, X, 2) + s.shape, s.dtype) for s in shards]
    out_shape += [saved[name] for layer in range(LAYERS) for name in names]
    vmem = lambda s: pltpu.VMEM(s.shape, s.dtype)
    down = max(ch[5] - ch[1] for ch in order)
    got = pl.pallas_call(
        functools.partial(forward_kernel, n, order),
        out_shape=out_shape,
        in_specs=[SM, SM, VM, ANY] + [VM if name in CAST else ANY for name in PARTS],
        out_specs=[ANY, VM, VM] + [ANY] * (len(out_shape) - 3),
        scratch_shapes=[vmem(saved[name]) for name in SAVED]
        + [
            pltpu.VMEM((rows, width), f32),
            pltpu.VMEM((2, 2, tree, tree), bf16),
            pltpu.VMEM((rows, lat), bf16),
            pltpu.VMEM((2, 2, rows, 256), f32),
            pltpu.VMEM((2 * GROUPS, LAT, width), bf16),
            pltpu.VMEM((width, 128), bf16),
            pltpu.VMEM((8, width), f32),
            pltpu.VMEM((width, wide), bf16),
            pltpu.VMEM((width, lat), bf16),
            pltpu.VMEM((width, half), bf16),
            pltpu.VMEM((width, wide), bf16),
            pltpu.VMEM((2, 2, width, 256), bf16),
            pltpu.VMEM((2, width, down), bf16),
        ]
        + [pltpu.VMEM((LAYERS,) + shapes[name], bf16) for name in CAST]
        + [DMA((RING,))]
        + [DMA((RING, 3, ends))] * 2
        + [DMA((RING, 6, sides))] * 2
        + [DMA((RING,))] * 2
        + [DMA((3,)), DMA((len(SAVED) + 1,)), DMA((2, 2)), DMA((2, 2)), DMA((2,)), DMA((2,))],
        compiler_params=pltpu.CompilerParams(
            collective_id=cid, has_side_effects=True, vmem_limit_bytes=67043328
        ),
    )(parents, lengths, tokens, gain_rows, *parts)
    final, bias, gains = got[:3]
    gathered = [g.reshape(n * s.shape[0], s.shape[1]) for g, s in zip(got[3:], shards)]
    rest = got[3 + len(shards) :]
    kept = [dict(zip(names, rest[i * len(names) : (i + 1) * len(names)])) for i in range(LAYERS)]
    weights = []
    for layer in range(LAYERS):
        q, l, kv, o, g, u, d = gathered[1 + layer * len(PARTS) : 1 + (layer + 1) * len(PARTS)]
        weights.append((q, l, kept[layer]["wkv"], o, g, u, d))
    return final, bias, gains, kept, weights


def body(inputs, cotangent, parents, lengths, g1, wq, wl, wk, wv, wo, g2, wg, wu, wd, *, n):
    trees, tree, width = inputs.shape
    rows = wq.shape[1]
    latr = wk.shape[2]

    kv = jnp.stack([wk, wv], axis=1).astype(bf16).reshape(LAYERS, 4 * latr, wk.shape[3])
    gain_rows = jnp.stack([g1[0], g2[0], g1[1], g2[1]], axis=1).astype(bf16)
    gain_rows = jnp.pad(gain_rows, ((0, 0), (0, 128 - 2 * LAYERS)))
    parts = [wq, wl, kv, wo.astype(bf16).transpose(0, 2, 1), wg, wu, wd.astype(bf16).transpose(0, 2, 1)]
    out, bias, gains, kept, weights = forward(
        n, inputs.reshape(trees * tree, width), parents, lengths, trees, gain_rows, parts, 576, 0
    )
    outputs = out.reshape(inputs.shape)
    cot = cotangent.reshape(trees * tree, width)
    grad, summed = backward(n, cot, gains, kept, weights, 576, 1)
    dd, dg, du, do, dq, kv, dl, gain = summed
    kv = kv.reshape(LAYERS, 2, GROUPS, latr, -1)
    gain = gain.T[: 2 * LAYERS].reshape(LAYERS, 2, rows)
    flip = lambda d: d.transpose(0, 2, 1)
    grads = (gain[:, 0], dq, dl, kv[:, 0], kv[:, 1], flip(do), gain[:, 1], dg, du, flip(dd))
    return (outputs, grad.reshape(inputs.shape)) + grads


def solution(mesh):
    n = mesh.shape["fsdp"]
    by_one, by_two = P(None, "fsdp"), P(None, "fsdp", None)
    by_lat, by_last = P(None, None, "fsdp", None), P(None, None, "fsdp")
    params = (by_one, by_two, by_two, by_lat, by_lat, by_last, by_one, by_two, by_two, by_last)
    trees = P("fsdp", None, None)
    return jax.shard_map(
        functools.partial(body, n=n),
        mesh=mesh,
        in_specs=(trees, trees, P("fsdp", None), P("fsdp", None)) + params,
        out_specs=(trees, trees) + params,
        check_vma=False,
    )
```
